256 devices in a mesh: replica: 32 (over x, z), tensor: 8 (over y, core).
Axes of the slice: x: 4, y: 4, z: 8, core: 2. Of those that a mesh axis runs over, the one named last changes fastest.
Arguments:
- tokens: bfloat16 [96, 2048], P('replica'), may hold values from -0.8984375 to 0.8984375
- long_tokens: bfloat16 [32, 2048], P('replica'), may hold values from -0.8984375 to 0.8984375
- cache: bfloat16 [2, 2, 96, 2048, 8, 128], P(None, None, 'replica', None, 'tensor')
- long_request_cache: bfloat16 [2, 2, 32, 2, 2048, 8, 128], P(None, None, 'replica', None, None, 'tensor')
- lengths: int32 [96], replicated, may hold values from 1 to 2047, as said below
- long_lengths: int32 [32], replicated, may hold values from 2049 to 4095, as said below
- norm_gain: float32 [2, 2048], replicated, may hold values from 0.1 to 1.9
- q_gain: float32 [2, 128], replicated, may hold values from 0.1 to 1.9
- k_gain: float32 [2, 128], replicated, may hold values from 0.1 to 1.9
- w_query: bfloat16 [2, 2048, 2048], P(None, None, 'tensor'), may hold values from -0.125 to 0.125
- key_weight: bfloat16 [2, 2048, 1024], P(None, None, 'tensor'), may hold values from -0.125 to 0.125
- value_weight: bfloat16 [2, 2048, 1024], P(None, None, 'tensor'), may hold values from -0.125 to 0.125
- w_out: bfloat16 [2, 2048, 2048], P(None, 'tensor'), may hold values from -0.125 to 0.125
Outputs:
- out_hidden: float32 [96, 2048], P('replica')
- out_long: float32 [32, 2048], P('replica')
- moved_cache: bfloat16 [32, 2, 2, 2048, 8, 128], P('replica', None, None, None, 'tensor')
The draws below stay inside these ranges and needn't reach their ends.
Inputs may be any that keep to these rules, and one draw needn't show every extreme that they name: `lengths`: cached length of each request; some request has 2047 in every draw. `long_lengths`: cached length of each long request, always past 2048; some long request has 4095 in every draw.
All inputs are finite; a program needn't handle non-finite values.
Results may differ from the reference program's by a relative error of at most 0.028.
Values may be sent and summed in bfloat16 or wider, within the bound.
No kernel may reach another device: no remote copies, remote signals or barrier semaphores. Data moves between devices by JAX's collectives and lax.ppermute only.
A program may use at most 64 MiB of HBM per device.

```python
import jax
import jax.numpy as jnp
from jax import lax

MODEL_WIDTH = 2048
HQ = 16
KEY_VALUE_HEADS = 8
HEAD_SIZE = 128
STAYING_REQUESTS = 2
CONTEXT_LENGTH = 2048
LAYER_COUNT = 2
HALF_CONTEXT = 2048
REQS = 96
N_REPLICA = 32


def key_value_pairs(key, shape):
    values = jax.random.normal(key, shape, jnp.float32)
    return values.astype(jnp.bfloat16)


def draw_cache(key, part):
    return key_value_pairs(key, (LAYER_COUNT, 2, N_REPLICA * (STAYING_REQUESTS + 1), CONTEXT_LENGTH, KEY_VALUE_HEADS, HEAD_SIZE))


def draw_long_request_cache(key, part):
    return key_value_pairs(key, (LAYER_COUNT, 2, N_REPLICA, 2, HALF_CONTEXT, KEY_VALUE_HEADS, HEAD_SIZE))


def draw_lengths(key, part):
    row_count = N_REPLICA * (STAYING_REQUESTS + 1)
    key_one, key_two, key_three = jax.random.split(key, 3)
    ceiling = jax.random.randint(key_one, (row_count,), 1, CONTEXT_LENGTH)
    values = 1 + jax.random.randint(key_two, (row_count,), 0, ceiling)
    chosen = jax.random.randint(key_three, (), 0, row_count)
    return jnp.where(jnp.arange(row_count) == chosen, CONTEXT_LENGTH - 1, values).astype(jnp.int32)


def draw_long_lengths(key, part):
    key_one, key_two = jax.random.split(key, 2)
    values = HALF_CONTEXT + 1 + jax.random.randint(key_one, (N_REPLICA,), 0, HALF_CONTEXT - 1)
    chosen = jax.random.randint(key_two, (), 0, N_REPLICA)
    return jnp.where(jnp.arange(N_REPLICA) == chosen, 2 * HALF_CONTEXT - 1, values).astype(jnp.int32)


def level_of(rng, shape, shards, least, largest):
    loudness = 1.0
    for position, blocks in shards:
        draws = jax.random.uniform(jax.random.fold_in(jax.random.fold_in(rng, 6), position), (blocks,), jnp.float32, least / len(shards), largest / len(shards))
        loudness = loudness * jnp.repeat(jnp.exp(draws), shape[position] // blocks).reshape((-1,) + (1,) * (len(shape) - 1 - position))
    return loudness


def gaussian(own_key, dims, width, reach, cuts=(), kind=jnp.bfloat16):
    level = level_of(own_key, dims, cuts, -0.22, 0.18) if cuts else 1.0
    drawn = jax.random.normal(own_key, dims, jnp.float32) * width * level
    return jnp.minimum(jnp.maximum(drawn, -reach), reach).astype(kind)


def setup_inputs(seed: int = 0) -> dict:
    keys = jax.random.split(jax.random.key(seed), 14)
    return {
        "tokens": gaussian(keys[0], (REQS, MODEL_WIDTH), 0.15, 0.8984375, ((0, 32),)),
        "long_tokens": gaussian(keys[1], (N_REPLICA, MODEL_WIDTH), 0.15, 0.8984375, ((0, 32),)),
        "cache": draw_cache(jax.random.fold_in(keys[13], 71), 0),
        "long_request_cache": draw_long_request_cache(jax.random.fold_in(keys[13], 71), 0),
        "lengths": draw_lengths(jax.random.fold_in(keys[13], 71), 0),
        "long_lengths": draw_long_lengths(jax.random.fold_in(keys[13], 71), 0),
        "norm_gain": jnp.clip(1.0 + 0.18 * jax.random.normal(keys[6], (LAYER_COUNT, MODEL_WIDTH), jnp.float32), 0.1, 1.9),
        "q_gain": jnp.clip(1.0 + 0.18 * jax.random.normal(keys[7], (LAYER_COUNT, HEAD_SIZE), jnp.float32), 0.1, 1.9),
        "k_gain": jnp.clip(1.0 + 0.18 * jax.random.normal(keys[8], (LAYER_COUNT, HEAD_SIZE), jnp.float32), 0.1, 1.9),
        "w_query": gaussian(keys[9], (LAYER_COUNT, MODEL_WIDTH, HQ * HEAD_SIZE), MODEL_WIDTH ** -0.5, 0.125, ((2, 8),)),
        "key_weight": gaussian(keys[10], (LAYER_COUNT, MODEL_WIDTH, KEY_VALUE_HEADS * HEAD_SIZE), MODEL_WIDTH ** -0.5, 0.125, ((2, 8),)),
        "value_weight": gaussian(keys[11], (LAYER_COUNT, MODEL_WIDTH, KEY_VALUE_HEADS * HEAD_SIZE), MODEL_WIDTH ** -0.5, 0.125, ((2, 8),)),
        "w_out": gaussian(keys[12], (LAYER_COUNT, HQ * HEAD_SIZE, MODEL_WIDTH), (HQ * HEAD_SIZE) ** -0.5, 0.125, ((1, 8),)),
    }


EPSILON = 1e-06
ROPE_BASE = 1000000.0
NEGATIVE = -1e+30

def rms_scale(values, gain_row):
    return values * lax.rsqrt(lax.optimization_barrier(jnp.mean(values * values, axis=-1, keepdims=True)) + EPSILON) * gain_row

def rotate(values, places):
    head_width = values.shape[-1]
    halfway = head_width // 2
    inverse = ROPE_BASE ** (-2.0 * jnp.arange(halfway, dtype=jnp.float32) / head_width)
    angles = places.astype(jnp.float32)[:, None, None] * inverse
    cosine = jnp.cos(angles)
    sine_of = jnp.sin(angles)
    leading = values[..., :halfway]
    trailing = values[..., halfway:]
    return jnp.concatenate([leading * cosine - trailing * sine_of, trailing * cosine + leading * sine_of], axis=-1)

def project(hidden, gain_row, w_query, key_weight, value_weight, query_gain, key_gain, places):
    head_width = query_gain.shape[-1]
    count_rows = hidden.shape[0]
    normed = rms_scale(hidden.astype(jnp.float32), gain_row).astype(jnp.bfloat16)
    queries = jnp.dot(normed, w_query, preferred_element_type=jnp.float32).reshape(count_rows, -1, head_width)
    keys_new = jnp.dot(normed, key_weight, preferred_element_type=jnp.float32).reshape(count_rows, -1, head_width)
    values_new = jnp.dot(normed, value_weight, preferred_element_type=jnp.float32).reshape(count_rows, -1, head_width).astype(jnp.bfloat16)
    queries = rotate(rms_scale(queries, query_gain), places).astype(jnp.bfloat16)
    keys_new = rotate(rms_scale(keys_new, key_gain), places).astype(jnp.bfloat16)
    return (queries, keys_new, values_new)

def attend(queries, key_rows, value_rows, visible, key_new, value_new):
    head_width = queries.shape[-1]
    factor = head_width ** (-0.5)
    grouped = queries.astype(jnp.float32).reshape(key_rows.shape[1], -1, head_width)
    scores = jnp.einsum('kgd,tkd->kgt', grouped, key_rows.astype(jnp.float32)) * factor
    scores = jnp.where(visible[None, None, :], scores, NEGATIVE)
    own_score = jnp.einsum('kgd,kd->kg', grouped, key_new.astype(jnp.float32)) * factor
    highest = jnp.maximum(lax.optimization_barrier(jnp.max(scores, axis=-1)), own_score)
    weights = jnp.exp(scores - highest[..., None])
    own_weight = jnp.exp(own_score - highest)
    denominator = lax.optimization_barrier(jnp.sum(weights, axis=-1)) + own_weight
    rounded = lax.optimization_barrier(weights.astype(jnp.bfloat16)).astype(jnp.float32)
    own_rounded = lax.optimization_barrier(own_weight.astype(jnp.bfloat16)).astype(jnp.float32)
    summed = jnp.einsum('kgt,tkd->kgd', rounded, value_rows.astype(jnp.float32))
    summed = summed + own_rounded[..., None] * value_new.astype(jnp.float32)[:, None, :]
    return (summed / denominator[..., None]).reshape(queries.shape).astype(jnp.bfloat16)

def reference(tokens, long_tokens, cache, long_request_cache, lengths, long_lengths, norm_gain, q_gain, k_gain, w_query, key_weight, value_weight, w_out):
    per_group = STAYING_REQUESTS + 1
    requests = N_REPLICA * per_group
    positions = jnp.arange(CONTEXT_LENGTH).astype(jnp.int32)
    visible = positions[None, :] < lengths[:, None]
    ordered_layout = long_request_cache.reshape(LAYER_COUNT, 2, N_REPLICA // 2, 2, 2, HALF_CONTEXT, KEY_VALUE_HEADS, HEAD_SIZE)
    ordered_layout = ordered_layout.transpose(0, 1, 2, 4, 3, 5, 6, 7).reshape(LAYER_COUNT, 2, N_REPLICA, 2 * HALF_CONTEXT, KEY_VALUE_HEADS, HEAD_SIZE)
    long_visible = jnp.arange(2 * HALF_CONTEXT).astype(jnp.int32)[None, :] < long_lengths[:, None]
    hidden = tokens
    long_hidden = long_tokens
    fresh_rows = []
    for layer_at in range(LAYER_COUNT):
        queries, keys_new, values_new = project(hidden, norm_gain[layer_at], w_query[layer_at], key_weight[layer_at], value_weight[layer_at], q_gain[layer_at], k_gain[layer_at], lengths)
        attended = jax.vmap(attend)(queries, cache[layer_at, 0], cache[layer_at, 1], visible, keys_new, values_new)
        fresh_rows.append(jnp.stack([keys_new, values_new], axis=1))
        long_queries, long_keys, long_values = project(long_hidden, norm_gain[layer_at], w_query[layer_at], key_weight[layer_at], value_weight[layer_at], q_gain[layer_at], k_gain[layer_at], long_lengths)
        long_attended = jax.vmap(attend)(long_queries, ordered_layout[layer_at, 0], ordered_layout[layer_at, 1], long_visible, long_keys, long_values)
        hidden = hidden.astype(jnp.float32) + jnp.dot(attended.reshape(requests, -1), w_out[layer_at], preferred_element_type=jnp.float32)
        long_hidden = long_hidden.astype(jnp.float32) + jnp.dot(long_attended.reshape(N_REPLICA, -1), w_out[layer_at], preferred_element_type=jnp.float32)
        if layer_at + 1 < LAYER_COUNT:
            hidden = hidden.astype(jnp.bfloat16)
            long_hidden = long_hidden.astype(jnp.bfloat16)
    sources = (jnp.arange(N_REPLICA).astype(jnp.int32) + N_REPLICA // 2) % N_REPLICA
    leaving = (sources * per_group + STAYING_REQUESTS).astype(jnp.int32)
    served = jnp.arange(requests).astype(jnp.int32).reshape(N_REPLICA, per_group).at[:, STAYING_REQUESTS].set(leaving).reshape(-1)
    out_hidden = hidden[served]
    fresh_all = jnp.stack(fresh_rows)[:, leaving]
    fresh_all = fresh_all.transpose(0, 2, 1, 3, 4)[:, :, :, None]
    base_cache = cache[:, :, leaving]
    at_length = positions[None, :] == lengths[leaving][:, None]
    moved_whole = jnp.where(at_length[None, None, :, :, None, None], fresh_all, base_cache)
    return (out_hidden, long_hidden, moved_whole.transpose(2, 0, 1, 3, 4, 5))
```

```python
import functools

import jax
import jax.numpy as jnp
import numpy as np
from jax import lax
from jax.experimental import pallas as pl
from jax.experimental.pallas import tpu as pltpu
from jax.sharding import PartitionSpec as P

EPSILON = 1e-06
ROPE_BASE = 1000000.0
NEGATIVE = -1e30
ROWS = 8
ANY = pl.BlockSpec(memory_space=pltpu.HBM)
VM = pl.BlockSpec(memory_space=pltpu.VMEM)
SM = pl.BlockSpec(memory_space=pltpu.SMEM)


def permute(value, axis, target):
    pairs = [(source, target(source)) for source in range(lax.axis_size(axis))]
    return lax.ppermute(value, axis, pairs)


def row_of(count):
    return lax.broadcasted_iota(jnp.int32, (count, 1), 0)


def attention_step(
    layer, group_ref, lengths_ref, long_lengths_ref, hidden, gain_ref, q_gain_ref, k_gain_ref,
    cosine_ref, sine_ref, cache_ref, long_ref, wq_ref, wk_ref, wv_ref,
    state_ref, side_ref, fresh_ref, buffers, semaphores,
):
    wq, wk, wv, keys, values, long_keys, long_values = buffers
    sources = (
        wq_ref.at[layer], wk_ref.at[layer], wv_ref.at[layer],
        cache_ref.at[layer, 0], long_ref.at[layer, 0, 0],
        cache_ref.at[layer, 1], long_ref.at[layer, 1, 0],
    )
    targets = (wq, wk, wv, keys, long_keys, values, long_values)
    copies = [
        pltpu.make_async_copy(source, target, semaphores.at[i])
        for i, (source, target) in enumerate(zip(sources, targets))
    ]
    for copy in copies:
        copy.start()
    rows = hidden()
    scale = lax.rsqrt(jnp.mean(rows * rows, axis=-1, keepdims=True) + EPSILON)
    normed = (rows * scale * gain_ref[layer : layer + 1, :]).astype(jnp.bfloat16)
    for copy in copies[:3]:
        copy.wait()
    queries = jnp.dot(normed, wq[...], preferred_element_type=jnp.float32)
    new_keys = jnp.dot(normed, wk[...], preferred_element_type=jnp.float32)
    new_values = jnp.dot(normed, wv[...], preferred_element_type=jnp.float32).astype(jnp.bfloat16)

    def finish(heads, gain, cosine, sine):
        heads = heads * lax.rsqrt(jnp.mean(heads * heads, axis=-1, keepdims=True) + EPSILON) * gain
        return (heads * cosine + pltpu.roll(heads, 64, 1) * sine).astype(jnp.bfloat16)

    cosine, sine = cosine_ref[...], sine_ref[...]
    q_gain = q_gain_ref[layer : layer + 1, :]
    q0 = finish(queries[:, :128], q_gain, cosine, sine).astype(jnp.float32)
    q1 = finish(queries[:, 128:], q_gain, cosine, sine).astype(jnp.float32)
    key_new = finish(new_keys, k_gain_ref[layer : layer + 1, :], cosine, sine).astype(jnp.float32)
    value_new = new_values.astype(jnp.float32)
    fresh_ref[0:1, :] = key_new[2:3, :]
    fresh_ref[1:2, :] = value_new[2:3, :]
    both = jnp.concatenate([q0, q1], axis=0)
    query = both.astype(jnp.bfloat16)
    keys_twice = jnp.concatenate([key_new, key_new], axis=0)
    values_twice = jnp.concatenate([value_new, value_new], axis=0)
    factor = 128 ** (-0.5)
    own = jnp.sum(both * keys_twice, axis=-1, keepdims=True) * factor

    group = group_ref[0]
    parity = lax.rem(group, 2)
    which = lax.rem(row_of(16), 8)
    limit = jnp.ones((16, 1), jnp.int32)
    for r in range(3):
        limit = jnp.where(which == r, lengths_ref[group * 3 + r], limit)
    for r in range(2):
        limit = jnp.where(
            which == 3 + r, long_lengths_ref[group - parity + r] - parity * 2048, limit
        )
    scores = jnp.zeros((16, 2048), jnp.float32)
    for r in range(5):
        if r == 0:
            copies[3].wait()
        if r == 3:
            copies[4].wait()
        block = keys[r] if r < 3 else long_keys[r - 3]
        product = lax.dot_general(
            query, block, (((1,), (1,)), ((), ())), preferred_element_type=jnp.float32
        )
        scores = jnp.where(which == r, product, scores)
    places = lax.broadcasted_iota(jnp.int32, (16, 2048), 1)
    scores = jnp.where(places < limit, scores * factor, NEGATIVE)
    is_main = which < 3
    highest = jnp.max(scores, axis=-1, keepdims=True)
    highest = jnp.where(is_main, jnp.maximum(highest, own), highest)
    weights = jnp.exp(scores - highest)
    own_weight = jnp.where(is_main, jnp.exp(own - highest), 0.0)
    total = jnp.sum(weights, axis=-1, keepdims=True) + own_weight
    rounded = weights.astype(jnp.bfloat16)
    summed = own_weight.astype(jnp.bfloat16).astype(jnp.float32) * values_twice
    for r in range(5):
        if r == 0:
            copies[5].wait()
        if r == 3:
            copies[6].wait()
        block = values[r] if r < 3 else long_values[r - 3]
        product = jnp.dot(rounded, block, preferred_element_type=jnp.float32)
        summed = summed + jnp.where(which == r, product, 0.0)
    state_ref[:, 0:128] = summed
    lanes = lax.broadcasted_iota(jnp.int32, (16, 128), 1)
    state_ref[:, 128:256] = jnp.where(lanes < 64, highest, total)
    side_ref[:, 0:128] = jnp.broadcast_to(own, (16, 128))
    side_ref[:, 128:256] = values_twice


def first_kernel(
    group_ref, lengths_ref, long_lengths_ref, tokens_ref, own_long_ref, far_long_ref, *rest
):
    *middle, state_ref, side_ref, fresh_ref, hidden_ref = rest[:14]
    buffers, semaphores = rest[14:21], rest[21]

    def hidden():
        own = own_long_ref[...].astype(jnp.float32)
        far = far_long_ref[...].astype(jnp.float32)
        even = lax.rem(group_ref[0], 2) == 0
        hidden_ref[...] = jnp.zeros((ROWS, 2048), jnp.float32)
        hidden_ref[0:3, :] = tokens_ref[...].astype(jnp.float32)
        hidden_ref[3:4, :] = jnp.where(even, own, far)
        hidden_ref[4:5, :] = jnp.where(even, far, own)
        return hidden_ref[...]

    attention_step(
        0, group_ref, lengths_ref, long_lengths_ref, hidden, *middle,
        state_ref, side_ref, fresh_ref, buffers, semaphores,
    )


def second_kernel(
    group_ref, lengths_ref, long_lengths_ref, before_ref, p_ref, r1_ref, r2_ref, r3_ref, *rest
):
    *middle, state_ref, side_ref, fresh_ref, hidden_ref = rest[:14]
    buffers, semaphores = rest[14:21], rest[21]

    def hidden():
        summed = (p_ref[...] + r1_ref[...]) + (r2_ref[...] + r3_ref[...])
        rows = (before_ref[...] + summed).astype(jnp.bfloat16).astype(jnp.float32)
        hidden_ref[...] = rows
        return rows

    attention_step(
        1, group_ref, lengths_ref, long_lengths_ref, hidden, *middle,
        state_ref, side_ref, fresh_ref, buffers, semaphores,
    )


def out_kernel(layer, state_ref, far_ref, side_ref, w_ref, out_ref, w, semaphore):
    copy = pltpu.make_async_copy(w_ref.at[layer], w, semaphore)
    copy.start()
    is_main = lax.rem(row_of(16), 8) < 3
    here, far = state_ref[...], far_ref[...]
    m_here, l_here, acc_here = here[:, 128:129], here[:, 192:193], here[:, :128]
    m_far, l_far, acc_far = far[:, 128:129], far[:, 192:193], far[:, :128]
    own, value = side_ref[:, 0:1], side_ref[:, 128:256]
    highest = jnp.maximum(jnp.maximum(m_here, m_far), own)
    f_here, f_far = jnp.exp(m_here - highest), jnp.exp(m_far - highest)
    own_weight = jnp.exp(own - highest)
    total = (l_here * f_here + l_far * f_far) + own_weight
    own_rounded = own_weight.astype(jnp.bfloat16).astype(jnp.float32)
    summed = (acc_here * f_here + acc_far * f_far) + own_rounded * value
    total = jnp.where(is_main, l_here, total)
    summed = jnp.where(is_main, acc_here, summed)
    attended = summed / total
    attended = jnp.concatenate([attended[:8], attended[8:]], axis=1).astype(jnp.bfloat16)
    copy.wait()
    out_ref[...] = jnp.dot(attended, w[...], preferred_element_type=jnp.float32)


def final_kernel(
    group_ref, before_ref, p_ref, r1_ref, r2_ref, r3_ref, fresh0_ref, fresh1_ref,
    stay_ref, long_ref, leave_ref, scratch,
):
    summed = (p_ref[...] + r1_ref[...]) + (r2_ref[...] + r3_ref[...])
    scratch[...] = before_ref[...] + summed
    stay_ref[...] = scratch[0:2, :]
    odd = lax.rem(group_ref[0], 2) == 1
    long_ref[...] = jnp.where(odd, scratch[4:5, :], scratch[3:4, :])
    leave_ref[0:1, 0:2048] = scratch[2:3, :]
    for i, ref in enumerate((fresh0_ref, fresh1_ref)):
        for j in range(2):
            leave_ref[0:1, 2048 + 128 * (2 * i + j) : 2176 + 128 * (2 * i + j)] = ref[j : j + 1, :]


def local(
    tokens, long_tokens, cache, long_cache, lengths, long_lengths, norm_gain, q_gain, k_gain,
    w_query, key_weight, value_weight, w_out,
):
    groups = lax.axis_size("replica")
    group = lax.axis_index("replica")
    parity = group % 2
    group_1 = group[None]
    cache = cache.reshape(2, 2, 3, 2048, 128)
    long_cache = long_cache.reshape(2, 2, 1, 2, 2048, 128)

    far_token = permute(long_tokens, "replica", lambda i: i ^ 1)
    moving = permute(cache[:, :, 2], "replica", lambda i: (i + groups // 2) % groups)

    places = jnp.concatenate(
        [
            lax.dynamic_slice_in_dim(lengths, group * 3, 3),
            lax.dynamic_slice_in_dim(long_lengths, group - parity, 2),
            jnp.zeros((3,), jnp.int32),
        ]
    ).astype(jnp.float32)
    inverse = np.float64(ROPE_BASE) ** (-2.0 * np.arange(64) / 128)
    inverse = jnp.asarray(np.concatenate([inverse, inverse]).astype(np.float32))
    sign = jnp.asarray(np.where(np.arange(128) < 64, -1.0, 1.0).astype(np.float32))
    angles = places[:, None] * inverse[None, :]
    cosine, sine = jnp.cos(angles), jnp.sin(angles) * sign

    out_shape = (
        jax.ShapeDtypeStruct((16, 256), jnp.float32),
        jax.ShapeDtypeStruct((16, 256), jnp.float32),
        jax.ShapeDtypeStruct((2, 128), jnp.float32),
        jax.ShapeDtypeStruct((ROWS, 2048), jnp.float32),
    )
    scratch = [
        pltpu.VMEM((2048, 256), jnp.bfloat16),
        pltpu.VMEM((2048, 128), jnp.bfloat16),
        pltpu.VMEM((2048, 128), jnp.bfloat16),
        pltpu.VMEM((3, 2048, 128), jnp.bfloat16),
        pltpu.VMEM((3, 2048, 128), jnp.bfloat16),
        pltpu.VMEM((2, 2048, 128), jnp.bfloat16),
        pltpu.VMEM((2, 2048, 128), jnp.bfloat16),
        pltpu.SemaphoreType.DMA((7,)),
    ]
    params = pltpu.CompilerParams(vmem_limit_bytes=24 * 2**20)
    middle = (norm_gain, q_gain, k_gain, cosine, sine, cache, long_cache, w_query, key_weight, value_weight)
    middle_specs = [VM] * 5 + [ANY] * 5

    def project_out(layer, state, side):
        far = permute(state, "replica", lambda i: i ^ 1)
        part = pl.pallas_call(
            functools.partial(out_kernel, layer),
            out_shape=jax.ShapeDtypeStruct((ROWS, 2048), jnp.float32),
            in_specs=[VM, VM, VM, ANY],
            out_specs=VM,
            scratch_shapes=[pltpu.VMEM((256, 2048), jnp.bfloat16), pltpu.SemaphoreType.DMA(())],
            compiler_params=params,
            name=f"out_projection_{layer}",
        )(state, far, side, w_out)
        part = part + permute(part, "tensor", lambda i: i ^ 1)
        received = [permute(part, "tensor", lambda i, k=k: i ^ k) for k in (2, 4, 6)]
        return (part, *received)

    state, side, fresh_0, hidden = pl.pallas_call(
        first_kernel,
        out_shape=out_shape,
        in_specs=[SM] * 3 + [VM] * 3 + middle_specs,
        out_specs=(VM,) * 4,
        scratch_shapes=scratch,
        compiler_params=params,
        name="attention_0",
    )(group_1, lengths, long_lengths, tokens, long_tokens, far_token, *middle)
    terms = project_out(0, state, side)
    state, side, fresh_1, hidden = pl.pallas_call(
        second_kernel,
        out_shape=out_shape,
        in_specs=[SM] * 3 + [VM] * 5 + middle_specs,
        out_specs=(VM,) * 4,
        scratch_shapes=scratch,
        compiler_params=params,
        name="attention_1",
    )(group_1, lengths, long_lengths, hidden, *terms, *middle)
    terms = project_out(1, state, side)
    stay, long_out, leave = pl.pallas_call(
        final_kernel,
        out_shape=(
            jax.ShapeDtypeStruct((2, 2048), jnp.float32),
            jax.ShapeDtypeStruct((1, 2048), jnp.float32),
            jax.ShapeDtypeStruct((1, 2560), jnp.float32),
        ),
        in_specs=[SM] + [VM] * 7,
        out_specs=(VM,) * 3,
        scratch_shapes=[pltpu.VMEM((ROWS, 2048), jnp.float32)],
        name="final_rows",
    )(group_1, hidden, *terms, fresh_0, fresh_1)
    arrived = permute(leave, "replica", lambda i: (i + groups // 2) % groups)
    out_hidden = jnp.concatenate([stay, arrived[:, :2048]], axis=0)
    fresh = arrived[0, 2048:].reshape(2, 2, 1, 128).astype(jnp.bfloat16)
    partner = (group + groups // 2) % groups
    arrived_len = lax.dynamic_index_in_dim(lengths, partner * 3 + 2, 0, keepdims=False)
    at = lax.broadcasted_iota(jnp.int32, (1, 1, 2048, 1), 2) == arrived_len
    moved = jnp.where(at, fresh, moving)
    return (out_hidden, long_out, moved[None, :, :, :, None, :])


def solution(mesh):
    return jax.shard_map(
        local,
        mesh=mesh,
        in_specs=(
            P("replica", None),
            P("replica", None),
            P(None, None, "replica", None, "tensor", None),
            P(None, None, "replica", None, None, "tensor", None),
            P(),
            P(),
            P(),
            P(),
            P(),
            P(None, None, "tensor"),
            P(None, None, "tensor"),
            P(None, None, "tensor"),
            P(None, "tensor", None),
        ),
        out_specs=(
            P("replica", None),
            P("replica", None),
            P("replica", None, None, None, "tensor", None),
        ),
        check_vma=False,
    )
```

```python
import functools

import jax
import jax.numpy as jnp
import numpy as np
from jax import lax
from jax.experimental import pallas as pl
from jax.experimental.pallas import tpu as pltpu
from jax.sharding import PartitionSpec as P

EPSILON = 1e-06
ROPE_BASE = 1000000.0
NEGATIVE = -1e30
ROWS = 8
ANY = pl.BlockSpec(memory_space=pl.ANY)
VM = pl.BlockSpec(memory_space=pltpu.VMEM)
SM = pl.BlockSpec(memory_space=pltpu.SMEM)


def permute(value, axis, target):
    pairs = [(source, target(source)) for source in range(lax.axis_size(axis))]
    return lax.ppermute(value, axis, pairs)


def in_hbm(value):
    return pltpu.with_memory_space_constraint(value, pltpu.HBM)


def row_of(count):
    return lax.broadcasted_iota(jnp.int32, (count, 1), 0)


def attention_step(
    layer, group_ref, lengths_ref, long_lengths_ref, hidden, gain_ref, q_gain_ref, k_gain_ref,
    cosine_ref, sine_ref, stored, state_ref, side_ref, fresh_ref, ready,
):
    wq, wk, wv, keys, long_keys, values, long_values = stored
    rows = hidden()
    scale = lax.rsqrt(jnp.mean(rows * rows, axis=-1, keepdims=True) + EPSILON)
    normed = (rows * scale * gain_ref[layer : layer + 1, :]).astype(jnp.bfloat16)
    ready(0, 1, 2)
    queries = jnp.dot(normed, wq[...], preferred_element_type=jnp.float32)
    new_keys = jnp.dot(normed, wk[...], preferred_element_type=jnp.float32)
    new_values = jnp.dot(normed, wv[...], preferred_element_type=jnp.float32).astype(jnp.bfloat16)

    def finish(heads, gain, cosine, sine):
        heads = heads * lax.rsqrt(jnp.mean(heads * heads, axis=-1, keepdims=True) + EPSILON) * gain
        return (heads * cosine + pltpu.roll(heads, 64, 1) * sine).astype(jnp.bfloat16)

    cosine, sine = cosine_ref[...], sine_ref[...]
    q_gain = q_gain_ref[layer : layer + 1, :]
    q0 = finish(queries[:, :128], q_gain, cosine, sine).astype(jnp.float32)
    q1 = finish(queries[:, 128:], q_gain, cosine, sine).astype(jnp.float32)
    key_new = finish(new_keys, k_gain_ref[layer : layer + 1, :], cosine, sine).astype(jnp.float32)
    value_new = new_values.astype(jnp.float32)
    fresh_ref[0:1, :] = key_new[2:3, :]
    fresh_ref[1:2, :] = value_new[2:3, :]
    both = jnp.concatenate([q0, q1], axis=0)
    query = both.astype(jnp.bfloat16)
    keys_twice = jnp.concatenate([key_new, key_new], axis=0)
    values_twice = jnp.concatenate([value_new, value_new], axis=0)
    factor = 128 ** (-0.5)
    own = jnp.sum(both * keys_twice, axis=-1, keepdims=True) * factor

    group = group_ref[0]
    parity = lax.rem(group, 2)
    which = lax.rem(row_of(16), 8)
    limit = jnp.ones((16, 1), jnp.int32)
    for r in range(3):
        limit = jnp.where(which == r, lengths_ref[group * 3 + r], limit)
    for r in range(2):
        limit = jnp.where(
            which == 3 + r, long_lengths_ref[group - parity + r] - parity * 2048, limit
        )
    scores = jnp.zeros((16, 2048), jnp.float32)
    for r in range(5):
        if r == 0:
            ready(3)
        if r == 3:
            ready(4)
        block = keys[r] if r < 3 else long_keys[r - 3]
        product = lax.dot_general(
            query, block, (((1,), (1,)), ((), ())), preferred_element_type=jnp.float32
        )
        scores = jnp.where(which == r, product, scores)
    places = lax.broadcasted_iota(jnp.int32, (16, 2048), 1)
    scores = jnp.where(places < limit, scores * factor, NEGATIVE)
    is_main = which < 3
    highest = jnp.max(scores, axis=-1, keepdims=True)
    highest = jnp.where(is_main, jnp.maximum(highest, own), highest)
    weights = jnp.exp(scores - highest)
    own_weight = jnp.where(is_main, jnp.exp(own - highest), 0.0)
    total = jnp.sum(weights, axis=-1, keepdims=True) + own_weight
    rounded = weights.astype(jnp.bfloat16)
    summed = own_weight.astype(jnp.bfloat16).astype(jnp.float32) * values_twice
    for r in range(5):
        if r == 0:
            ready(5)
        if r == 3:
            ready(6)
        block = values[r] if r < 3 else long_values[r - 3]
        product = jnp.dot(rounded, block, preferred_element_type=jnp.float32)
        summed = summed + jnp.where(which == r, product, 0.0)
    state_ref[:, 0:128] = summed
    lanes = lax.broadcasted_iota(jnp.int32, (16, 128), 1)
    state_ref[:, 128:256] = jnp.where(lanes < 64, highest, total)
    side_ref[:, 0:128] = jnp.broadcast_to(own, (16, 128))
    side_ref[:, 128:256] = values_twice


def parts_of(layer, cache_ref, long_ref, wq_ref, wk_ref, wv_ref):
    return (
        wq_ref.at[layer], wk_ref.at[layer], wv_ref.at[layer],
        cache_ref.at[layer, 0], long_ref.at[layer, 0, 0],
        cache_ref.at[layer, 1], long_ref.at[layer, 1, 0],
    )


def first_kernel(
    group_ref, lengths_ref, long_lengths_ref, tokens_ref, own_long_ref, far_long_ref, *rest
):
    tables, held = rest[:5], rest[5:10]
    state_ref, side_ref, fresh_ref, hidden_ref = rest[10:14]
    buffers, semaphores = rest[14:21], rest[21]
    copies = [
        pltpu.make_async_copy(source, target, semaphores.at[i])
        for i, (source, target) in enumerate(zip(parts_of(0, *held), buffers))
    ]
    for copy in copies:
        copy.start()

    def ready(*which):
        for i in which:
            copies[i].wait()

    def hidden():
        own = own_long_ref[...].astype(jnp.float32)
        far = far_long_ref[...].astype(jnp.float32)
        even = lax.rem(group_ref[0], 2) == 0
        hidden_ref[...] = jnp.zeros((ROWS, 2048), jnp.float32)
        hidden_ref[0:3, :] = tokens_ref[...].astype(jnp.float32)
        hidden_ref[3:4, :] = jnp.where(even, own, far)
        hidden_ref[4:5, :] = jnp.where(even, far, own)
        return hidden_ref[...]

    attention_step(
        0, group_ref, lengths_ref, long_lengths_ref, hidden, *tables, buffers,
        state_ref, side_ref, fresh_ref, ready,
    )


def total_of(p_ref, r1_ref, r2_ref, r3_ref):
    p, r1, r2, r3 = (ref[...].astype(jnp.float32) for ref in (p_ref, r1_ref, r2_ref, r3_ref))
    return (p + r1) + (r2 + r3)


def second_kernel(
    group_ref, lengths_ref, long_lengths_ref, before_ref, p_ref, r1_ref, r2_ref, r3_ref, *rest
):
    tables, stored = rest[:5], rest[5:12]
    state_ref, side_ref, fresh_ref, hidden_ref = rest[12:16]

    def hidden():
        summed = total_of(p_ref, r1_ref, r2_ref, r3_ref)
        rows = (before_ref[...] + summed).astype(jnp.bfloat16).astype(jnp.float32)
        hidden_ref[...] = rows
        return rows

    attention_step(
        1, group_ref, lengths_ref, long_lengths_ref, hidden, *tables, stored,
        state_ref, side_ref, fresh_ref, lambda *which: None,
    )


def leaving_kernel(cache_ref, out_ref, semaphores):
    copies = [
        pltpu.make_async_copy(cache_ref.at[i, j, 2], out_ref.at[i, j], semaphores.at[2 * i + j])
        for i in range(2)
        for j in range(2)
    ]
    for copy in copies:
        copy.start()
    for copy in copies:
        copy.wait()


def arrival_kernel(
    length_ref, stay_ref, arrived_ref, moving_ref, out_ref, moved_ref, blocks, semaphores
):
    start = pl.multiple_of(length_ref[0] // 16 * 16, 16)
    places = [(i, j) for i in range(2) for j in range(2)]
    bodies = [
        pltpu.make_async_copy(moving_ref.at[i, j], moved_ref.at[i, j], semaphores.at[0, i, j])
        for i, j in places
    ]
    reads = [
        pltpu.make_async_copy(
            moving_ref.at[i, j, pl.ds(start, 16)], blocks.at[i, j], semaphores.at[1, i, j]
        )
        for i, j in places
    ]
    for copy in (*reads, *bodies):
        copy.start()
    out_ref[0:2, :] = stay_ref[...]
    out_ref[2:3, :] = arrived_ref[0:1, 0:2048]
    hit = row_of(16) == length_ref[0] - start
    for n, (i, j) in enumerate(places):
        fresh = arrived_ref[0:1, 2048 + 128 * n : 2176 + 128 * n]
        reads[n].wait()
        block = jnp.where(hit, fresh, blocks[i, j].astype(jnp.float32))
        blocks[i, j] = block.astype(jnp.bfloat16)
    writes = []
    for n, (i, j) in enumerate(places):
        bodies[n].wait()
        writes.append(
            pltpu.make_async_copy(
                blocks.at[i, j], moved_ref.at[i, j, pl.ds(start, 16)], semaphores.at[2, i, j]
            )
        )
        writes[-1].start()
    for copy in writes:
        copy.wait()


def fetch_kernel(*refs):
    held, outputs, semaphores = refs[:5], refs[5:12], refs[12]
    copies = [
        pltpu.make_async_copy(source, target, semaphores.at[i])
        for i, (source, target) in enumerate(zip(parts_of(1, *held), outputs))
    ]
    for copy in copies:
        copy.start()
    for copy in copies:
        copy.wait()


def out_kernel(layer, state_ref, far_ref, side_ref, w_ref, out_ref, w, semaphore):
    copy = pltpu.make_async_copy(w_ref.at[layer], w, semaphore)
    copy.start()
    is_main = lax.rem(row_of(16), 8) < 3
    here, far = state_ref[...], far_ref[...]
    m_here, l_here, acc_here = here[:, 128:129], here[:, 192:193], here[:, :128]
    m_far, l_far, acc_far = far[:, 128:129], far[:, 192:193], far[:, :128]
    own, value = side_ref[:, 0:1], side_ref[:, 128:256]
    highest = jnp.maximum(jnp.maximum(m_here, m_far), own)
    f_here, f_far = jnp.exp(m_here - highest), jnp.exp(m_far - highest)
    own_weight = jnp.exp(own - highest)
    total = (l_here * f_here + l_far * f_far) + own_weight
    own_rounded = own_weight.astype(jnp.bfloat16).astype(jnp.float32)
    summed = (acc_here * f_here + acc_far * f_far) + own_rounded * value
    total = jnp.where(is_main, l_here, total)
    summed = jnp.where(is_main, acc_here, summed)
    attended = summed / total
    attended = jnp.concatenate([attended[:8], attended[8:]], axis=1).astype(jnp.bfloat16)
    copy.wait()
    out_ref[...] = jnp.dot(attended, w[...], preferred_element_type=jnp.float32)


def final_kernel(
    group_ref, before_ref, p_ref, r1_ref, r2_ref, r3_ref, fresh0_ref, fresh1_ref,
    stay_ref, long_ref, leave_ref, scratch,
):
    scratch[...] = before_ref[...] + total_of(p_ref, r1_ref, r2_ref, r3_ref)
    stay_ref[...] = scratch[0:2, :]
    odd = lax.rem(group_ref[0], 2) == 1
    long_ref[...] = jnp.where(odd, scratch[4:5, :], scratch[3:4, :])
    leave_ref[0:1, 0:2048] = scratch[2:3, :]
    for i, ref in enumerate((fresh0_ref, fresh1_ref)):
        for j in range(2):
            leave_ref[0:1, 2048 + 128 * (2 * i + j) : 2176 + 128 * (2 * i + j)] = ref[j : j + 1, :]


def local(
    tokens, long_tokens, cache, long_cache, lengths, long_lengths, norm_gain, q_gain, k_gain,
    w_query, key_weight, value_weight, w_out,
):
    groups = lax.axis_size("replica")
    group = lax.axis_index("replica")
    parity = group % 2
    group_1 = group[None]
    cache = cache.reshape(2, 2, 3, 2048, 128)
    long_cache = long_cache.reshape(2, 2, 1, 2, 2048, 128)

    far_token = permute(long_tokens, "replica", lambda i: i ^ 1)
    params = pltpu.CompilerParams(vmem_limit_bytes=16 * 2**20)
    small = pltpu.CompilerParams(vmem_limit_bytes=2 * 2**20)
    held = in_hbm(cache)
    leaving = pl.pallas_call(
        leaving_kernel,
        out_shape=jax.ShapeDtypeStruct((2, 2, 2048, 128), jnp.bfloat16),
        in_specs=[ANY],
        out_specs=ANY,
        scratch_shapes=[pltpu.SemaphoreType.DMA((4,))],
        compiler_params=small,
        name="leaving_cache",
    )(held)
    moving = permute(leaving, "replica", lambda i: (i + groups // 2) % groups)

    places = jnp.concatenate(
        [
            lax.dynamic_slice_in_dim(lengths, group * 3, 3),
            lax.dynamic_slice_in_dim(long_lengths, group - parity, 2),
            jnp.zeros((3,), jnp.int32),
        ]
    ).astype(jnp.float32)
    inverse = np.float64(ROPE_BASE) ** (-2.0 * np.arange(64) / 128)
    inverse = jnp.asarray(np.concatenate([inverse, inverse]).astype(np.float32))
    sign = jnp.asarray(np.where(np.arange(128) < 64, -1.0, 1.0).astype(np.float32))
    angles = places[:, None] * inverse[None, :]
    cosine, sine = jnp.cos(angles), jnp.sin(angles) * sign

    out_shape = (
        jax.ShapeDtypeStruct((16, 256), jnp.float32),
        jax.ShapeDtypeStruct((16, 256), jnp.float32),
        jax.ShapeDtypeStruct((2, 128), jnp.float32),
        jax.ShapeDtypeStruct((ROWS, 2048), jnp.float32),
    )
    scratch = [
        pltpu.VMEM((2048, 256), jnp.bfloat16),
        pltpu.VMEM((2048, 128), jnp.bfloat16),
        pltpu.VMEM((2048, 128), jnp.bfloat16),
        pltpu.VMEM((3, 2048, 128), jnp.bfloat16),
        pltpu.VMEM((2, 2048, 128), jnp.bfloat16),
        pltpu.VMEM((3, 2048, 128), jnp.bfloat16),
        pltpu.VMEM((2, 2048, 128), jnp.bfloat16),
        pltpu.SemaphoreType.DMA((7,)),
    ]
    stored = (cache, long_cache, w_query, key_weight, value_weight)
    tables = (norm_gain, q_gain, k_gain, cosine, sine)

    def project_out(layer, state, side):
        far = permute(state, "replica", lambda i: i ^ 1)
        part = pl.pallas_call(
            functools.partial(out_kernel, layer),
            out_shape=jax.ShapeDtypeStruct((ROWS, 2048), jnp.float32),
            in_specs=[VM, VM, VM, ANY],
            out_specs=VM,
            scratch_shapes=[pltpu.VMEM((256, 2048), jnp.bfloat16), pltpu.SemaphoreType.DMA(())],
            compiler_params=params,
            name=f"out_projection_{layer}",
        )(state, far, side, w_out)
        part = (part + permute(part, "tensor", lambda i: i ^ 1)).astype(jnp.bfloat16)
        received = [permute(part, "tensor", lambda i, k=k: i ^ k) for k in (2, 4, 6)]
        return (part, *received)

    state, side, fresh_0, hidden = pl.pallas_call(
        first_kernel,
        out_shape=out_shape,
        in_specs=[SM] * 3 + [VM] * 8 + [ANY] * 5,
        out_specs=(VM,) * 4,
        scratch_shapes=scratch,
        compiler_params=params,
        name="attention_0",
    )(group_1, lengths, long_lengths, tokens, long_tokens, far_token, *tables, *map(in_hbm, stored))
    terms = project_out(0, state, side)
    buffers = ((2048, 256), (2048, 128), (2048, 128)) + ((3, 2048, 128), (2, 2048, 128)) * 2
    gate, *stored = lax.optimization_barrier((terms[0], *stored))
    terms = (gate, *terms[1:])
    stored = pl.pallas_call(
        fetch_kernel,
        out_shape=tuple(pltpu.VMEM(shape, jnp.bfloat16) for shape in buffers),
        in_specs=[ANY] * 5,
        out_specs=(ANY,) * 7,
        scratch_shapes=[pltpu.SemaphoreType.DMA((7,))],
        compiler_params=small,
        name="fetch_1",
    )(*map(in_hbm, stored))
    state, side, fresh_1, hidden = pl.pallas_call(
        second_kernel,
        out_shape=out_shape,
        in_specs=[SM] * 3 + [VM] * 17,
        out_specs=(VM,) * 4,
        compiler_params=params,
        name="attention_1",
    )(group_1, lengths, long_lengths, hidden, *terms, *tables, *stored)
    terms = project_out(1, state, side)
    stay, long_out, leave = pl.pallas_call(
        final_kernel,
        out_shape=(
            jax.ShapeDtypeStruct((2, 2048), jnp.float32),
            jax.ShapeDtypeStruct((1, 2048), jnp.float32),
            jax.ShapeDtypeStruct((1, 2560), jnp.float32),
        ),
        in_specs=[SM] + [VM] * 7,
        out_specs=(VM,) * 3,
        scratch_shapes=[pltpu.VMEM((ROWS, 2048), jnp.float32)],
        compiler_params=params,
        name="final_rows",
    )(group_1, hidden, *terms, fresh_0, fresh_1)
    arrived = permute(leave, "replica", lambda i: (i + groups // 2) % groups)
    partner = (group + groups // 2) % groups
    arrived_len = lax.dynamic_slice_in_dim(lengths, partner * 3 + 2, 1)
    out_hidden, moved = pl.pallas_call(
        arrival_kernel,
        out_shape=(
            jax.ShapeDtypeStruct((3, 2048), jnp.float32),
            jax.ShapeDtypeStruct((2, 2, 2048, 128), jnp.bfloat16),
        ),
        in_specs=[SM, VM, VM, ANY],
        out_specs=(VM, ANY),
        scratch_shapes=[
            pltpu.VMEM((2, 2, 16, 128), jnp.bfloat16),
            pltpu.SemaphoreType.DMA((3, 2, 2)),
        ],
        compiler_params=small,
        name="arrival",
    )(arrived_len, stay, arrived, moving)
    return (out_hidden, long_out, moved[None, :, :, :, None, :])


def solution(mesh):
    return jax.shard_map(
        local,
        mesh=mesh,
        in_specs=(
            P("replica", None),
            P("replica", None),
            P(None, None, "replica", None, "tensor", None),
            P(None, None, "replica", None, None, "tensor", None),
            P(),
            P(),
            P(),
            P(),
            P(),
            P(None, None, "tensor"),
            P(None, None, "tensor"),
            P(None, None, "tensor"),
            P(None, "tensor", None),
        ),
        out_specs=(
            P("replica", None),
            P("replica", None),
            P("replica", None, None, None, "tensor", None),
        ),
        check_vma=False,
    )
```

```python
import functools

import jax
import jax.numpy as jnp
import numpy as np
from jax import lax
from jax.experimental import pallas as pl
from jax.experimental.pallas import tpu as pltpu
from jax.sharding import PartitionSpec as P

EPSILON = 1e-06
ROPE_BASE = 1000000.0
NEGATIVE = -1e30
ROWS = 8
ANY = pl.BlockSpec(memory_space=pl.ANY)
VM = pl.BlockSpec(memory_space=pltpu.VMEM)
SM = pl.BlockSpec(memory_space=pltpu.SMEM)


def permute(value, axis, target):
    pairs = [(source, target(source)) for source in range(lax.axis_size(axis))]
    return lax.ppermute(value, axis, pairs)


def in_hbm(value):
    return pltpu.with_memory_space_constraint(value, pltpu.HBM)


def in_vmem(value):
    return pltpu.with_memory_space_constraint(value, pltpu.VMEM)


def row_of(count):
    return lax.broadcasted_iota(jnp.int32, (count, 1), 0)


def attention_step(
    layer, group_ref, lengths_ref, long_lengths_ref, hidden, gain_ref, q_gain_ref, k_gain_ref,
    cosine_ref, sine_ref, stored, state_ref, side_ref, fresh_ref, ready,
):
    wq, wk, wv, keys, long_keys, values, long_values = stored
    rows = hidden()
    scale = lax.rsqrt(jnp.mean(rows * rows, axis=-1, keepdims=True) + EPSILON)
    normed = (rows * scale * gain_ref[layer : layer + 1, :]).astype(jnp.bfloat16)
    ready(0, 1, 2)
    queries = jnp.dot(normed, wq[...], preferred_element_type=jnp.float32)
    new_keys = jnp.dot(normed, wk[...], preferred_element_type=jnp.float32)
    new_values = jnp.dot(normed, wv[...], preferred_element_type=jnp.float32).astype(jnp.bfloat16)

    def finish(heads, gain, cosine, sine):
        heads = heads * lax.rsqrt(jnp.mean(heads * heads, axis=-1, keepdims=True) + EPSILON) * gain
        return (heads * cosine + pltpu.roll(heads, 64, 1) * sine).astype(jnp.bfloat16)

    cosine, sine = cosine_ref[...], sine_ref[...]
    q_gain = q_gain_ref[layer : layer + 1, :]
    q0 = finish(queries[:, :128], q_gain, cosine, sine).astype(jnp.float32)
    q1 = finish(queries[:, 128:], q_gain, cosine, sine).astype(jnp.float32)
    key_new = finish(new_keys, k_gain_ref[layer : layer + 1, :], cosine, sine).astype(jnp.float32)
    value_new = new_values.astype(jnp.float32)
    fresh_ref[0:1, :] = key_new[2:3, :]
    fresh_ref[1:2, :] = value_new[2:3, :]
    both = jnp.concatenate([q0, q1], axis=0)
    query = both.astype(jnp.bfloat16)
    keys_twice = jnp.concatenate([key_new, key_new], axis=0)
    values_twice = jnp.concatenate([value_new, value_new], axis=0)
    factor = 128 ** (-0.5)
    own = jnp.sum(both * keys_twice, axis=-1, keepdims=True) * factor

    group = group_ref[0]
    parity = lax.rem(group, 2)
    which = lax.rem(row_of(16), 8)
    limit = jnp.ones((16, 1), jnp.int32)
    for r in range(3):
        limit = jnp.where(which == r, lengths_ref[group * 3 + r], limit)
    for r in range(2):
        limit = jnp.where(
            which == 3 + r, long_lengths_ref[group - parity + r] - parity * 2048, limit
        )
    scores = jnp.zeros((16, 2048), jnp.float32)
    for r in range(5):
        if r == 0:
            ready(3)
        if r == 3:
            ready(4)
        block = keys[r] if r < 3 else long_keys[r - 3]
        product = lax.dot_general(
            query, block, (((1,), (1,)), ((), ())), preferred_element_type=jnp.float32
        )
        scores = jnp.where(which == r, product, scores)
    places = lax.broadcasted_iota(jnp.int32, (16, 2048), 1)
    scores = jnp.where(places < limit, scores * factor, NEGATIVE)
    is_main = which < 3
    highest = jnp.max(scores, axis=-1, keepdims=True)
    highest = jnp.where(is_main, jnp.maximum(highest, own), highest)
    weights = jnp.exp(scores - highest)
    own_weight = jnp.where(is_main, jnp.exp(own - highest), 0.0)
    total = jnp.sum(weights, axis=-1, keepdims=True) + own_weight
    rounded = weights.astype(jnp.bfloat16)
    summed = own_weight.astype(jnp.bfloat16).astype(jnp.float32) * values_twice
    for r in range(5):
        if r == 0:
            ready(5)
        if r == 3:
            ready(6)
        block = values[r] if r < 3 else long_values[r - 3]
        product = jnp.dot(rounded, block, preferred_element_type=jnp.float32)
        summed = summed + jnp.where(which == r, product, 0.0)
    state_ref[:, 0:128] = summed
    lanes = lax.broadcasted_iota(jnp.int32, (16, 128), 1)
    state_ref[:, 128:256] = jnp.where(lanes < 64, highest, total)
    side_ref[:, 0:128] = jnp.broadcast_to(own, (16, 128))
    side_ref[:, 128:256] = values_twice


def parts_of(layer, cache_ref, long_ref, wq_ref, wk_ref, wv_ref):
    return (
        wq_ref.at[layer], wk_ref.at[layer], wv_ref.at[layer],
        cache_ref.at[layer, 0], long_ref.at[layer, 0, 0],
        cache_ref.at[layer, 1], long_ref.at[layer, 1, 0],
    )


def first_kernel(
    group_ref, lengths_ref, long_lengths_ref, tokens_ref, own_long_ref, far_long_ref, *rest
):
    tables, held = rest[:5], rest[5:10]
    state_ref, side_ref, fresh_ref, hidden_ref = rest[10:14]
    buffers, semaphores = rest[14:21], rest[21]
    copies = [
        pltpu.make_async_copy(source, target, semaphores.at[i])
        for i, (source, target) in enumerate(zip(parts_of(0, *held), buffers))
    ]
    for copy in copies:
        copy.start()

    def ready(*which):
        for i in which:
            copies[i].wait()

    def hidden():
        own = own_long_ref[...].astype(jnp.float32)
        far = far_long_ref[...].astype(jnp.float32)
        even = lax.rem(group_ref[0], 2) == 0
        hidden_ref[...] = jnp.zeros((ROWS, 2048), jnp.float32)
        hidden_ref[0:3, :] = tokens_ref[...].astype(jnp.float32)
        hidden_ref[3:4, :] = jnp.where(even, own, far)
        hidden_ref[4:5, :] = jnp.where(even, far, own)
        return hidden_ref[...]

    attention_step(
        0, group_ref, lengths_ref, long_lengths_ref, hidden, *tables, buffers,
        state_ref, side_ref, fresh_ref, ready,
    )


def total_of(p_ref, r1_ref, r2_ref, r3_ref):
    p, r1, r2, r3 = (ref[...].astype(jnp.float32) for ref in (p_ref, r1_ref, r2_ref, r3_ref))
    return (p + r1) + (r2 + r3)


def second_kernel(
    group_ref, lengths_ref, long_lengths_ref, before_ref, p_ref, r1_ref, r2_ref, r3_ref, *rest
):
    tables, stored = rest[:5], rest[5:12]
    state_ref, side_ref, fresh_ref, hidden_ref = rest[12:16]

    def hidden():
        summed = total_of(p_ref, r1_ref, r2_ref, r3_ref)
        rows = (before_ref[...] + summed).astype(jnp.bfloat16).astype(jnp.float32)
        hidden_ref[...] = rows
        return rows

    attention_step(
        1, group_ref, lengths_ref, long_lengths_ref, hidden, *tables, stored,
        state_ref, side_ref, fresh_ref, lambda *which: None,
    )


def leaving_kernel(cache_ref, out_ref, semaphores):
    copies = [
        pltpu.make_async_copy(cache_ref.at[i, j, 2], out_ref.at[i, j], semaphores.at[2 * i + j])
        for i in range(2)
        for j in range(2)
    ]
    for copy in copies:
        copy.start()
    for copy in copies:
        copy.wait()


def arrival_kernel(
    length_ref, stay_ref, arrived_ref, moving_ref, out_ref, moved_ref, rows, blocks, semaphores
):
    places = [(i, j) for i in range(2) for j in range(2)]
    bodies = [
        pltpu.make_async_copy(moving_ref.at[i, j], moved_ref.at[i, j], semaphores.at[2 * i + j])
        for i, j in places
    ]
    for copy in bodies:
        copy.start()
    rows[0:2, :] = stay_ref[...]
    rows[2:3, :] = arrived_ref[0:1, 0:2048]
    out = pltpu.make_async_copy(rows, out_ref, semaphores.at[8])
    out.start()
    start = pl.multiple_of(length_ref[0] // 16 * 16, 16)
    hit = row_of(16) == length_ref[0] - start
    for n, (i, j) in enumerate(places):
        fresh = arrived_ref[0:1, 2048 + 128 * n : 2176 + 128 * n]
        block = moving_ref[i, j, pl.ds(start, 16), :].astype(jnp.float32)
        blocks[i, j] = jnp.where(hit, fresh, block).astype(jnp.bfloat16)
    writes = [
        pltpu.make_async_copy(
            blocks.at[i, j], moved_ref.at[i, j, pl.ds(start, 16)], semaphores.at[4 + 2 * i + j]
        )
        for i, j in places
    ]
    for body, write in zip(bodies, writes):
        body.wait()
        write.start()
    for write in writes:
        write.wait()
    out.wait()


def fetch_kernel(*refs):
    held, outputs, semaphores = refs[:5], refs[5:12], refs[12]
    copies = [
        pltpu.make_async_copy(source, target, semaphores.at[i])
        for i, (source, target) in enumerate(zip(parts_of(1, *held), outputs))
    ]
    for copy in copies:
        copy.start()
    for copy in copies:
        copy.wait()


def out_kernel(layer, state_ref, far_ref, side_ref, w_ref, out_ref, w, semaphore):
    copy = pltpu.make_async_copy(w_ref.at[layer], w, semaphore)
    copy.start()
    is_main = lax.rem(row_of(16), 8) < 3
    here, far = state_ref[...], far_ref[...]
    m_here, l_here, acc_here = here[:, 128:129], here[:, 192:193], here[:, :128]
    m_far, l_far, acc_far = far[:, 128:129], far[:, 192:193], far[:, :128]
    own, value = side_ref[:, 0:1], side_ref[:, 128:256]
    highest = jnp.maximum(jnp.maximum(m_here, m_far), own)
    f_here, f_far = jnp.exp(m_here - highest), jnp.exp(m_far - highest)
    own_weight = jnp.exp(own - highest)
    total = (l_here * f_here + l_far * f_far) + own_weight
    own_rounded = own_weight.astype(jnp.bfloat16).astype(jnp.float32)
    summed = (acc_here * f_here + acc_far * f_far) + own_rounded * value
    total = jnp.where(is_main, l_here, total)
    summed = jnp.where(is_main, acc_here, summed)
    attended = summed / total
    attended = jnp.concatenate([attended[:8], attended[8:]], axis=1).astype(jnp.bfloat16)
    copy.wait()
    out_ref[...] = jnp.dot(attended, w[...], preferred_element_type=jnp.float32)


def final_kernel(
    group_ref, before_ref, p_ref, r1_ref, r2_ref, r3_ref, fresh0_ref, fresh1_ref,
    stay_ref, long_ref, leave_ref, scratch,
):
    scratch[...] = before_ref[...] + total_of(p_ref, r1_ref, r2_ref, r3_ref)
    stay_ref[...] = scratch[0:2, :]
    odd = lax.rem(group_ref[0], 2) == 1
    long_ref[...] = jnp.where(odd, scratch[4:5, :], scratch[3:4, :])
    leave_ref[0:1, 0:2048] = scratch[2:3, :]
    for i, ref in enumerate((fresh0_ref, fresh1_ref)):
        for j in range(2):
            leave_ref[0:1, 2048 + 128 * (2 * i + j) : 2176 + 128 * (2 * i + j)] = ref[j : j + 1, :]


def local(
    tokens, long_tokens, cache, long_cache, lengths, long_lengths, norm_gain, q_gain, k_gain,
    w_query, key_weight, value_weight, w_out,
):
    groups = lax.axis_size("replica")
    group = lax.axis_index("replica")
    parity = group % 2
    group_1 = group[None]
    cache = cache.reshape(2, 2, 3, 2048, 128)
    long_cache = long_cache.reshape(2, 2, 1, 2, 2048, 128)

    far_token = permute(long_tokens, "replica", lambda i: i ^ 1)
    params = pltpu.CompilerParams(vmem_limit_bytes=16 * 2**20)
    small = pltpu.CompilerParams(vmem_limit_bytes=2 * 2**20)
    held = in_hbm(cache)
    leaving = pl.pallas_call(
        leaving_kernel,
        out_shape=pltpu.VMEM((2, 2, 2048, 128), jnp.bfloat16),
        in_specs=[ANY],
        out_specs=ANY,
        scratch_shapes=[pltpu.SemaphoreType.DMA((4,))],
        compiler_params=small,
        name="leaving_cache",
    )(held)
    moving = permute(leaving, "replica", lambda i: (i + groups // 2) % groups)

    places = jnp.concatenate(
        [
            lax.dynamic_slice_in_dim(lengths, group * 3, 3),
            lax.dynamic_slice_in_dim(long_lengths, group - parity, 2),
            jnp.zeros((3,), jnp.int32),
        ]
    ).astype(jnp.float32)
    inverse = np.float64(ROPE_BASE) ** (-2.0 * np.arange(64) / 128)
    inverse = jnp.asarray(np.concatenate([inverse, inverse]).astype(np.float32))
    sign = jnp.asarray(np.where(np.arange(128) < 64, -1.0, 1.0).astype(np.float32))
    angles = places[:, None] * inverse[None, :]
    cosine, sine = jnp.cos(angles), jnp.sin(angles) * sign

    out_shape = (
        jax.ShapeDtypeStruct((16, 256), jnp.float32),
        jax.ShapeDtypeStruct((16, 256), jnp.float32),
        jax.ShapeDtypeStruct((2, 128), jnp.float32),
        jax.ShapeDtypeStruct((ROWS, 2048), jnp.float32),
    )
    scratch = [
        pltpu.VMEM((2048, 256), jnp.bfloat16),
        pltpu.VMEM((2048, 128), jnp.bfloat16),
        pltpu.VMEM((2048, 128), jnp.bfloat16),
        pltpu.VMEM((3, 2048, 128), jnp.bfloat16),
        pltpu.VMEM((2, 2048, 128), jnp.bfloat16),
        pltpu.VMEM((3, 2048, 128), jnp.bfloat16),
        pltpu.VMEM((2, 2048, 128), jnp.bfloat16),
        pltpu.SemaphoreType.DMA((7,)),
    ]
    stored = (cache, long_cache, w_query, key_weight, value_weight)
    tables = (norm_gain, q_gain, k_gain, cosine, sine)

    def project_out(layer, state, side):
        far = permute(state, "replica", lambda i: i ^ 1)
        part = pl.pallas_call(
            functools.partial(out_kernel, layer),
            out_shape=jax.ShapeDtypeStruct((ROWS, 2048), jnp.float32),
            in_specs=[VM, VM, VM, ANY],
            out_specs=VM,
            scratch_shapes=[pltpu.VMEM((256, 2048), jnp.bfloat16), pltpu.SemaphoreType.DMA(())],
            compiler_params=params,
            name=f"out_projection_{layer}",
        )(state, far, side, w_out)
        part = (part + permute(part, "tensor", lambda i: i ^ 1)).astype(jnp.bfloat16)
        received = [permute(part, "tensor", lambda i, k=k: i ^ k) for k in (2, 4, 6)]
        return (part, *received)

    state, side, fresh_0, hidden = pl.pallas_call(
        first_kernel,
        out_shape=out_shape,
        in_specs=[SM] * 3 + [VM] * 8 + [ANY] * 5,
        out_specs=(VM,) * 4,
        scratch_shapes=scratch,
        compiler_params=params,
        name="attention_0",
    )(group_1, lengths, long_lengths, tokens, long_tokens, far_token, *tables, *map(in_hbm, stored))
    terms = project_out(0, state, side)
    buffers = ((2048, 256), (2048, 128), (2048, 128)) + ((3, 2048, 128), (2, 2048, 128)) * 2
    gate, *stored = lax.optimization_barrier((terms[0], *stored))
    terms = (gate, *terms[1:])
    stored = pl.pallas_call(
        fetch_kernel,
        out_shape=tuple(pltpu.VMEM(shape, jnp.bfloat16) for shape in buffers),
        in_specs=[ANY] * 5,
        out_specs=(ANY,) * 7,
        scratch_shapes=[pltpu.SemaphoreType.DMA((7,))],
        compiler_params=small,
        name="fetch_1",
    )(*map(in_hbm, stored))
    state, side, fresh_1, hidden = pl.pallas_call(
        second_kernel,
        out_shape=out_shape,
        in_specs=[SM] * 3 + [VM] * 17,
        out_specs=(VM,) * 4,
        compiler_params=params,
        name="attention_1",
    )(group_1, lengths, long_lengths, hidden, *terms, *tables, *stored)
    terms = project_out(1, state, side)
    stay, long_out, leave = pl.pallas_call(
        final_kernel,
        out_shape=(
            jax.ShapeDtypeStruct((2, 2048), jnp.float32),
            jax.ShapeDtypeStruct((1, 2048), jnp.float32),
            jax.ShapeDtypeStruct((1, 2560), jnp.float32),
        ),
        in_specs=[SM] + [VM] * 7,
        out_specs=(VM,) * 3,
        scratch_shapes=[pltpu.VMEM((ROWS, 2048), jnp.float32)],
        compiler_params=params,
        name="final_rows",
    )(group_1, hidden, *terms, fresh_0, fresh_1)
    arrived = permute(leave, "replica", lambda i: (i + groups // 2) % groups)
    partner = (group + groups // 2) % groups
    arrived_len = lax.dynamic_slice_in_dim(lengths, partner * 3 + 2, 1)
    out_hidden, moved = pl.pallas_call(
        arrival_kernel,
        out_shape=(
            pltpu.HBM((3, 2048), jnp.float32),
            pltpu.HBM((2, 2, 2048, 128), jnp.bfloat16),
        ),
        in_specs=[SM, VM, VM, VM],
        out_specs=(ANY, ANY),
        scratch_shapes=[
            pltpu.VMEM((3, 2048), jnp.float32),
            pltpu.VMEM((2, 2, 16, 128), jnp.bfloat16),
            pltpu.SemaphoreType.DMA((9,)),
        ],
        compiler_params=small,
        name="arrival",
    )(arrived_len, stay, arrived, in_vmem(moving))
    return (out_hidden, long_out, moved[None, :, :, :, None, :])


def solution(mesh):
    return jax.shard_map(
        local,
        mesh=mesh,
        in_specs=(
            P("replica", None),
            P("replica", None),
            P(None, None, "replica", None, "tensor", None),
            P(None, None, "replica", None, None, "tensor", None),
            P(),
            P(),
            P(),
            P(),
            P(),
            P(None, None, "tensor"),
            P(None, None, "tensor"),
            P(None, None, "tensor"),
            P(None, "tensor", None),
        ),
        out_specs=(
            P("replica", None),
            P("replica", None),
            P("replica", None, None, None, "tensor", None),
        ),
        check_vma=False,
    )
```

```python
import functools

import jax
import jax.numpy as jnp
import numpy as np
from jax import lax
from jax.experimental import pallas as pl
from jax.experimental.pallas import tpu as pltpu
from jax.sharding import PartitionSpec as P

EPSILON = 1e-06
ROPE_BASE = 1000000.0
NEGATIVE = -1e30
ROWS = 8
ANY = pl.BlockSpec(memory_space=pl.ANY)
VM = pl.BlockSpec(memory_space=pltpu.VMEM)
SM = pl.BlockSpec(memory_space=pltpu.SMEM)


def permute(value, axis, target):
    pairs = [(source, target(source)) for source in range(lax.axis_size(axis))]
    return lax.ppermute(value, axis, pairs)


def in_hbm(value):
    return pltpu.with_memory_space_constraint(value, pltpu.HBM)


def in_vmem(value):
    return pltpu.with_memory_space_constraint(value, pltpu.VMEM)


def row_of(count):
    return lax.broadcasted_iota(jnp.int32, (count, 1), 0)


def attention_step(
    layer, group_ref, lengths_ref, long_lengths_ref, hidden, gain_ref, q_gain_ref, k_gain_ref,
    cosine_ref, sine_ref, stored, state_ref, side_ref, fresh_ref, ready,
):
    wq, wk, wv, keys, long_keys, values, long_values = stored
    rows = hidden()
    scale = lax.rsqrt(jnp.mean(rows * rows, axis=-1, keepdims=True) + EPSILON)
    normed = (rows * scale * gain_ref[layer : layer + 1, :]).astype(jnp.bfloat16)
    ready(0, 1, 2)
    queries = jnp.dot(normed, wq[...], preferred_element_type=jnp.float32)
    new_keys = jnp.dot(normed, wk[...], preferred_element_type=jnp.float32)
    new_values = jnp.dot(normed, wv[...], preferred_element_type=jnp.float32).astype(jnp.bfloat16)

    def finish(heads, gain, cosine, sine):
        heads = heads * lax.rsqrt(jnp.mean(heads * heads, axis=-1, keepdims=True) + EPSILON) * gain
        return (heads * cosine + pltpu.roll(heads, 64, 1) * sine).astype(jnp.bfloat16)

    cosine, sine = cosine_ref[...], sine_ref[...]
    q_gain = q_gain_ref[layer : layer + 1, :]
    q0 = finish(queries[:, :128], q_gain, cosine, sine).astype(jnp.float32)
    q1 = finish(queries[:, 128:], q_gain, cosine, sine).astype(jnp.float32)
    key_new = finish(new_keys, k_gain_ref[layer : layer + 1, :], cosine, sine).astype(jnp.float32)
    value_new = new_values.astype(jnp.float32)
    fresh_ref[0:1, :] = key_new[2:3, :]
    fresh_ref[1:2, :] = value_new[2:3, :]
    both = jnp.concatenate([q0, q1], axis=0)
    query = both.astype(jnp.bfloat16)
    keys_twice = jnp.concatenate([key_new, key_new], axis=0)
    values_twice = jnp.concatenate([value_new, value_new], axis=0)
    factor = 128 ** (-0.5)
    own = jnp.sum(both * keys_twice, axis=-1, keepdims=True) * factor

    group = group_ref[0]
    parity = lax.rem(group, 2)
    which = lax.rem(row_of(16), 8)
    limit = jnp.ones((16, 1), jnp.int32)
    for r in range(3):
        limit = jnp.where(which == r, lengths_ref[group * 3 + r], limit)
    for r in range(2):
        limit = jnp.where(
            which == 3 + r, long_lengths_ref[group - parity + r] - parity * 2048, limit
        )
    scores = jnp.zeros((16, 2048), jnp.float32)
    for r in range(5):
        if r == 0:
            ready(3)
        if r == 3:
            ready(4)
        block = keys[r] if r < 3 else long_keys[r - 3]
        product = lax.dot_general(
            query, block, (((1,), (1,)), ((), ())), preferred_element_type=jnp.float32
        )
        scores = jnp.where(which == r, product, scores)
    places = lax.broadcasted_iota(jnp.int32, (16, 2048), 1)
    scores = jnp.where(places < limit, scores * factor, NEGATIVE)
    is_main = which < 3
    highest = jnp.max(scores, axis=-1, keepdims=True)
    highest = jnp.where(is_main, jnp.maximum(highest, own), highest)
    weights = jnp.exp(scores - highest)
    own_weight = jnp.where(is_main, jnp.exp(own - highest), 0.0)
    total = jnp.sum(weights, axis=-1, keepdims=True) + own_weight
    rounded = weights.astype(jnp.bfloat16)
    summed = own_weight.astype(jnp.bfloat16).astype(jnp.float32) * values_twice
    for r in range(5):
        if r == 0:
            ready(5)
        if r == 3:
            ready(6)
        block = values[r] if r < 3 else long_values[r - 3]
        product = jnp.dot(rounded, block, preferred_element_type=jnp.float32)
        summed = summed + jnp.where(which == r, product, 0.0)
    state_ref[:, 0:128] = summed
    lanes = lax.broadcasted_iota(jnp.int32, (16, 128), 1)
    state_ref[:, 128:256] = jnp.where(lanes < 64, highest, total)
    side_ref[:, 0:128] = jnp.broadcast_to(own, (16, 128))
    side_ref[:, 128:256] = values_twice


def parts_of(layer, cache_ref, long_ref, wq_ref, wk_ref, wv_ref):
    return (
        wq_ref.at[layer], wk_ref.at[layer], wv_ref.at[layer],
        cache_ref.at[layer, 0], long_ref.at[layer, 0, 0],
        cache_ref.at[layer, 1], long_ref.at[layer, 1, 0],
    )


def first_kernel(
    group_ref, lengths_ref, long_lengths_ref, tokens_ref, own_long_ref, far_long_ref, *rest
):
    tables, held = rest[:5], rest[5:10]
    state_ref, side_ref, fresh_ref, hidden_ref = rest[10:14]
    buffers, semaphores = rest[14:21], rest[21]
    copies = [
        pltpu.make_async_copy(source, target, semaphores.at[i])
        for i, (source, target) in enumerate(zip(parts_of(0, *held), buffers))
    ]
    for copy in copies:
        copy.start()

    def ready(*which):
        for i in which:
            copies[i].wait()

    def hidden():
        own = own_long_ref[...].astype(jnp.float32)
        far = far_long_ref[...].astype(jnp.float32)
        even = lax.rem(group_ref[0], 2) == 0
        hidden_ref[...] = jnp.zeros((ROWS, 2048), jnp.float32)
        hidden_ref[0:3, :] = tokens_ref[...].astype(jnp.float32)
        hidden_ref[3:4, :] = jnp.where(even, own, far)
        hidden_ref[4:5, :] = jnp.where(even, far, own)
        return hidden_ref[...]

    attention_step(
        0, group_ref, lengths_ref, long_lengths_ref, hidden, *tables, buffers,
        state_ref, side_ref, fresh_ref, ready,
    )


def total_of(p_ref, r1_ref, r2_ref, r3_ref):
    p, r1, r2, r3 = (ref[...].astype(jnp.float32) for ref in (p_ref, r1_ref, r2_ref, r3_ref))
    return (p + r1) + (r2 + r3)


def second_kernel(
    group_ref, lengths_ref, long_lengths_ref, before_ref, p_ref, r1_ref, r2_ref, r3_ref, *rest
):
    tables, stored = rest[:5], rest[5:12]
    state_ref, side_ref, fresh_ref, hidden_ref = rest[12:16]

    def hidden():
        summed = total_of(p_ref, r1_ref, r2_ref, r3_ref)
        rows = (before_ref[...] + summed).astype(jnp.bfloat16).astype(jnp.float32)
        hidden_ref[...] = rows
        return rows

    attention_step(
        1, group_ref, lengths_ref, long_lengths_ref, hidden, *tables, stored,
        state_ref, side_ref, fresh_ref, lambda *which: None,
    )


def leaving_kernel(cache_ref, out_ref, unused_ref, semaphores):
    unused_ref[...] = jnp.zeros_like(unused_ref)
    copies = [
        pltpu.make_async_copy(cache_ref.at[i, j, 2], out_ref.at[i, j], semaphores.at[2 * i + j])
        for i in range(2)
        for j in range(2)
    ]
    for copy in copies:
        copy.start()
    for copy in copies:
        copy.wait()


def arrival_kernel(
    length_ref, stay_ref, arrived_ref, moving_ref, out_ref, moved_ref, rows, blocks, semaphores
):
    places = [(i, j) for i in range(2) for j in range(2)]
    bodies = [
        pltpu.make_async_copy(moving_ref.at[i, j], moved_ref.at[i, j], semaphores.at[2 * i + j])
        for i, j in places
    ]
    for copy in bodies:
        copy.start()
    rows[0:2, :] = stay_ref[...]
    rows[2:3, :] = arrived_ref[0:1, 0:2048]
    out = pltpu.make_async_copy(rows, out_ref, semaphores.at[8])
    out.start()
    start = pl.multiple_of(length_ref[0] // 16 * 16, 16)
    hit = row_of(16) == length_ref[0] - start
    for n, (i, j) in enumerate(places):
        fresh = arrived_ref[0:1, 2048 + 128 * n : 2176 + 128 * n]
        block = moving_ref[i, j, pl.ds(start, 16), :].astype(jnp.float32)
        blocks[i, j] = jnp.where(hit, fresh, block).astype(jnp.bfloat16)
    writes = [
        pltpu.make_async_copy(
            blocks.at[i, j], moved_ref.at[i, j, pl.ds(start, 16)], semaphores.at[4 + 2 * i + j]
        )
        for i, j in places
    ]
    for body, write in zip(bodies, writes):
        body.wait()
        write.start()
    for write in writes:
        write.wait()
    out.wait()


def fetch_kernel(*refs):
    held, outputs, semaphores = refs[:5], refs[5:12], refs[12]
    copies = [
        pltpu.make_async_copy(source, target, semaphores.at[i])
        for i, (source, target) in enumerate(zip(parts_of(1, *held), outputs))
    ]
    for copy in copies:
        copy.start()
    for copy in copies:
        copy.wait()


def out_kernel(layer, state_ref, far_ref, side_ref, w_ref, out_ref, w, semaphore):
    copy = pltpu.make_async_copy(w_ref.at[layer], w, semaphore)
    copy.start()
    is_main = lax.rem(row_of(16), 8) < 3
    here, far = state_ref[...], far_ref[...]
    m_here, l_here, acc_here = here[:, 128:129], here[:, 192:193], here[:, :128]
    m_far, l_far, acc_far = far[:, 128:129], far[:, 192:193], far[:, :128]
    own, value = side_ref[:, 0:1], side_ref[:, 128:256]
    highest = jnp.maximum(jnp.maximum(m_here, m_far), own)
    f_here, f_far = jnp.exp(m_here - highest), jnp.exp(m_far - highest)
    own_weight = jnp.exp(own - highest)
    total = (l_here * f_here + l_far * f_far) + own_weight
    own_rounded = own_weight.astype(jnp.bfloat16).astype(jnp.float32)
    summed = (acc_here * f_here + acc_far * f_far) + own_rounded * value
    total = jnp.where(is_main, l_here, total)
    summed = jnp.where(is_main, acc_here, summed)
    attended = summed / total
    attended = jnp.concatenate([attended[:8], attended[8:]], axis=1).astype(jnp.bfloat16)
    copy.wait()
    out_ref[...] = jnp.dot(attended, w[...], preferred_element_type=jnp.float32)


def final_kernel(
    group_ref, before_ref, p_ref, r1_ref, r2_ref, r3_ref, fresh0_ref, fresh1_ref,
    stay_ref, long_ref, leave_ref, scratch,
):
    scratch[...] = before_ref[...] + total_of(p_ref, r1_ref, r2_ref, r3_ref)
    stay_ref[...] = scratch[0:2, :]
    odd = lax.rem(group_ref[0], 2) == 1
    long_ref[...] = jnp.where(odd, scratch[4:5, :], scratch[3:4, :])
    leave_ref[0:1, 0:2048] = scratch[2:3, :]
    for i, ref in enumerate((fresh0_ref, fresh1_ref)):
        for j in range(2):
            leave_ref[0:1, 2048 + 128 * (2 * i + j) : 2176 + 128 * (2 * i + j)] = ref[j : j + 1, :]


def local(
    tokens, long_tokens, cache, long_cache, lengths, long_lengths, norm_gain, q_gain, k_gain,
    w_query, key_weight, value_weight, w_out,
):
    groups = lax.axis_size("replica")
    group = lax.axis_index("replica")
    parity = group % 2
    group_1 = group[None]
    cache = cache.reshape(2, 2, 3, 2048, 128)
    long_cache = long_cache.reshape(2, 2, 1, 2, 2048, 128)

    far_token = permute(long_tokens, "replica", lambda i: i ^ 1)
    params = pltpu.CompilerParams(vmem_limit_bytes=16 * 2**20)
    small = pltpu.CompilerParams(vmem_limit_bytes=2 * 2**20)
    held = in_hbm(cache)
    leaving, _ = pl.pallas_call(
        leaving_kernel,
        out_shape=(
            pltpu.VMEM((2, 2, 2048, 128), jnp.bfloat16),
            pltpu.VMEM((8, 128), jnp.float32),
        ),
        in_specs=[ANY],
        out_specs=(ANY, VM),
        scratch_shapes=[pltpu.SemaphoreType.DMA((4,))],
        compiler_params=small,
        name="leaving_cache",
    )(held)
    moving = permute(leaving, "replica", lambda i: (i + groups // 2) % groups)

    places = jnp.concatenate(
        [
            lax.dynamic_slice_in_dim(lengths, group * 3, 3),
            lax.dynamic_slice_in_dim(long_lengths, group - parity, 2),
            jnp.zeros((3,), jnp.int32),
        ]
    ).astype(jnp.float32)
    inverse = np.float64(ROPE_BASE) ** (-2.0 * np.arange(64) / 128)
    inverse = jnp.asarray(np.concatenate([inverse, inverse]).astype(np.float32))
    sign = jnp.asarray(np.where(np.arange(128) < 64, -1.0, 1.0).astype(np.float32))
    angles = places[:, None] * inverse[None, :]
    cosine, sine = jnp.cos(angles), jnp.sin(angles) * sign

    out_shape = (
        jax.ShapeDtypeStruct((16, 256), jnp.float32),
        jax.ShapeDtypeStruct((16, 256), jnp.float32),
        jax.ShapeDtypeStruct((2, 128), jnp.float32),
        jax.ShapeDtypeStruct((ROWS, 2048), jnp.float32),
    )
    scratch = [
        pltpu.VMEM((2048, 256), jnp.bfloat16),
        pltpu.VMEM((2048, 128), jnp.bfloat16),
        pltpu.VMEM((2048, 128), jnp.bfloat16),
        pltpu.VMEM((3, 2048, 128), jnp.bfloat16),
        pltpu.VMEM((2, 2048, 128), jnp.bfloat16),
        pltpu.VMEM((3, 2048, 128), jnp.bfloat16),
        pltpu.VMEM((2, 2048, 128), jnp.bfloat16),
        pltpu.SemaphoreType.DMA((7,)),
    ]
    stored = (cache, long_cache, w_query, key_weight, value_weight)
    tables = (norm_gain, q_gain, k_gain, cosine, sine)

    def project_out(layer, state, side):
        far = permute(state, "replica", lambda i: i ^ 1)
        part = pl.pallas_call(
            functools.partial(out_kernel, layer),
            out_shape=jax.ShapeDtypeStruct((ROWS, 2048), jnp.float32),
            in_specs=[VM, VM, VM, ANY],
            out_specs=VM,
            scratch_shapes=[pltpu.VMEM((256, 2048), jnp.bfloat16), pltpu.SemaphoreType.DMA(())],
            compiler_params=params,
            name=f"out_projection_{layer}",
        )(state, far, side, w_out)
        part = (part + permute(part, "tensor", lambda i: i ^ 1)).astype(jnp.bfloat16)
        received = [permute(part, "tensor", lambda i, k=k: i ^ k) for k in (2, 4, 6)]
        return (part, *received)

    state, side, fresh_0, hidden = pl.pallas_call(
        first_kernel,
        out_shape=out_shape,
        in_specs=[SM] * 3 + [VM] * 8 + [ANY] * 5,
        out_specs=(VM,) * 4,
        scratch_shapes=scratch,
        compiler_params=params,
        name="attention_0",
    )(group_1, lengths, long_lengths, tokens, long_tokens, far_token, *tables, *map(in_hbm, stored))
    terms = project_out(0, state, side)
    buffers = ((2048, 256), (2048, 128), (2048, 128)) + ((3, 2048, 128), (2, 2048, 128)) * 2
    gate, *stored = lax.optimization_barrier((terms[0], *stored))
    terms = (gate, *terms[1:])
    stored = pl.pallas_call(
        fetch_kernel,
        out_shape=tuple(pltpu.VMEM(shape, jnp.bfloat16) for shape in buffers),
        in_specs=[ANY] * 5,
        out_specs=(ANY,) * 7,
        scratch_shapes=[pltpu.SemaphoreType.DMA((7,))],
        compiler_params=small,
        name="fetch_1",
    )(*map(in_hbm, stored))
    state, side, fresh_1, hidden = pl.pallas_call(
        second_kernel,
        out_shape=out_shape,
        in_specs=[SM] * 3 + [VM] * 17,
        out_specs=(VM,) * 4,
        compiler_params=params,
        name="attention_1",
    )(group_1, lengths, long_lengths, hidden, *terms, *tables, *stored)
    terms = project_out(1, state, side)
    stay, long_out, leave = pl.pallas_call(
        final_kernel,
        out_shape=(
            jax.ShapeDtypeStruct((2, 2048), jnp.float32),
            jax.ShapeDtypeStruct((1, 2048), jnp.float32),
            jax.ShapeDtypeStruct((1, 2560), jnp.float32),
        ),
        in_specs=[SM] + [VM] * 7,
        out_specs=(VM,) * 3,
        scratch_shapes=[pltpu.VMEM((ROWS, 2048), jnp.float32)],
        compiler_params=params,
        name="final_rows",
    )(group_1, hidden, *terms, fresh_0, fresh_1)
    arrived = permute(leave, "replica", lambda i: (i + groups // 2) % groups)
    partner = (group + groups // 2) % groups
    arrived_len = lax.dynamic_slice_in_dim(lengths, partner * 3 + 2, 1)
    out_hidden, moved = pl.pallas_call(
        arrival_kernel,
        out_shape=(
            pltpu.HBM((3, 2048), jnp.float32),
            pltpu.HBM((2, 2, 2048, 128), jnp.bfloat16),
        ),
        in_specs=[SM, VM, VM, VM],
        out_specs=(ANY, ANY),
        scratch_shapes=[
            pltpu.VMEM((3, 2048), jnp.float32),
            pltpu.VMEM((2, 2, 16, 128), jnp.bfloat16),
            pltpu.SemaphoreType.DMA((9,)),
        ],
        compiler_params=small,
        name="arrival",
    )(arrived_len, stay, arrived, in_vmem(moving))
    return (out_hidden, long_out, moved[None, :, :, :, None, :])


def solution(mesh):
    return jax.shard_map(
        local,
        mesh=mesh,
        in_specs=(
            P("replica", None),
            P("replica", None),
            P(None, None, "replica", None, "tensor", None),
            P(None, None, "replica", None, None, "tensor", None),
            P(),
            P(),
            P(),
            P(),
            P(),
            P(None, None, "tensor"),
            P(None, None, "tensor"),
            P(None, None, "tensor"),
            P(None, "tensor", None),
        ),
        out_specs=(
            P("replica", None),
            P("replica", None),
            P("replica", None, None, None, "tensor", None),
        ),
        check_vma=False,
    )
```

```python
import functools

import jax
import jax.numpy as jnp
import numpy as np
from jax import lax
from jax.experimental import pallas as pl
from jax.experimental.pallas import tpu as pltpu
from jax.sharding import PartitionSpec as P

EPSILON = 1e-06
ROPE_BASE = 1000000.0
NEGATIVE = -1e30
ROWS = 8
ANY = pl.BlockSpec(memory_space=pl.ANY)
VM = pl.BlockSpec(memory_space=pltpu.VMEM)
SM = pl.BlockSpec(memory_space=pltpu.SMEM)


def permute(value, axis, target):
    pairs = [(source, target(source)) for source in range(lax.axis_size(axis))]
    return lax.ppermute(value, axis, pairs)


def in_hbm(value):
    return pltpu.with_memory_space_constraint(value, pltpu.HBM)


def in_vmem(value):
    return pltpu.with_memory_space_constraint(value, pltpu.VMEM)


def row_of(count):
    return lax.broadcasted_iota(jnp.int32, (count, 1), 0)


def attention_step(
    layer, group_ref, lengths_ref, long_lengths_ref, hidden, gain_ref, q_gain_ref, k_gain_ref,
    cosine_ref, sine_ref, stored, state_ref, side_ref, fresh_ref, ready,
):
    wq, wk, wv, keys, long_keys, values, long_values = stored
    rows = hidden()
    scale = lax.rsqrt(jnp.mean(rows * rows, axis=-1, keepdims=True) + EPSILON)
    normed = (rows * scale * gain_ref[layer : layer + 1, :]).astype(jnp.bfloat16)
    ready(0, 1, 2)
    queries = jnp.dot(normed, wq[...], preferred_element_type=jnp.float32)
    new_keys = jnp.dot(normed, wk[...], preferred_element_type=jnp.float32)
    new_values = jnp.dot(normed, wv[...], preferred_element_type=jnp.float32).astype(jnp.bfloat16)

    def finish(heads, gain, cosine, sine):
        heads = heads * lax.rsqrt(jnp.mean(heads * heads, axis=-1, keepdims=True) + EPSILON) * gain
        return (heads * cosine + pltpu.roll(heads, 64, 1) * sine).astype(jnp.bfloat16)

    cosine, sine = cosine_ref[...], sine_ref[...]
    q_gain = q_gain_ref[layer : layer + 1, :]
    q0 = finish(queries[:, :128], q_gain, cosine, sine).astype(jnp.float32)
    q1 = finish(queries[:, 128:], q_gain, cosine, sine).astype(jnp.float32)
    key_new = finish(new_keys, k_gain_ref[layer : layer + 1, :], cosine, sine).astype(jnp.float32)
    value_new = new_values.astype(jnp.float32)
    fresh_ref[0:1, :] = key_new[2:3, :]
    fresh_ref[1:2, :] = value_new[2:3, :]
    both = jnp.concatenate([q0, q1], axis=0)
    query = both.astype(jnp.bfloat16)
    keys_twice = jnp.concatenate([key_new, key_new], axis=0)
    values_twice = jnp.concatenate([value_new, value_new], axis=0)
    factor = 128 ** (-0.5)
    own = jnp.sum(both * keys_twice, axis=-1, keepdims=True) * factor

    group = group_ref[0]
    parity = lax.rem(group, 2)
    which = lax.rem(row_of(16), 8)
    limit = jnp.ones((16, 1), jnp.int32)
    for r in range(3):
        limit = jnp.where(which == r, lengths_ref[group * 3 + r], limit)
    for r in range(2):
        limit = jnp.where(
            which == 3 + r, long_lengths_ref[group - parity + r] - parity * 2048, limit
        )
    scores = jnp.zeros((16, 2048), jnp.float32)
    for r in range(5):
        if r == 0:
            ready(3)
        if r == 3:
            ready(4)
        block = keys[r] if r < 3 else long_keys[r - 3]
        product = lax.dot_general(
            query, block, (((1,), (1,)), ((), ())), preferred_element_type=jnp.float32
        )
        scores = jnp.where(which == r, product, scores)
    places = lax.broadcasted_iota(jnp.int32, (16, 2048), 1)
    scores = jnp.where(places < limit, scores * factor, NEGATIVE)
    is_main = which < 3
    highest = jnp.max(scores, axis=-1, keepdims=True)
    highest = jnp.where(is_main, jnp.maximum(highest, own), highest)
    weights = jnp.exp(scores - highest)
    own_weight = jnp.where(is_main, jnp.exp(own - highest), 0.0)
    total = jnp.sum(weights, axis=-1, keepdims=True) + own_weight
    rounded = weights.astype(jnp.bfloat16)
    summed = own_weight.astype(jnp.bfloat16).astype(jnp.float32) * values_twice
    for r in range(5):
        if r == 0:
            ready(5)
        if r == 3:
            ready(6)
        block = values[r] if r < 3 else long_values[r - 3]
        product = jnp.dot(rounded, block, preferred_element_type=jnp.float32)
        summed = summed + jnp.where(which == r, product, 0.0)
    state_ref[:, 0:128] = summed
    lanes = lax.broadcasted_iota(jnp.int32, (16, 128), 1)
    state_ref[:, 128:256] = jnp.where(lanes < 64, highest, total)
    side_ref[:, 0:128] = jnp.broadcast_to(own, (16, 128))
    side_ref[:, 128:256] = values_twice


def parts_of(layer, cache_ref, long_ref, wq_ref, wk_ref, wv_ref):
    return (
        wq_ref.at[layer], wk_ref.at[layer], wv_ref.at[layer],
        cache_ref.at[layer, 0], long_ref.at[layer, 0, 0],
        cache_ref.at[layer, 1], long_ref.at[layer, 1, 0],
    )


def first_kernel(
    group_ref, lengths_ref, long_lengths_ref, tokens_ref, own_long_ref, far_long_ref, *rest
):
    tables, held = rest[:5], rest[5:10]
    state_ref, side_ref, fresh_ref, hidden_ref = rest[10:14]
    buffers, semaphores = rest[14:21], rest[21]
    copies = [
        pltpu.make_async_copy(source, target, semaphores.at[i])
        for i, (source, target) in enumerate(zip(parts_of(0, *held), buffers))
    ]
    for copy in copies:
        copy.start()

    def ready(*which):
        for i in which:
            copies[i].wait()

    def hidden():
        own = own_long_ref[...].astype(jnp.float32)
        far = far_long_ref[...].astype(jnp.float32)
        even = lax.rem(group_ref[0], 2) == 0
        hidden_ref[...] = jnp.zeros((ROWS, 2048), jnp.float32)
        hidden_ref[0:3, :] = tokens_ref[...].astype(jnp.float32)
        hidden_ref[3:4, :] = jnp.where(even, own, far)
        hidden_ref[4:5, :] = jnp.where(even, far, own)
        return hidden_ref[...]

    attention_step(
        0, group_ref, lengths_ref, long_lengths_ref, hidden, *tables, buffers,
        state_ref, side_ref, fresh_ref, ready,
    )


def total_of(p_ref, r1_ref, r2_ref, r3_ref):
    p, r1, r2, r3 = (ref[...].astype(jnp.float32) for ref in (p_ref, r1_ref, r2_ref, r3_ref))
    return (p + r1) + (r2 + r3)


def second_kernel(
    group_ref, lengths_ref, long_lengths_ref, before_ref, p_ref, r1_ref, r2_ref, r3_ref, *rest
):
    tables, stored = rest[:5], rest[5:12]
    state_ref, side_ref, fresh_ref, hidden_ref = rest[12:16]

    def hidden():
        summed = total_of(p_ref, r1_ref, r2_ref, r3_ref)
        rows = (before_ref[...] + summed).astype(jnp.bfloat16).astype(jnp.float32)
        hidden_ref[...] = rows
        return rows

    attention_step(
        1, group_ref, lengths_ref, long_lengths_ref, hidden, *tables, stored,
        state_ref, side_ref, fresh_ref, lambda *which: None,
    )


def leaving_kernel(cache_ref, out_ref, blocks, semaphores):
    places = [(i, j) for i in range(2) for j in range(2)]
    reads = [
        pltpu.make_async_copy(cache_ref.at[i, j, 2], blocks.at[i, j], semaphores.at[0, i, j])
        for i, j in places
    ]
    writes = [
        pltpu.make_async_copy(blocks.at[i, j], out_ref.at[i, j], semaphores.at[1, i, j])
        for i, j in places
    ]
    for copy in reads:
        copy.start()
    for read, write in zip(reads, writes):
        read.wait()
        write.start()
    for copy in writes:
        copy.wait()


def arrival_kernel(
    length_ref, stay_ref, arrived_ref, moving_ref, out_ref, moved_ref, rows, blocks, semaphores
):
    places = [(i, j) for i in range(2) for j in range(2)]
    bodies = [
        pltpu.make_async_copy(moving_ref.at[i, j], moved_ref.at[i, j], semaphores.at[2 * i + j])
        for i, j in places
    ]
    for copy in bodies:
        copy.start()
    rows[0:2, :] = stay_ref[...]
    rows[2:3, :] = arrived_ref[0:1, 0:2048]
    out = pltpu.make_async_copy(rows, out_ref, semaphores.at[8])
    out.start()
    start = pl.multiple_of(length_ref[0] // 16 * 16, 16)
    hit = row_of(16) == length_ref[0] - start
    for n, (i, j) in enumerate(places):
        fresh = arrived_ref[0:1, 2048 + 128 * n : 2176 + 128 * n]
        block = moving_ref[i, j, pl.ds(start, 16), :].astype(jnp.float32)
        blocks[i, j] = jnp.where(hit, fresh, block).astype(jnp.bfloat16)
    writes = [
        pltpu.make_async_copy(
            blocks.at[i, j], moved_ref.at[i, j, pl.ds(start, 16)], semaphores.at[4 + 2 * i + j]
        )
        for i, j in places
    ]
    for body, write in zip(bodies, writes):
        body.wait()
        write.start()
    for write in writes:
        write.wait()
    out.wait()


def fetch_kernel(*refs):
    held, outputs, semaphores = refs[:5], refs[5:12], refs[12]
    copies = [
        pltpu.make_async_copy(source, target, semaphores.at[i])
        for i, (source, target) in enumerate(zip(parts_of(1, *held), outputs))
    ]
    for copy in copies:
        copy.start()
    for copy in copies:
        copy.wait()


def out_kernel(layer, state_ref, far_ref, side_ref, w_ref, out_ref, w, semaphore):
    copy = pltpu.make_async_copy(w_ref.at[layer], w, semaphore)
    copy.start()
    is_main = lax.rem(row_of(16), 8) < 3
    here, far = state_ref[...], far_ref[...]
    m_here, l_here, acc_here = here[:, 128:129], here[:, 192:193], here[:, :128]
    m_far, l_far, acc_far = far[:, 128:129], far[:, 192:193], far[:, :128]
    own, value = side_ref[:, 0:1], side_ref[:, 128:256]
    highest = jnp.maximum(jnp.maximum(m_here, m_far), own)
    f_here, f_far = jnp.exp(m_here - highest), jnp.exp(m_far - highest)
    own_weight = jnp.exp(own - highest)
    total = (l_here * f_here + l_far * f_far) + own_weight
    own_rounded = own_weight.astype(jnp.bfloat16).astype(jnp.float32)
    summed = (acc_here * f_here + acc_far * f_far) + own_rounded * value
    total = jnp.where(is_main, l_here, total)
    summed = jnp.where(is_main, acc_here, summed)
    attended = summed / total
    attended = jnp.concatenate([attended[:8], attended[8:]], axis=1).astype(jnp.bfloat16)
    copy.wait()
    out_ref[...] = jnp.dot(attended, w[...], preferred_element_type=jnp.float32)


def final_kernel(
    group_ref, before_ref, p_ref, r1_ref, r2_ref, r3_ref, fresh0_ref, fresh1_ref,
    stay_ref, long_ref, leave_ref, scratch,
):
    scratch[...] = before_ref[...] + total_of(p_ref, r1_ref, r2_ref, r3_ref)
    stay_ref[...] = scratch[0:2, :]
    odd = lax.rem(group_ref[0], 2) == 1
    long_ref[...] = jnp.where(odd, scratch[4:5, :], scratch[3:4, :])
    leave_ref[0:1, 0:2048] = scratch[2:3, :]
    for i, ref in enumerate((fresh0_ref, fresh1_ref)):
        for j in range(2):
            leave_ref[0:1, 2048 + 128 * (2 * i + j) : 2176 + 128 * (2 * i + j)] = ref[j : j + 1, :]


def local(
    tokens, long_tokens, cache, long_cache, lengths, long_lengths, norm_gain, q_gain, k_gain,
    w_query, key_weight, value_weight, w_out,
):
    groups = lax.axis_size("replica")
    group = lax.axis_index("replica")
    parity = group % 2
    group_1 = group[None]
    cache = cache.reshape(2, 2, 3, 2048, 128)
    long_cache = long_cache.reshape(2, 2, 1, 2, 2048, 128)

    far_token = permute(long_tokens, "replica", lambda i: i ^ 1)
    params = pltpu.CompilerParams(vmem_limit_bytes=16 * 2**20)
    small = pltpu.CompilerParams(vmem_limit_bytes=2 * 2**20)
    held = in_hbm(cache)
    leaving = pl.pallas_call(
        leaving_kernel,
        out_shape=pltpu.HBM((2, 2, 2048, 128), jnp.bfloat16),
        in_specs=[ANY],
        out_specs=ANY,
        scratch_shapes=[
            pltpu.VMEM((2, 2, 2048, 128), jnp.bfloat16),
            pltpu.SemaphoreType.DMA((2, 2, 2)),
        ],
        compiler_params=pltpu.CompilerParams(vmem_limit_bytes=4 * 2**20),
        name="leaving_cache",
    )(held)
    moving = permute(leaving, "replica", lambda i: (i + groups // 2) % groups)

    places = jnp.concatenate(
        [
            lax.dynamic_slice_in_dim(lengths, group * 3, 3),
            lax.dynamic_slice_in_dim(long_lengths, group - parity, 2),
            jnp.zeros((3,), jnp.int32),
        ]
    ).astype(jnp.float32)
    inverse = np.float64(ROPE_BASE) ** (-2.0 * np.arange(64) / 128)
    inverse = jnp.asarray(np.concatenate([inverse, inverse]).astype(np.float32))
    sign = jnp.asarray(np.where(np.arange(128) < 64, -1.0, 1.0).astype(np.float32))
    angles = places[:, None] * inverse[None, :]
    cosine, sine = jnp.cos(angles), jnp.sin(angles) * sign

    out_shape = (
        jax.ShapeDtypeStruct((16, 256), jnp.float32),
        jax.ShapeDtypeStruct((16, 256), jnp.float32),
        jax.ShapeDtypeStruct((2, 128), jnp.float32),
        jax.ShapeDtypeStruct((ROWS, 2048), jnp.float32),
    )
    scratch = [
        pltpu.VMEM((2048, 256), jnp.bfloat16),
        pltpu.VMEM((2048, 128), jnp.bfloat16),
        pltpu.VMEM((2048, 128), jnp.bfloat16),
        pltpu.VMEM((3, 2048, 128), jnp.bfloat16),
        pltpu.VMEM((2, 2048, 128), jnp.bfloat16),
        pltpu.VMEM((3, 2048, 128), jnp.bfloat16),
        pltpu.VMEM((2, 2048, 128), jnp.bfloat16),
        pltpu.SemaphoreType.DMA((7,)),
    ]
    stored = (cache, long_cache, w_query, key_weight, value_weight)
    tables = (norm_gain, q_gain, k_gain, cosine, sine)

    def project_out(layer, state, side):
        far = permute(state, "replica", lambda i: i ^ 1)
        part = pl.pallas_call(
            functools.partial(out_kernel, layer),
            out_shape=jax.ShapeDtypeStruct((ROWS, 2048), jnp.float32),
            in_specs=[VM, VM, VM, ANY],
            out_specs=VM,
            scratch_shapes=[pltpu.VMEM((256, 2048), jnp.bfloat16), pltpu.SemaphoreType.DMA(())],
            compiler_params=params,
            name=f"out_projection_{layer}",
        )(state, far, side, w_out)
        part = (part + permute(part, "tensor", lambda i: i ^ 1)).astype(jnp.bfloat16)
        received = [permute(part, "tensor", lambda i, k=k: i ^ k) for k in (2, 4, 6)]
        return (part, *received)

    state, side, fresh_0, hidden = pl.pallas_call(
        first_kernel,
        out_shape=out_shape,
        in_specs=[SM] * 3 + [VM] * 8 + [ANY] * 5,
        out_specs=(VM,) * 4,
        scratch_shapes=scratch,
        compiler_params=params,
        name="attention_0",
    )(group_1, lengths, long_lengths, tokens, long_tokens, far_token, *tables, *map(in_hbm, stored))
    terms = project_out(0, state, side)
    buffers = ((2048, 256), (2048, 128), (2048, 128)) + ((3, 2048, 128), (2, 2048, 128)) * 2
    gate, *stored = lax.optimization_barrier((terms[0], *stored))
    terms = (gate, *terms[1:])
    stored = pl.pallas_call(
        fetch_kernel,
        out_shape=tuple(pltpu.VMEM(shape, jnp.bfloat16) for shape in buffers),
        in_specs=[ANY] * 5,
        out_specs=(ANY,) * 7,
        scratch_shapes=[pltpu.SemaphoreType.DMA((7,))],
        compiler_params=small,
        name="fetch_1",
    )(*map(in_hbm, stored))
    state, side, fresh_1, hidden = pl.pallas_call(
        second_kernel,
        out_shape=out_shape,
        in_specs=[SM] * 3 + [VM] * 17,
        out_specs=(VM,) * 4,
        compiler_params=params,
        name="attention_1",
    )(group_1, lengths, long_lengths, hidden, *terms, *tables, *stored)
    terms = project_out(1, state, side)
    stay, long_out, leave = pl.pallas_call(
        final_kernel,
        out_shape=(
            jax.ShapeDtypeStruct((2, 2048), jnp.float32),
            jax.ShapeDtypeStruct((1, 2048), jnp.float32),
            jax.ShapeDtypeStruct((1, 2560), jnp.float32),
        ),
        in_specs=[SM] + [VM] * 7,
        out_specs=(VM,) * 3,
        scratch_shapes=[pltpu.VMEM((ROWS, 2048), jnp.float32)],
        compiler_params=params,
        name="final_rows",
    )(group_1, hidden, *terms, fresh_0, fresh_1)
    arrived = permute(leave, "replica", lambda i: (i + groups // 2) % groups)
    partner = (group + groups // 2) % groups
    arrived_len = lax.dynamic_slice_in_dim(lengths, partner * 3 + 2, 1)
    out_hidden, moved = pl.pallas_call(
        arrival_kernel,
        out_shape=(
            pltpu.HBM((3, 2048), jnp.float32),
            pltpu.HBM((2, 2, 2048, 128), jnp.bfloat16),
        ),
        in_specs=[SM, VM, VM, VM],
        out_specs=(ANY, ANY),
        scratch_shapes=[
            pltpu.VMEM((3, 2048), jnp.float32),
            pltpu.VMEM((2, 2, 16, 128), jnp.bfloat16),
            pltpu.SemaphoreType.DMA((9,)),
        ],
        compiler_params=small,
        name="arrival",
    )(arrived_len, stay, arrived, in_vmem(moving))
    return (out_hidden, long_out, moved[None, :, :, :, None, :])


def solution(mesh):
    return jax.shard_map(
        local,
        mesh=mesh,
        in_specs=(
            P("replica", None),
            P("replica", None),
            P(None, None, "replica", None, "tensor", None),
            P(None, None, "replica", None, None, "tensor", None),
            P(),
            P(),
            P(),
            P(),
            P(),
            P(None, None, "tensor"),
            P(None, None, "tensor"),
            P(None, None, "tensor"),
            P(None, "tensor", None),
        ),
        out_specs=(
            P("replica", None),
            P("replica", None),
            P("replica", None, None, None, "tensor", None),
        ),
        check_vma=False,
    )
```

```python
import functools

import jax
import jax.numpy as jnp
import numpy as np
from jax import lax
from jax.experimental import pallas as pl
from jax.experimental.pallas import tpu as pltpu
from jax.sharding import PartitionSpec as P

EPSILON = 1e-06
ROPE_BASE = 1000000.0
NEGATIVE = -1e30
ROWS = 8
ANY = pl.BlockSpec(memory_space=pl.ANY)
VM = pl.BlockSpec(memory_space=pltpu.VMEM)
SM = pl.BlockSpec(memory_space=pltpu.SMEM)


def permute(value, axis, target):
    pairs = [(source, target(source)) for source in range(lax.axis_size(axis))]
    return lax.ppermute(value, axis, pairs)


def in_hbm(value):
    return pltpu.with_memory_space_constraint(value, pltpu.HBM)


def in_vmem(value):
    return pltpu.with_memory_space_constraint(value, pltpu.VMEM)


def row_of(count):
    return lax.broadcasted_iota(jnp.int32, (count, 1), 0)


def attention_step(
    layer, group_ref, lengths_ref, long_lengths_ref, hidden, gain_ref, q_gain_ref, k_gain_ref,
    cosine_ref, sine_ref, stored, state_ref, side_ref, fresh_ref, ready,
):
    wq, wk, wv, keys, long_keys, values, long_values = stored
    rows = hidden()
    scale = lax.rsqrt(jnp.mean(rows * rows, axis=-1, keepdims=True) + EPSILON)
    normed = (rows * scale * gain_ref[layer : layer + 1, :]).astype(jnp.bfloat16)
    ready(0, 1, 2)
    queries = jnp.dot(normed, wq[...], preferred_element_type=jnp.float32)
    new_keys = jnp.dot(normed, wk[...], preferred_element_type=jnp.float32)
    new_values = jnp.dot(normed, wv[...], preferred_element_type=jnp.float32).astype(jnp.bfloat16)

    def finish(heads, gain, cosine, sine):
        heads = heads * lax.rsqrt(jnp.mean(heads * heads, axis=-1, keepdims=True) + EPSILON) * gain
        return (heads * cosine + pltpu.roll(heads, 64, 1) * sine).astype(jnp.bfloat16)

    cosine, sine = cosine_ref[...], sine_ref[...]
    q_gain = q_gain_ref[layer : layer + 1, :]
    q0 = finish(queries[:, :128], q_gain, cosine, sine).astype(jnp.float32)
    q1 = finish(queries[:, 128:], q_gain, cosine, sine).astype(jnp.float32)
    key_new = finish(new_keys, k_gain_ref[layer : layer + 1, :], cosine, sine).astype(jnp.float32)
    value_new = new_values.astype(jnp.float32)
    fresh_ref[0:1, :] = key_new[2:3, :]
    fresh_ref[1:2, :] = value_new[2:3, :]
    both = jnp.concatenate([q0, q1], axis=0)
    query = both.astype(jnp.bfloat16)
    keys_twice = jnp.concatenate([key_new, key_new], axis=0)
    values_twice = jnp.concatenate([value_new, value_new], axis=0)
    factor = 128 ** (-0.5)
    own = jnp.sum(both * keys_twice, axis=-1, keepdims=True) * factor

    group = group_ref[0]
    parity = lax.rem(group, 2)
    which = lax.rem(row_of(16), 8)
    limit = jnp.ones((16, 1), jnp.int32)
    for r in range(3):
        limit = jnp.where(which == r, lengths_ref[group * 3 + r], limit)
    for r in range(2):
        limit = jnp.where(
            which == 3 + r, long_lengths_ref[group - parity + r] - parity * 2048, limit
        )
    scores = jnp.zeros((16, 2048), jnp.float32)
    for r in range(5):
        if r == 0:
            ready(3)
        if r == 3:
            ready(4)
        block = keys[r] if r < 3 else long_keys[r - 3]
        product = lax.dot_general(
            query, block, (((1,), (1,)), ((), ())), preferred_element_type=jnp.float32
        )
        scores = jnp.where(which == r, product, scores)
    places = lax.broadcasted_iota(jnp.int32, (16, 2048), 1)
    scores = jnp.where(places < limit, scores * factor, NEGATIVE)
    is_main = which < 3
    highest = jnp.max(scores, axis=-1, keepdims=True)
    highest = jnp.where(is_main, jnp.maximum(highest, own), highest)
    weights = jnp.exp(scores - highest)
    own_weight = jnp.where(is_main, jnp.exp(own - highest), 0.0)
    total = jnp.sum(weights, axis=-1, keepdims=True) + own_weight
    rounded = weights.astype(jnp.bfloat16)
    summed = own_weight.astype(jnp.bfloat16).astype(jnp.float32) * values_twice
    for r in range(5):
        if r == 0:
            ready(5)
        if r == 3:
            ready(6)
        block = values[r] if r < 3 else long_values[r - 3]
        product = jnp.dot(rounded, block, preferred_element_type=jnp.float32)
        summed = summed + jnp.where(which == r, product, 0.0)
    state_ref[:, 0:128] = summed
    lanes = lax.broadcasted_iota(jnp.int32, (16, 128), 1)
    state_ref[:, 128:256] = jnp.where(lanes < 64, highest, total)
    side_ref[:, 0:128] = jnp.broadcast_to(own, (16, 128))
    side_ref[:, 128:256] = values_twice


def parts_of(layer, cache_ref, long_ref, wq_ref, wk_ref, wv_ref):
    return (
        wq_ref.at[layer], wk_ref.at[layer], wv_ref.at[layer],
        cache_ref.at[layer, 0], long_ref.at[layer, 0, 0],
        cache_ref.at[layer, 1], long_ref.at[layer, 1, 0],
    )


def first_kernel(
    group_ref, lengths_ref, long_lengths_ref, tokens_ref, own_long_ref, far_long_ref, *rest
):
    tables, held = rest[:5], rest[5:10]
    state_ref, side_ref, fresh_ref, hidden_ref = rest[10:14]
    buffers, semaphores = rest[14:21], rest[21]
    copies = [
        pltpu.make_async_copy(source, target, semaphores.at[i])
        for i, (source, target) in enumerate(zip(parts_of(0, *held), buffers))
    ]
    for copy in copies:
        copy.start()

    def ready(*which):
        for i in which:
            copies[i].wait()

    def hidden():
        own = own_long_ref[...].astype(jnp.float32)
        far = far_long_ref[...].astype(jnp.float32)
        even = lax.rem(group_ref[0], 2) == 0
        hidden_ref[...] = jnp.zeros((ROWS, 2048), jnp.float32)
        hidden_ref[0:3, :] = tokens_ref[...].astype(jnp.float32)
        hidden_ref[3:4, :] = jnp.where(even, own, far)
        hidden_ref[4:5, :] = jnp.where(even, far, own)
        return hidden_ref[...]

    attention_step(
        0, group_ref, lengths_ref, long_lengths_ref, hidden, *tables, buffers,
        state_ref, side_ref, fresh_ref, ready,
    )


def total_of(p_ref, r1_ref, r2_ref, r3_ref):
    p, r1, r2, r3 = (ref[...].astype(jnp.float32) for ref in (p_ref, r1_ref, r2_ref, r3_ref))
    return (p + r1) + (r2 + r3)


def second_kernel(
    group_ref, lengths_ref, long_lengths_ref, before_ref, p_ref, r1_ref, r2_ref, r3_ref, *rest
):
    tables, stored = rest[:5], rest[5:12]
    state_ref, side_ref, fresh_ref, hidden_ref = rest[12:16]

    def hidden():
        summed = total_of(p_ref, r1_ref, r2_ref, r3_ref)
        rows = (before_ref[...] + summed).astype(jnp.bfloat16).astype(jnp.float32)
        hidden_ref[...] = rows
        return rows

    attention_step(
        1, group_ref, lengths_ref, long_lengths_ref, hidden, *tables, stored,
        state_ref, side_ref, fresh_ref, lambda *which: None,
    )


PLANES = ((0, 0), (0, 1), (1, 0), (1, 1))
FIRST = 3


def leaving_kernel(planes, cache_ref, out_ref, blocks, semaphores):
    pieces = [(n, i, j, pl.ds(at, 512)) for n, (i, j) in enumerate(planes) for at in range(0, 2048, 512)]
    reads = [
        pltpu.make_async_copy(cache_ref.at[i, j, 2, at], blocks.at[n, at], semaphores.at[0, m])
        for m, (n, i, j, at) in enumerate(pieces)
    ]
    writes = [
        pltpu.make_async_copy(blocks.at[n, at], out_ref.at[n, at], semaphores.at[1, m])
        for m, (n, i, j, at) in enumerate(pieces)
    ]
    for copy in reads:
        copy.start()
    for read, write in zip(reads, writes):
        read.wait()
        write.start()
    for copy in writes:
        copy.wait()


def store_kernel(moving_ref, moved_ref, semaphores):
    copies = [
        pltpu.make_async_copy(moving_ref.at[n], moved_ref.at[i, j], semaphores.at[n])
        for n, (i, j) in enumerate(PLANES[:FIRST])
    ]
    for copy in copies:
        copy.start()
    for copy in copies:
        copy.wait()


def arrival_kernel(
    length_ref, stay_ref, arrived_ref, first_ref, second_ref, stored_ref, out_ref, moved_ref,
    rows, blocks, semaphores,
):
    del stored_ref
    bodies = [
        pltpu.make_async_copy(second_ref.at[n], moved_ref.at[i, j], semaphores.at[n])
        for n, (i, j) in enumerate(PLANES[FIRST:])
    ]
    for copy in bodies:
        copy.start()
    start = pl.multiple_of(length_ref[0] // 16 * 16, 16)
    hit = row_of(16) == length_ref[0] - start
    writes = []
    for n, (i, j) in enumerate(PLANES):
        fresh = arrived_ref[0:1, 2048 + 128 * n : 2176 + 128 * n]
        plane = first_ref.at[n] if n < FIRST else second_ref.at[n - FIRST]
        block = plane[pl.ds(start, 16), :].astype(jnp.float32)
        blocks[n] = jnp.where(hit, fresh, block).astype(jnp.bfloat16)
        writes.append(
            pltpu.make_async_copy(
                blocks.at[n], moved_ref.at[i, j, pl.ds(start, 16)], semaphores.at[4 + n]
            )
        )
        if n < FIRST:
            writes[-1].start()
    rows[0:2, :] = stay_ref[...]
    rows[2:3, :] = arrived_ref[0:1, 0:2048]
    out = pltpu.make_async_copy(rows, out_ref, semaphores.at[8])
    out.start()
    for body, write in zip(bodies, writes[FIRST:]):
        body.wait()
        write.start()
    for write in writes:
        write.wait()
    out.wait()


def fetch_kernel(*refs):
    held, outputs, semaphores = refs[:5], refs[5:12], refs[12]
    copies = [
        pltpu.make_async_copy(source, target, semaphores.at[i])
        for i, (source, target) in enumerate(zip(parts_of(1, *held), outputs))
    ]
    for copy in copies:
        copy.start()
    for copy in copies:
        copy.wait()


def out_kernel(layer, state_ref, far_ref, side_ref, w_ref, out_ref, w, semaphore):
    copy = pltpu.make_async_copy(w_ref.at[layer], w, semaphore)
    copy.start()
    is_main = lax.rem(row_of(16), 8) < 3
    here, far = state_ref[...], far_ref[...]
    m_here, l_here, acc_here = here[:, 128:129], here[:, 192:193], here[:, :128]
    m_far, l_far, acc_far = far[:, 128:129], far[:, 192:193], far[:, :128]
    own, value = side_ref[:, 0:1], side_ref[:, 128:256]
    highest = jnp.maximum(jnp.maximum(m_here, m_far), own)
    f_here, f_far = jnp.exp(m_here - highest), jnp.exp(m_far - highest)
    own_weight = jnp.exp(own - highest)
    total = (l_here * f_here + l_far * f_far) + own_weight
    own_rounded = own_weight.astype(jnp.bfloat16).astype(jnp.float32)
    summed = (acc_here * f_here + acc_far * f_far) + own_rounded * value
    total = jnp.where(is_main, l_here, total)
    summed = jnp.where(is_main, acc_here, summed)
    attended = summed / total
    attended = jnp.concatenate([attended[:8], attended[8:]], axis=1).astype(jnp.bfloat16)
    copy.wait()
    out_ref[...] = jnp.dot(attended, w[...], preferred_element_type=jnp.float32)


def final_kernel(
    group_ref, before_ref, p_ref, r1_ref, r2_ref, r3_ref, fresh0_ref, fresh1_ref,
    stay_ref, long_ref, leave_ref, scratch,
):
    scratch[...] = before_ref[...] + total_of(p_ref, r1_ref, r2_ref, r3_ref)
    stay_ref[...] = scratch[0:2, :]
    odd = lax.rem(group_ref[0], 2) == 1
    long_ref[...] = jnp.where(odd, scratch[4:5, :], scratch[3:4, :])
    leave_ref[0:1, 0:2048] = scratch[2:3, :]
    for i, ref in enumerate((fresh0_ref, fresh1_ref)):
        for j in range(2):
            leave_ref[0:1, 2048 + 128 * (2 * i + j) : 2176 + 128 * (2 * i + j)] = ref[j : j + 1, :]


def local(
    tokens, long_tokens, cache, long_cache, lengths, long_lengths, norm_gain, q_gain, k_gain,
    w_query, key_weight, value_weight, w_out,
):
    groups = lax.axis_size("replica")
    group = lax.axis_index("replica")
    parity = group % 2
    group_1 = group[None]
    cache = cache.reshape(2, 2, 3, 2048, 128)
    long_cache = long_cache.reshape(2, 2, 1, 2, 2048, 128)

    far_token = permute(long_tokens, "replica", lambda i: i ^ 1)
    params = pltpu.CompilerParams(vmem_limit_bytes=16 * 2**20)
    small = pltpu.CompilerParams(vmem_limit_bytes=2 * 2**20)
    held = in_hbm(cache)

    def leaving(planes, name):
        count = len(planes)
        return pl.pallas_call(
            functools.partial(leaving_kernel, planes),
            out_shape=pltpu.HBM((count, 2048, 128), jnp.bfloat16),
            in_specs=[ANY],
            out_specs=ANY,
            scratch_shapes=[
                pltpu.VMEM((count, 2048, 128), jnp.bfloat16),
                pltpu.SemaphoreType.DMA((2, 4 * count)),
            ],
            compiler_params=pltpu.CompilerParams(vmem_limit_bytes=4 * 2**20),
            name=name,
        )(held)

    first, second = (
        permute(leaving(planes, name), "replica", lambda i: (i + groups // 2) % groups)
        for planes, name in ((PLANES[:FIRST], "leaving_first"), (PLANES[FIRST:], "leaving_last"))
    )

    places = jnp.concatenate(
        [
            lax.dynamic_slice_in_dim(lengths, group * 3, 3),
            lax.dynamic_slice_in_dim(long_lengths, group - parity, 2),
            jnp.zeros((3,), jnp.int32),
        ]
    ).astype(jnp.float32)
    inverse = np.float64(ROPE_BASE) ** (-2.0 * np.arange(64) / 128)
    inverse = jnp.asarray(np.concatenate([inverse, inverse]).astype(np.float32))
    sign = jnp.asarray(np.where(np.arange(128) < 64, -1.0, 1.0).astype(np.float32))
    angles = places[:, None] * inverse[None, :]
    cosine, sine = jnp.cos(angles), jnp.sin(angles) * sign

    out_shape = (
        jax.ShapeDtypeStruct((16, 256), jnp.float32),
        jax.ShapeDtypeStruct((16, 256), jnp.float32),
        jax.ShapeDtypeStruct((2, 128), jnp.float32),
        jax.ShapeDtypeStruct((ROWS, 2048), jnp.float32),
    )
    scratch = [
        pltpu.VMEM((2048, 256), jnp.bfloat16),
        pltpu.VMEM((2048, 128), jnp.bfloat16),
        pltpu.VMEM((2048, 128), jnp.bfloat16),
        pltpu.VMEM((3, 2048, 128), jnp.bfloat16),
        pltpu.VMEM((2, 2048, 128), jnp.bfloat16),
        pltpu.VMEM((3, 2048, 128), jnp.bfloat16),
        pltpu.VMEM((2, 2048, 128), jnp.bfloat16),
        pltpu.SemaphoreType.DMA((7,)),
    ]
    stored = (cache, long_cache, w_query, key_weight, value_weight)
    tables = (norm_gain, q_gain, k_gain, cosine, sine)

    def project_out(layer, state, side):
        far = permute(state, "replica", lambda i: i ^ 1)
        part = pl.pallas_call(
            functools.partial(out_kernel, layer),
            out_shape=jax.ShapeDtypeStruct((ROWS, 2048), jnp.float32),
            in_specs=[VM, VM, VM, ANY],
            out_specs=VM,
            scratch_shapes=[pltpu.VMEM((256, 2048), jnp.bfloat16), pltpu.SemaphoreType.DMA(())],
            compiler_params=params,
            name=f"out_projection_{layer}",
        )(state, far, side, w_out)
        part = (part + permute(part, "tensor", lambda i: i ^ 1)).astype(jnp.bfloat16)
        received = [permute(part, "tensor", lambda i, k=k: i ^ k) for k in (2, 4, 6)]
        return (part, *received)

    state, side, fresh_0, hidden = pl.pallas_call(
        first_kernel,
        out_shape=out_shape,
        in_specs=[SM] * 3 + [VM] * 8 + [ANY] * 5,
        out_specs=(VM,) * 4,
        scratch_shapes=scratch,
        compiler_params=params,
        name="attention_0",
    )(group_1, lengths, long_lengths, tokens, long_tokens, far_token, *tables, *map(in_hbm, stored))
    terms = project_out(0, state, side)
    buffers = ((2048, 256), (2048, 128), (2048, 128)) + ((3, 2048, 128), (2, 2048, 128)) * 2
    gate, *stored = lax.optimization_barrier((terms[0], *stored))
    terms = (gate, *terms[1:])
    stored = pl.pallas_call(
        fetch_kernel,
        out_shape=tuple(pltpu.VMEM(shape, jnp.bfloat16) for shape in buffers),
        in_specs=[ANY] * 5,
        out_specs=(ANY,) * 7,
        scratch_shapes=[pltpu.SemaphoreType.DMA((7,))],
        compiler_params=small,
        name="fetch_1",
    )(*map(in_hbm, stored))
    state, side, fresh_1, hidden = pl.pallas_call(
        second_kernel,
        out_shape=out_shape,
        in_specs=[SM] * 3 + [VM] * 17,
        out_specs=(VM,) * 4,
        compiler_params=params,
        name="attention_1",
    )(group_1, lengths, long_lengths, hidden, *terms, *tables, *stored)
    terms = project_out(1, state, side)
    stay, long_out, leave = pl.pallas_call(
        final_kernel,
        out_shape=(
            jax.ShapeDtypeStruct((2, 2048), jnp.float32),
            jax.ShapeDtypeStruct((1, 2048), jnp.float32),
            jax.ShapeDtypeStruct((1, 2560), jnp.float32),
        ),
        in_specs=[SM] + [VM] * 7,
        out_specs=(VM,) * 3,
        scratch_shapes=[pltpu.VMEM((ROWS, 2048), jnp.float32)],
        compiler_params=params,
        name="final_rows",
    )(group_1, hidden, *terms, fresh_0, fresh_1)
    arrived = permute(leave, "replica", lambda i: (i + groups // 2) % groups)
    partner = (group + groups // 2) % groups
    arrived_len = lax.dynamic_slice_in_dim(lengths, partner * 3 + 2, 1)
    first, second = in_vmem(first), in_vmem(second)
    stored = pl.pallas_call(
        store_kernel,
        out_shape=pltpu.HBM((2, 2, 2048, 128), jnp.bfloat16),
        in_specs=[ANY],
        out_specs=ANY,
        scratch_shapes=[pltpu.SemaphoreType.DMA((FIRST,))],
        compiler_params=small,
        name="store_first",
    )(first)
    out_hidden, moved = pl.pallas_call(
        arrival_kernel,
        out_shape=(
            pltpu.HBM((3, 2048), jnp.float32),
            pltpu.HBM((2, 2, 2048, 128), jnp.bfloat16),
        ),
        in_specs=[SM, VM, VM, VM, VM, ANY],
        out_specs=(ANY, ANY),
        input_output_aliases={5: 1},
        scratch_shapes=[
            pltpu.VMEM((3, 2048), jnp.float32),
            pltpu.VMEM((4, 16, 128), jnp.bfloat16),
            pltpu.SemaphoreType.DMA((9,)),
        ],
        compiler_params=small,
        name="arrival",
    )(arrived_len, stay, arrived, first, second, stored)
    return (out_hidden, long_out, moved[None, :, :, :, None, :])


def solution(mesh):
    return jax.shard_map(
        local,
        mesh=mesh,
        in_specs=(
            P("replica", None),
            P("replica", None),
            P(None, None, "replica", None, "tensor", None),
            P(None, None, "replica", None, None, "tensor", None),
            P(),
            P(),
            P(),
            P(),
            P(),
            P(None, None, "tensor"),
            P(None, None, "tensor"),
            P(None, None, "tensor"),
            P(None, "tensor", None),
        ),
        out_specs=(
            P("replica", None),
            P("replica", None),
            P("replica", None, None, None, "tensor", None),
        ),
        check_vma=False,
    )
```

```python
import functools

import jax
import jax.numpy as jnp
import numpy as np
from jax import lax
from jax.experimental import pallas as pl
from jax.experimental.pallas import tpu as pltpu
from jax.sharding import PartitionSpec as P

EPSILON = 1e-06
ROPE_BASE = 1000000.0
NEGATIVE = -1e30
ROWS = 8
ANY = pl.BlockSpec(memory_space=pl.ANY)
VM = pl.BlockSpec(memory_space=pltpu.VMEM)
SM = pl.BlockSpec(memory_space=pltpu.SMEM)


def permute(value, axis, target):
    pairs = [(source, target(source)) for source in range(lax.axis_size(axis))]
    return lax.ppermute(value, axis, pairs)


def in_hbm(value):
    return pltpu.with_memory_space_constraint(value, pltpu.HBM)


def in_vmem(value):
    return pltpu.with_memory_space_constraint(value, pltpu.VMEM)


def row_of(count):
    return lax.broadcasted_iota(jnp.int32, (count, 1), 0)


def attention_step(
    layer, group_ref, lengths_ref, long_lengths_ref, hidden, gain_ref, q_gain_ref, k_gain_ref,
    cosine_ref, sine_ref, stored, state_ref, side_ref, fresh_ref, ready,
):
    wq, wk, wv, keys, long_keys, values, long_values = stored
    rows = hidden()
    scale = lax.rsqrt(jnp.mean(rows * rows, axis=-1, keepdims=True) + EPSILON)
    normed = (rows * scale * gain_ref[layer : layer + 1, :]).astype(jnp.bfloat16)
    ready(0, 1, 2)
    queries = jnp.dot(normed, wq[...], preferred_element_type=jnp.float32)
    new_keys = jnp.dot(normed, wk[...], preferred_element_type=jnp.float32)
    new_values = jnp.dot(normed, wv[...], preferred_element_type=jnp.float32).astype(jnp.bfloat16)

    def finish(heads, gain, cosine, sine):
        heads = heads * lax.rsqrt(jnp.mean(heads * heads, axis=-1, keepdims=True) + EPSILON) * gain
        return (heads * cosine + pltpu.roll(heads, 64, 1) * sine).astype(jnp.bfloat16)

    cosine, sine = cosine_ref[...], sine_ref[...]
    q_gain = q_gain_ref[layer : layer + 1, :]
    q0 = finish(queries[:, :128], q_gain, cosine, sine).astype(jnp.float32)
    q1 = finish(queries[:, 128:], q_gain, cosine, sine).astype(jnp.float32)
    key_new = finish(new_keys, k_gain_ref[layer : layer + 1, :], cosine, sine).astype(jnp.float32)
    value_new = new_values.astype(jnp.float32)
    fresh_ref[0:1, :] = key_new[2:3, :]
    fresh_ref[1:2, :] = value_new[2:3, :]
    both = jnp.concatenate([q0, q1], axis=0)
    query = both.astype(jnp.bfloat16)
    keys_twice = jnp.concatenate([key_new, key_new], axis=0)
    values_twice = jnp.concatenate([value_new, value_new], axis=0)
    factor = 128 ** (-0.5)
    own = jnp.sum(both * keys_twice, axis=-1, keepdims=True) * factor

    group = group_ref[0]
    parity = lax.rem(group, 2)
    which = lax.rem(row_of(16), 8)
    limit = jnp.ones((16, 1), jnp.int32)
    for r in range(3):
        limit = jnp.where(which == r, lengths_ref[group * 3 + r], limit)
    for r in range(2):
        limit = jnp.where(
            which == 3 + r, long_lengths_ref[group - parity + r] - parity * 2048, limit
        )
    scores = jnp.zeros((16, 2048), jnp.float32)
    for r in range(5):
        if r == 0:
            ready(3)
        if r == 3:
            ready(4)
        block = keys[r] if r < 3 else long_keys[r - 3]
        product = lax.dot_general(
            query, block, (((1,), (1,)), ((), ())), preferred_element_type=jnp.float32
        )
        scores = jnp.where(which == r, product, scores)
    places = lax.broadcasted_iota(jnp.int32, (16, 2048), 1)
    scores = jnp.where(places < limit, scores * factor, NEGATIVE)
    is_main = which < 3
    highest = jnp.max(scores, axis=-1, keepdims=True)
    highest = jnp.where(is_main, jnp.maximum(highest, own), highest)
    weights = jnp.exp(scores - highest)
    own_weight = jnp.where(is_main, jnp.exp(own - highest), 0.0)
    total = jnp.sum(weights, axis=-1, keepdims=True) + own_weight
    rounded = weights.astype(jnp.bfloat16)
    summed = own_weight.astype(jnp.bfloat16).astype(jnp.float32) * values_twice
    for r in range(5):
        if r == 0:
            ready(5)
        if r == 3:
            ready(6)
        block = values[r] if r < 3 else long_values[r - 3]
        product = jnp.dot(rounded, block, preferred_element_type=jnp.float32)
        summed = summed + jnp.where(which == r, product, 0.0)
    state_ref[:, 0:128] = summed
    lanes = lax.broadcasted_iota(jnp.int32, (16, 128), 1)
    state_ref[:, 128:256] = jnp.where(lanes < 64, highest, total)
    side_ref[:, 0:128] = jnp.broadcast_to(own, (16, 128))
    side_ref[:, 128:256] = values_twice


def parts_of(layer, cache_ref, long_ref, wq_ref, wk_ref, wv_ref):
    return (
        wq_ref.at[layer], wk_ref.at[layer], wv_ref.at[layer],
        cache_ref.at[layer, 0], long_ref.at[layer, 0, 0],
        cache_ref.at[layer, 1], long_ref.at[layer, 1, 0],
    )


def first_kernel(
    group_ref, lengths_ref, long_lengths_ref, tokens_ref, own_long_ref, far_long_ref, *rest
):
    tables, held = rest[:5], rest[5:10]
    state_ref, side_ref, fresh_ref, hidden_ref = rest[10:14]
    buffers, semaphores = rest[14:21], rest[21]
    copies = [
        pltpu.make_async_copy(source, target, semaphores.at[i])
        for i, (source, target) in enumerate(zip(parts_of(0, *held), buffers))
    ]
    for copy in copies:
        copy.start()

    def ready(*which):
        for i in which:
            copies[i].wait()

    def hidden():
        own = own_long_ref[...].astype(jnp.float32)
        far = far_long_ref[...].astype(jnp.float32)
        even = lax.rem(group_ref[0], 2) == 0
        hidden_ref[...] = jnp.zeros((ROWS, 2048), jnp.float32)
        hidden_ref[0:3, :] = tokens_ref[...].astype(jnp.float32)
        hidden_ref[3:4, :] = jnp.where(even, own, far)
        hidden_ref[4:5, :] = jnp.where(even, far, own)
        return hidden_ref[...]

    attention_step(
        0, group_ref, lengths_ref, long_lengths_ref, hidden, *tables, buffers,
        state_ref, side_ref, fresh_ref, ready,
    )


def total_of(p_ref, r1_ref, r2_ref, r3_ref):
    p, r1, r2, r3 = (ref[...].astype(jnp.float32) for ref in (p_ref, r1_ref, r2_ref, r3_ref))
    return (p + r1) + (r2 + r3)


def second_kernel(
    group_ref, lengths_ref, long_lengths_ref, before_ref, p_ref, r1_ref, r2_ref, r3_ref, *rest
):
    tables, stored = rest[:5], rest[5:12]
    state_ref, side_ref, fresh_ref, hidden_ref = rest[12:16]

    def hidden():
        summed = total_of(p_ref, r1_ref, r2_ref, r3_ref)
        rows = (before_ref[...] + summed).astype(jnp.bfloat16).astype(jnp.float32)
        hidden_ref[...] = rows
        return rows

    attention_step(
        1, group_ref, lengths_ref, long_lengths_ref, hidden, *tables, stored,
        state_ref, side_ref, fresh_ref, lambda *which: None,
    )


UNIT = 256
FIRST = 23
PER = 2048 // UNIT
SECOND = 4 * PER - FIRST


def plane_of(unit):
    return unit // (2 * PER), unit // PER % 2, pl.ds(unit % PER * UNIT, UNIT)


def runs(begin, end):
    out, at = [], begin
    while at < end:
        stop = min(end, at // PER * PER + PER)
        i, j, _ = plane_of(at)
        out.append((i, j, at % PER * UNIT, (stop - at) * UNIT, (at - begin) * UNIT))
        at = stop
    return out


def leaving_kernel(begin, end, cache_ref, out_ref, unused_ref, semaphores):
    del unused_ref
    copies = []
    for n, (i, j, place, size, at) in enumerate(runs(begin, end)):
        copies.append(
            pltpu.make_async_copy(
                cache_ref.at[i, j, 2, pl.ds(place, size)], out_ref.at[pl.ds(at, size)],
                semaphores.at[n],
            )
        )
    for copy in copies:
        copy.start()
    for copy in copies:
        copy.wait()


def store_kernel(length_ref, first_ref, stored_ref, blocks_ref, buffer, semaphores):
    reads, writes = [], []
    for n in range(FIRST):
        i, j, rows = plane_of(n)
        piece = pl.ds(n * UNIT, UNIT)
        reads.append(
            pltpu.make_async_copy(first_ref.at[piece], buffer.at[piece], semaphores.at[0, n])
        )
        writes.append(
            pltpu.make_async_copy(buffer.at[piece], stored_ref.at[i, j, rows], semaphores.at[1, n])
        )
    for copy in reads:
        copy.start()
    for read, write in zip(reads, writes):
        read.wait()
        write.start()
    start = length_ref[0] // 16 * 16
    for plane in range(4):
        at = jnp.minimum(plane * 2048 + start, FIRST * UNIT - 16)
        blocks_ref[plane] = buffer[pl.ds(pl.multiple_of(at, 16), 16), :]
    for copy in writes:
        copy.wait()


def arrival_kernel(
    length_ref, stay_ref, arrived_ref, blocks_ref, second_ref, stored_ref, out_ref, moved_ref,
    rows, blocks, patched, semaphores,
):
    del stored_ref
    length = length_ref[0]
    hit_unit = length // UNIT
    units = [(unit, *plane_of(unit)) for unit in range(FIRST, 4 * PER)]

    def straight(unit, i, j, place):
        return pltpu.make_async_copy(
            second_ref.at[pl.ds((unit - FIRST) * UNIT, UNIT)], moved_ref.at[i, j, place],
            semaphores.at[unit - FIRST],
        )

    def changed(unit, i, j, place):
        return pltpu.make_async_copy(
            patched.at[unit // PER], moved_ref.at[i, j, place], semaphores.at[unit - FIRST]
        )

    for unit in units:

        @pl.when(hit_unit != unit[0] % PER)
        def _():
            straight(*unit).start()

    fresh = [arrived_ref[0:1, 2048 + 128 * n : 2176 + 128 * n] for n in range(4)]
    start = pl.multiple_of(length // 16 * 16, 16)
    early = []
    for plane in range((FIRST + PER - 1) // PER):
        block = blocks_ref[plane].astype(jnp.float32)
        blocks[plane] = jnp.where(row_of(16) == length - start, fresh[plane], block).astype(
            jnp.bfloat16
        )
        write = pltpu.make_async_copy(
            blocks.at[plane], moved_ref.at[plane // 2, plane % 2, pl.ds(start, 16)],
            semaphores.at[SECOND + plane],
        )
        early.append((plane * PER + hit_unit < FIRST, write))
    for inside, write in early:
        pl.when(inside)(write.start)
    for plane in range(FIRST // PER, 4):
        at = jnp.maximum(plane * PER + hit_unit - FIRST, 0) * UNIT
        whole = second_ref[pl.ds(pl.multiple_of(at, UNIT), UNIT), :].astype(jnp.float32)
        patched[plane] = jnp.where(
            row_of(UNIT) == length - hit_unit * UNIT, fresh[plane], whole
        ).astype(jnp.bfloat16)
    for unit in units:

        @pl.when(hit_unit == unit[0] % PER)
        def _():
            changed(*unit).start()

    rows[0:2, :] = stay_ref[...]
    rows[2:3, :] = arrived_ref[0:1, 0:2048]
    out = pltpu.make_async_copy(rows, out_ref, semaphores.at[SECOND + 4])
    out.start()
    for unit in units:
        straight(*unit).wait()
    for inside, write in early:
        pl.when(inside)(write.wait)
    out.wait()


def fetch_kernel(*refs):
    held, outputs, semaphores = refs[:5], refs[5:12], refs[12]
    copies = [
        pltpu.make_async_copy(source, target, semaphores.at[i])
        for i, (source, target) in enumerate(zip(parts_of(1, *held), outputs))
    ]
    for copy in copies:
        copy.start()
    for copy in copies:
        copy.wait()


def out_kernel(layer, state_ref, far_ref, side_ref, w_ref, out_ref, w, semaphore):
    copy = pltpu.make_async_copy(w_ref.at[layer], w, semaphore)
    copy.start()
    is_main = lax.rem(row_of(16), 8) < 3
    here, far = state_ref[...], far_ref[...]
    m_here, l_here, acc_here = here[:, 128:129], here[:, 192:193], here[:, :128]
    m_far, l_far, acc_far = far[:, 128:129], far[:, 192:193], far[:, :128]
    own, value = side_ref[:, 0:1], side_ref[:, 128:256]
    highest = jnp.maximum(jnp.maximum(m_here, m_far), own)
    f_here, f_far = jnp.exp(m_here - highest), jnp.exp(m_far - highest)
    own_weight = jnp.exp(own - highest)
    total = (l_here * f_here + l_far * f_far) + own_weight
    own_rounded = own_weight.astype(jnp.bfloat16).astype(jnp.float32)
    summed = (acc_here * f_here + acc_far * f_far) + own_rounded * value
    total = jnp.where(is_main, l_here, total)
    summed = jnp.where(is_main, acc_here, summed)
    attended = summed / total
    attended = jnp.concatenate([attended[:8], attended[8:]], axis=1).astype(jnp.bfloat16)
    copy.wait()
    out_ref[...] = jnp.dot(attended, w[...], preferred_element_type=jnp.float32)


def final_kernel(
    group_ref, before_ref, p_ref, r1_ref, r2_ref, r3_ref, fresh0_ref, fresh1_ref,
    stay_ref, long_ref, leave_ref, scratch,
):
    scratch[...] = before_ref[...] + total_of(p_ref, r1_ref, r2_ref, r3_ref)
    stay_ref[...] = scratch[0:2, :]
    odd = lax.rem(group_ref[0], 2) == 1
    long_ref[...] = jnp.where(odd, scratch[4:5, :], scratch[3:4, :])
    leave_ref[0:1, 0:2048] = scratch[2:3, :]
    for i, ref in enumerate((fresh0_ref, fresh1_ref)):
        for j in range(2):
            leave_ref[0:1, 2048 + 128 * (2 * i + j) : 2176 + 128 * (2 * i + j)] = ref[j : j + 1, :]


def local(
    tokens, long_tokens, cache, long_cache, lengths, long_lengths, norm_gain, q_gain, k_gain,
    w_query, key_weight, value_weight, w_out,
):
    groups = lax.axis_size("replica")
    group = lax.axis_index("replica")
    parity = group % 2
    group_1 = group[None]
    cache = cache.reshape(2, 2, 3, 2048, 128)
    long_cache = long_cache.reshape(2, 2, 1, 2, 2048, 128)

    params = pltpu.CompilerParams(vmem_limit_bytes=16 * 2**20)
    small = pltpu.CompilerParams(vmem_limit_bytes=2 * 2**20)
    held = in_hbm(cache)

    def leaving(begin, count, name):
        return pl.pallas_call(
            functools.partial(leaving_kernel, begin, begin + count),
            out_shape=(
                pltpu.VMEM((count * UNIT, 128), jnp.bfloat16),
                pltpu.VMEM((8, 128), jnp.float32),
            ),
            in_specs=[ANY],
            out_specs=(ANY, ANY),
            scratch_shapes=[pltpu.SemaphoreType.DMA((4,))],
            compiler_params=small,
            name=name,
        )(held)

    first, _ = leaving(0, FIRST, "leaving_first")
    second, _ = leaving(FIRST, SECOND, "leaving_second")
    first, second = (
        permute(piece, "replica", lambda i: (i + groups // 2) % groups) for piece in (first, second)
    )
    far_token = permute(long_tokens, "replica", lambda i: i ^ 1)

    places = jnp.concatenate(
        [
            lax.dynamic_slice_in_dim(lengths, group * 3, 3),
            lax.dynamic_slice_in_dim(long_lengths, group - parity, 2),
            jnp.zeros((3,), jnp.int32),
        ]
    ).astype(jnp.float32)
    inverse = np.float64(ROPE_BASE) ** (-2.0 * np.arange(64) / 128)
    inverse = jnp.asarray(np.concatenate([inverse, inverse]).astype(np.float32))
    sign = jnp.asarray(np.where(np.arange(128) < 64, -1.0, 1.0).astype(np.float32))
    angles = places[:, None] * inverse[None, :]
    cosine, sine = jnp.cos(angles), jnp.sin(angles) * sign

    out_shape = (
        jax.ShapeDtypeStruct((16, 256), jnp.float32),
        jax.ShapeDtypeStruct((16, 256), jnp.float32),
        jax.ShapeDtypeStruct((2, 128), jnp.float32),
        jax.ShapeDtypeStruct((ROWS, 2048), jnp.float32),
    )
    scratch = [
        pltpu.VMEM((2048, 256), jnp.bfloat16),
        pltpu.VMEM((2048, 128), jnp.bfloat16),
        pltpu.VMEM((2048, 128), jnp.bfloat16),
        pltpu.VMEM((3, 2048, 128), jnp.bfloat16),
        pltpu.VMEM((2, 2048, 128), jnp.bfloat16),
        pltpu.VMEM((3, 2048, 128), jnp.bfloat16),
        pltpu.VMEM((2, 2048, 128), jnp.bfloat16),
        pltpu.SemaphoreType.DMA((7,)),
    ]
    stored = (cache, long_cache, w_query, key_weight, value_weight)
    tables = (norm_gain, q_gain, k_gain, cosine, sine)

    def project_out(layer, state, side):
        far = permute(state, "replica", lambda i: i ^ 1)
        part = pl.pallas_call(
            functools.partial(out_kernel, layer),
            out_shape=jax.ShapeDtypeStruct((ROWS, 2048), jnp.float32),
            in_specs=[VM, VM, VM, ANY],
            out_specs=VM,
            scratch_shapes=[pltpu.VMEM((256, 2048), jnp.bfloat16), pltpu.SemaphoreType.DMA(())],
            compiler_params=params,
            name=f"out_projection_{layer}",
        )(state, far, side, w_out)
        part = (part + permute(part, "tensor", lambda i: i ^ 1)).astype(jnp.bfloat16)
        received = [permute(part, "tensor", lambda i, k=k: i ^ k) for k in (2, 4, 6)]
        return (part, *received)

    state, side, fresh_0, hidden = pl.pallas_call(
        first_kernel,
        out_shape=out_shape,
        in_specs=[SM] * 3 + [VM] * 8 + [ANY] * 5,
        out_specs=(VM,) * 4,
        scratch_shapes=scratch,
        compiler_params=params,
        name="attention_0",
    )(group_1, lengths, long_lengths, tokens, long_tokens, far_token, *tables, *map(in_hbm, stored))
    terms = project_out(0, state, side)
    buffers = ((2048, 256), (2048, 128), (2048, 128)) + ((3, 2048, 128), (2, 2048, 128)) * 2
    gate, *stored = lax.optimization_barrier((terms[0], *stored))
    terms = (gate, *terms[1:])
    stored = pl.pallas_call(
        fetch_kernel,
        out_shape=tuple(pltpu.VMEM(shape, jnp.bfloat16) for shape in buffers),
        in_specs=[ANY] * 5,
        out_specs=(ANY,) * 7,
        scratch_shapes=[pltpu.SemaphoreType.DMA((7,))],
        compiler_params=small,
        name="fetch_1",
    )(*map(in_hbm, stored))
    state, side, fresh_1, hidden = pl.pallas_call(
        second_kernel,
        out_shape=out_shape,
        in_specs=[SM] * 3 + [VM] * 17,
        out_specs=(VM,) * 4,
        compiler_params=params,
        name="attention_1",
    )(group_1, lengths, long_lengths, hidden, *terms, *tables, *stored)
    terms = project_out(1, state, side)
    stay, long_out, leave = pl.pallas_call(
        final_kernel,
        out_shape=(
            jax.ShapeDtypeStruct((2, 2048), jnp.float32),
            jax.ShapeDtypeStruct((1, 2048), jnp.float32),
            jax.ShapeDtypeStruct((1, 2560), jnp.float32),
        ),
        in_specs=[SM] + [VM] * 7,
        out_specs=(VM,) * 3,
        scratch_shapes=[pltpu.VMEM((ROWS, 2048), jnp.float32)],
        compiler_params=params,
        name="final_rows",
    )(group_1, hidden, *terms, fresh_0, fresh_1)
    arrived = permute(leave, "replica", lambda i: (i + groups // 2) % groups)
    partner = (group + groups // 2) % groups
    arrived_len = lax.dynamic_slice_in_dim(lengths, partner * 3 + 2, 1)
    stored, blocks = pl.pallas_call(
        store_kernel,
        out_shape=(
            pltpu.HBM((2, 2, 2048, 128), jnp.bfloat16),
            pltpu.VMEM((4, 16, 128), jnp.bfloat16),
        ),
        in_specs=[SM, ANY],
        out_specs=(ANY, VM),
        scratch_shapes=[
            pltpu.VMEM((FIRST * UNIT, 128), jnp.bfloat16),
            pltpu.SemaphoreType.DMA((2, FIRST)),
        ],
        compiler_params=pltpu.CompilerParams(vmem_limit_bytes=4 * 2**20),
        name="store_first",
    )(arrived_len, in_hbm(first))
    out_hidden, moved = pl.pallas_call(
        arrival_kernel,
        out_shape=(
            pltpu.HBM((3, 2048), jnp.float32),
            pltpu.HBM((2, 2, 2048, 128), jnp.bfloat16),
        ),
        in_specs=[SM, VM, VM, VM, VM, ANY],
        out_specs=(ANY, ANY),
        input_output_aliases={5: 1},
        scratch_shapes=[
            pltpu.VMEM((3, 2048), jnp.float32),
            pltpu.VMEM((4, 16, 128), jnp.bfloat16),
            pltpu.VMEM((4, UNIT, 128), jnp.bfloat16),
            pltpu.SemaphoreType.DMA((SECOND + 5,)),
        ],
        compiler_params=small,
        name="arrival",
    )(arrived_len, stay, arrived, blocks, in_vmem(second), stored)
    return (out_hidden, long_out, moved[None, :, :, :, None, :])


def solution(mesh):
    return jax.shard_map(
        local,
        mesh=mesh,
        in_specs=(
            P("replica", None),
            P("replica", None),
            P(None, None, "replica", None, "tensor", None),
            P(None, None, "replica", None, None, "tensor", None),
            P(),
            P(),
            P(),
            P(),
            P(),
            P(None, None, "tensor"),
            P(None, None, "tensor"),
            P(None, None, "tensor"),
            P(None, "tensor", None),
        ),
        out_specs=(
            P("replica", None),
            P("replica", None),
            P("replica", None, None, None, "tensor", None),
        ),
        check_vma=False,
    )
```

```python
import functools

import jax
import jax.numpy as jnp
import numpy as np
from jax import lax
from jax.experimental import pallas as pl
from jax.experimental.pallas import tpu as pltpu
from jax.sharding import PartitionSpec as P

EPSILON = 1e-06
ROPE_BASE = 1000000.0
NEGATIVE = -1e30
ROWS = 8
ANY = pl.BlockSpec(memory_space=pl.ANY)
VM = pl.BlockSpec(memory_space=pltpu.VMEM)
SM = pl.BlockSpec(memory_space=pltpu.SMEM)


def permute(value, axis, target):
    pairs = [(source, target(source)) for source in range(lax.axis_size(axis))]
    return lax.ppermute(value, axis, pairs)


def in_hbm(value):
    return pltpu.with_memory_space_constraint(value, pltpu.HBM)


def in_vmem(value):
    return pltpu.with_memory_space_constraint(value, pltpu.VMEM)


def row_of(count):
    return lax.broadcasted_iota(jnp.int32, (count, 1), 0)


def attention_step(
    layer, group_ref, lengths_ref, long_lengths_ref, hidden, gain_ref, q_gain_ref, k_gain_ref,
    cosine_ref, sine_ref, stored, state_ref, side_ref, fresh_ref, ready,
):
    wq, wk, wv, keys, long_keys, values, long_values = stored
    rows = hidden()
    scale = lax.rsqrt(jnp.mean(rows * rows, axis=-1, keepdims=True) + EPSILON)
    normed = (rows * scale * gain_ref[layer : layer + 1, :]).astype(jnp.bfloat16)
    ready(0, 1, 2)
    queries = jnp.dot(normed, wq[...], preferred_element_type=jnp.float32)
    new_keys = jnp.dot(normed, wk[...], preferred_element_type=jnp.float32)
    new_values = jnp.dot(normed, wv[...], preferred_element_type=jnp.float32).astype(jnp.bfloat16)

    def finish(heads, gain, cosine, sine):
        heads = heads * lax.rsqrt(jnp.mean(heads * heads, axis=-1, keepdims=True) + EPSILON) * gain
        return (heads * cosine + pltpu.roll(heads, 64, 1) * sine).astype(jnp.bfloat16)

    cosine, sine = cosine_ref[...], sine_ref[...]
    q_gain = q_gain_ref[layer : layer + 1, :]
    q0 = finish(queries[:, :128], q_gain, cosine, sine).astype(jnp.float32)
    q1 = finish(queries[:, 128:], q_gain, cosine, sine).astype(jnp.float32)
    key_new = finish(new_keys, k_gain_ref[layer : layer + 1, :], cosine, sine).astype(jnp.float32)
    value_new = new_values.astype(jnp.float32)
    fresh_ref[0:1, :] = key_new[2:3, :]
    fresh_ref[1:2, :] = value_new[2:3, :]
    both = jnp.concatenate([q0, q1], axis=0)
    query = both.astype(jnp.bfloat16)
    keys_twice = jnp.concatenate([key_new, key_new], axis=0)
    values_twice = jnp.concatenate([value_new, value_new], axis=0)
    factor = 128 ** (-0.5)
    own = jnp.sum(both * keys_twice, axis=-1, keepdims=True) * factor

    group = group_ref[0]
    parity = lax.rem(group, 2)
    which = lax.rem(row_of(16), 8)
    limit = jnp.ones((16, 1), jnp.int32)
    for r in range(3):
        limit = jnp.where(which == r, lengths_ref[group * 3 + r], limit)
    for r in range(2):
        limit = jnp.where(
            which == 3 + r, long_lengths_ref[group - parity + r] - parity * 2048, limit
        )
    scores = jnp.zeros((16, 2048), jnp.float32)
    for r in range(5):
        if r == 0:
            ready(3)
        if r == 3:
            ready(4)
        block = keys[r] if r < 3 else long_keys[r - 3]
        product = lax.dot_general(
            query, block, (((1,), (1,)), ((), ())), preferred_element_type=jnp.float32
        )
        scores = jnp.where(which == r, product, scores)
    places = lax.broadcasted_iota(jnp.int32, (16, 2048), 1)
    scores = jnp.where(places < limit, scores * factor, NEGATIVE)
    is_main = which < 3
    highest = jnp.max(scores, axis=-1, keepdims=True)
    highest = jnp.where(is_main, jnp.maximum(highest, own), highest)
    weights = jnp.exp(scores - highest)
    own_weight = jnp.where(is_main, jnp.exp(own - highest), 0.0)
    total = jnp.sum(weights, axis=-1, keepdims=True) + own_weight
    rounded = weights.astype(jnp.bfloat16)
    summed = own_weight.astype(jnp.bfloat16).astype(jnp.float32) * values_twice
    for r in range(5):
        if r == 0:
            ready(5)
        if r == 3:
            ready(6)
        block = values[r] if r < 3 else long_values[r - 3]
        product = jnp.dot(rounded, block, preferred_element_type=jnp.float32)
        summed = summed + jnp.where(which == r, product, 0.0)
    state_ref[:, 0:128] = summed
    lanes = lax.broadcasted_iota(jnp.int32, (16, 128), 1)
    state_ref[:, 128:256] = jnp.where(lanes < 64, highest, total)
    side_ref[:, 0:128] = jnp.broadcast_to(own, (16, 128))
    side_ref[:, 128:256] = values_twice


def parts_of(layer, cache_ref, long_ref, wq_ref, wk_ref, wv_ref):
    return (
        wq_ref.at[layer], wk_ref.at[layer], wv_ref.at[layer],
        cache_ref.at[layer, 0], long_ref.at[layer, 0, 0],
        cache_ref.at[layer, 1], long_ref.at[layer, 1, 0],
    )


def first_kernel(
    group_ref, lengths_ref, long_lengths_ref, tokens_ref, own_long_ref, far_long_ref, *rest
):
    tables, resident, held = rest[:5], rest[5:10], rest[10:12]
    state_ref, side_ref, fresh_ref, hidden_ref = rest[12:16]
    buffers, semaphores = rest[16:18], rest[18]
    sources = (held[0].at[0, 1], held[1].at[0, 1, 0])
    copies = [
        pltpu.make_async_copy(source, target, semaphores.at[i])
        for i, (source, target) in enumerate(zip(sources, buffers))
    ]
    for copy in copies:
        copy.start()

    def ready(*which):
        for i in which:
            if i >= 5:
                copies[i - 5].wait()

    def hidden():
        own = own_long_ref[...].astype(jnp.float32)
        far = far_long_ref[...].astype(jnp.float32)
        even = lax.rem(group_ref[0], 2) == 0
        hidden_ref[...] = jnp.zeros((ROWS, 2048), jnp.float32)
        hidden_ref[0:3, :] = tokens_ref[...].astype(jnp.float32)
        hidden_ref[3:4, :] = jnp.where(even, own, far)
        hidden_ref[4:5, :] = jnp.where(even, far, own)
        return hidden_ref[...]

    attention_step(
        0, group_ref, lengths_ref, long_lengths_ref, hidden, *tables, (*resident, *buffers),
        state_ref, side_ref, fresh_ref, ready,
    )


def total_of(p_ref, r1_ref, r2_ref, r3_ref):
    p, r1, r2, r3 = (ref[...].astype(jnp.float32) for ref in (p_ref, r1_ref, r2_ref, r3_ref))
    return (p + r1) + (r2 + r3)


def second_kernel(
    group_ref, lengths_ref, long_lengths_ref, before_ref, p_ref, r1_ref, r2_ref, r3_ref, *rest
):
    tables, stored = rest[:5], rest[5:12]
    state_ref, side_ref, fresh_ref, hidden_ref = rest[12:16]

    def hidden():
        summed = total_of(p_ref, r1_ref, r2_ref, r3_ref)
        rows = (before_ref[...] + summed).astype(jnp.bfloat16).astype(jnp.float32)
        hidden_ref[...] = rows
        return rows

    attention_step(
        1, group_ref, lengths_ref, long_lengths_ref, hidden, *tables, stored,
        state_ref, side_ref, fresh_ref, lambda *which: None,
    )


UNIT = 256
FIRST = 23
PER = 2048 // UNIT
SECOND = 4 * PER - FIRST


def plane_of(unit):
    return unit // (2 * PER), unit // PER % 2, pl.ds(unit % PER * UNIT, UNIT)


def runs(begin, end):
    out, at = [], begin
    while at < end:
        stop = min(end, at // PER * PER + PER)
        i, j, _ = plane_of(at)
        out.append((i, j, at % PER * UNIT, (stop - at) * UNIT, (at - begin) * UNIT))
        at = stop
    return out


def leaving_kernel(begin, end, cache_ref, out_ref, unused_ref, semaphores):
    del unused_ref
    copies = []
    for n, (i, j, place, size, at) in enumerate(runs(begin, end)):
        copies.append(
            pltpu.make_async_copy(
                cache_ref.at[i, j, 2, pl.ds(place, size)], out_ref.at[pl.ds(at, size)],
                semaphores.at[n],
            )
        )
    for copy in copies:
        copy.start()
    for copy in copies:
        copy.wait()


def store_kernel(length_ref, first_ref, after_ref, stored_ref, blocks_ref, buffer, semaphores):
    del after_ref
    reads, writes = [], []
    for n in range(FIRST):
        i, j, rows = plane_of(n)
        piece = pl.ds(n * UNIT, UNIT)
        reads.append(
            pltpu.make_async_copy(first_ref.at[piece], buffer.at[piece], semaphores.at[0, n])
        )
        writes.append(
            pltpu.make_async_copy(buffer.at[piece], stored_ref.at[i, j, rows], semaphores.at[1, n])
        )
    for copy in reads:
        copy.start()
    for read, write in zip(reads, writes):
        read.wait()
        write.start()
    start = length_ref[0] // 16 * 16
    for plane in range(4):
        at = jnp.minimum(plane * 2048 + start, FIRST * UNIT - 16)
        blocks_ref[plane] = buffer[pl.ds(pl.multiple_of(at, 16), 16), :]
    for copy in writes:
        copy.wait()


def arrival_kernel(
    length_ref, stay_ref, arrived_ref, blocks_ref, second_ref, stored_ref, out_ref, moved_ref,
    rows, blocks, patched, semaphores,
):
    del stored_ref
    length = length_ref[0]
    hit_unit = length // UNIT
    units = [(unit, *plane_of(unit)) for unit in range(FIRST, 4 * PER)]

    def straight(unit, i, j, place):
        return pltpu.make_async_copy(
            second_ref.at[pl.ds((unit - FIRST) * UNIT, UNIT)], moved_ref.at[i, j, place],
            semaphores.at[unit - FIRST],
        )

    def changed(unit, i, j, place):
        return pltpu.make_async_copy(
            patched.at[unit // PER], moved_ref.at[i, j, place], semaphores.at[unit - FIRST]
        )

    for unit in units:

        @pl.when(hit_unit != unit[0] % PER)
        def _():
            straight(*unit).start()

    fresh = [arrived_ref[0:1, 2048 + 128 * n : 2176 + 128 * n] for n in range(4)]
    start = pl.multiple_of(length // 16 * 16, 16)
    early = []
    for plane in range((FIRST + PER - 1) // PER):
        block = blocks_ref[plane].astype(jnp.float32)
        blocks[plane] = jnp.where(row_of(16) == length - start, fresh[plane], block).astype(
            jnp.bfloat16
        )
        write = pltpu.make_async_copy(
            blocks.at[plane], moved_ref.at[plane // 2, plane % 2, pl.ds(start, 16)],
            semaphores.at[SECOND + plane],
        )
        early.append((plane * PER + hit_unit < FIRST, write))
    for inside, write in early:
        pl.when(inside)(write.start)
    for plane in range(FIRST // PER, 4):
        at = jnp.maximum(plane * PER + hit_unit - FIRST, 0) * UNIT
        whole = second_ref[pl.ds(pl.multiple_of(at, UNIT), UNIT), :].astype(jnp.float32)
        patched[plane] = jnp.where(
            row_of(UNIT) == length - hit_unit * UNIT, fresh[plane], whole
        ).astype(jnp.bfloat16)
    for unit in units:

        @pl.when(hit_unit == unit[0] % PER)
        def _():
            changed(*unit).start()

    rows[0:2, :] = stay_ref[...]
    rows[2:3, :] = arrived_ref[0:1, 0:2048]
    out = pltpu.make_async_copy(rows, out_ref, semaphores.at[SECOND + 4])
    out.start()
    for unit in units:
        straight(*unit).wait()
    for inside, write in early:
        pl.when(inside)(write.wait)
    out.wait()


def fetch_kernel(layer, which, *refs):
    held, outputs, semaphores = refs[:5], refs[6 : 6 + len(which)], refs[-1]
    sources = parts_of(layer, *held)
    copies = [
        pltpu.make_async_copy(sources[i], output, semaphores.at[n])
        for n, (i, output) in enumerate(zip(which, outputs))
    ]
    for copy in copies:
        copy.start()
    for copy in copies:
        copy.wait()


def out_kernel(layer, state_ref, far_ref, side_ref, w_ref, after_ref, out_ref, w, semaphore):
    del after_ref
    copy = pltpu.make_async_copy(w_ref.at[layer], w, semaphore)
    copy.start()
    is_main = lax.rem(row_of(16), 8) < 3
    here, far = state_ref[...], far_ref[...]
    m_here, l_here, acc_here = here[:, 128:129], here[:, 192:193], here[:, :128]
    m_far, l_far, acc_far = far[:, 128:129], far[:, 192:193], far[:, :128]
    own, value = side_ref[:, 0:1], side_ref[:, 128:256]
    highest = jnp.maximum(jnp.maximum(m_here, m_far), own)
    f_here, f_far = jnp.exp(m_here - highest), jnp.exp(m_far - highest)
    own_weight = jnp.exp(own - highest)
    total = (l_here * f_here + l_far * f_far) + own_weight
    own_rounded = own_weight.astype(jnp.bfloat16).astype(jnp.float32)
    summed = (acc_here * f_here + acc_far * f_far) + own_rounded * value
    total = jnp.where(is_main, l_here, total)
    summed = jnp.where(is_main, acc_here, summed)
    attended = summed / total
    attended = jnp.concatenate([attended[:8], attended[8:]], axis=1).astype(jnp.bfloat16)
    copy.wait()
    out_ref[...] = jnp.dot(attended, w[...], preferred_element_type=jnp.float32)


def final_kernel(
    group_ref, before_ref, p_ref, r1_ref, r2_ref, r3_ref, fresh0_ref, fresh1_ref, after_ref,
    stay_ref, long_ref, leave_ref, scratch,
):
    del after_ref
    scratch[...] = before_ref[...] + total_of(p_ref, r1_ref, r2_ref, r3_ref)
    stay_ref[...] = scratch[0:2, :]
    odd = lax.rem(group_ref[0], 2) == 1
    long_ref[...] = jnp.where(odd, scratch[4:5, :], scratch[3:4, :])
    leave_ref[0:1, 0:2048] = scratch[2:3, :]
    for i, ref in enumerate((fresh0_ref, fresh1_ref)):
        for j in range(2):
            leave_ref[0:1, 2048 + 128 * (2 * i + j) : 2176 + 128 * (2 * i + j)] = ref[j : j + 1, :]


def local(
    tokens, long_tokens, cache, long_cache, lengths, long_lengths, norm_gain, q_gain, k_gain,
    w_query, key_weight, value_weight, w_out,
):
    groups = lax.axis_size("replica")
    group = lax.axis_index("replica")
    parity = group % 2
    group_1 = group[None]
    cache = cache.reshape(2, 2, 3, 2048, 128)
    long_cache = long_cache.reshape(2, 2, 1, 2, 2048, 128)

    params = pltpu.CompilerParams(vmem_limit_bytes=16 * 2**20)
    small = pltpu.CompilerParams(vmem_limit_bytes=2 * 2**20)
    held = in_hbm(cache)

    def leaving(begin, count, name):
        return pl.pallas_call(
            functools.partial(leaving_kernel, begin, begin + count),
            out_shape=(
                pltpu.VMEM((count * UNIT, 128), jnp.bfloat16),
                pltpu.VMEM((8, 128), jnp.float32),
            ),
            in_specs=[ANY],
            out_specs=(ANY, ANY),
            scratch_shapes=[pltpu.SemaphoreType.DMA((4,))],
            compiler_params=small,
            name=name,
        )(held)

    leaving_first, _ = leaving(0, FIRST, "leaving_first")
    leaving_second, _ = leaving(FIRST, SECOND, "leaving_second")
    first, second = (
        permute(piece, "replica", lambda i: (i + groups // 2) % groups)
        for piece in (leaving_first, leaving_second)
    )
    far_token = permute(long_tokens, "replica", lambda i: i ^ 1)

    places = jnp.concatenate(
        [
            lax.dynamic_slice_in_dim(lengths, group * 3, 3),
            lax.dynamic_slice_in_dim(long_lengths, group - parity, 2),
            jnp.zeros((3,), jnp.int32),
        ]
    ).astype(jnp.float32)
    inverse = np.float64(ROPE_BASE) ** (-2.0 * np.arange(64) / 128)
    inverse = jnp.asarray(np.concatenate([inverse, inverse]).astype(np.float32))
    sign = jnp.asarray(np.where(np.arange(128) < 64, -1.0, 1.0).astype(np.float32))
    angles = places[:, None] * inverse[None, :]
    cosine, sine = jnp.cos(angles), jnp.sin(angles) * sign

    out_shape = (
        jax.ShapeDtypeStruct((16, 256), jnp.float32),
        jax.ShapeDtypeStruct((16, 256), jnp.float32),
        jax.ShapeDtypeStruct((2, 128), jnp.float32),
        jax.ShapeDtypeStruct((ROWS, 2048), jnp.float32),
    )
    stored = (cache, long_cache, w_query, key_weight, value_weight)
    tables = (norm_gain, q_gain, k_gain, cosine, sine)

    def project_out(layer, state, side, after):
        far = permute(state, "replica", lambda i: i ^ 1)
        part = pl.pallas_call(
            functools.partial(out_kernel, layer),
            out_shape=jax.ShapeDtypeStruct((ROWS, 2048), jnp.float32),
            in_specs=[VM, VM, VM, ANY, ANY],
            out_specs=VM,
            scratch_shapes=[pltpu.VMEM((256, 2048), jnp.bfloat16), pltpu.SemaphoreType.DMA(())],
            compiler_params=params,
            name=f"out_projection_{layer}",
        )(state, far, side, w_out, after)
        part = (part + permute(part, "tensor", lambda i: i ^ 1)).astype(jnp.bfloat16)
        received = [permute(part, "tensor", lambda i, k=k: i ^ k) for k in (2, 4, 6)]
        return (part, *received)

    buffers = ((2048, 256), (2048, 128), (2048, 128)) + ((3, 2048, 128), (2, 2048, 128)) * 2

    def fetch(layer, which, after, name):
        return pl.pallas_call(
            functools.partial(fetch_kernel, layer, which),
            out_shape=tuple(pltpu.VMEM(buffers[i], jnp.bfloat16) for i in which),
            in_specs=[ANY] * 6,
            out_specs=(ANY,) * len(which),
            scratch_shapes=[pltpu.SemaphoreType.DMA((len(which),))],
            compiler_params=small,
            name=name,
        )(*map(in_hbm, stored), after)

    state, side, fresh_0, hidden = pl.pallas_call(
        first_kernel,
        out_shape=out_shape,
        in_specs=[SM] * 3 + [VM] * 13 + [ANY] * 2,
        out_specs=(VM,) * 4,
        scratch_shapes=[
            pltpu.VMEM((3, 2048, 128), jnp.bfloat16),
            pltpu.VMEM((2, 2048, 128), jnp.bfloat16),
            pltpu.SemaphoreType.DMA((2,)),
        ],
        compiler_params=params,
        name="attention_0",
    )(
        group_1, lengths, long_lengths, tokens, long_tokens, far_token, *tables,
        *fetch(0, (0, 1, 2, 3, 4), leaving_first, "fetch_0"), in_hbm(cache), in_hbm(long_cache),
    )
    resident = fetch(1, (0, 1, 2, 3, 4), state, "fetch_1_keys")
    terms = project_out(0, state, side, resident[1])
    resident = (*resident, *fetch(1, (5, 6), terms[0], "fetch_1_values"))
    state, side, fresh_1, hidden = pl.pallas_call(
        second_kernel,
        out_shape=out_shape,
        in_specs=[SM] * 3 + [VM] * 17,
        out_specs=(VM,) * 4,
        compiler_params=params,
        name="attention_1",
    )(group_1, lengths, long_lengths, hidden, *terms, *tables, *resident)
    terms = project_out(1, state, side, side)
    partner = (group + groups // 2) % groups
    arrived_len = lax.dynamic_slice_in_dim(lengths, partner * 3 + 2, 1)
    stored_first, blocks = pl.pallas_call(
        store_kernel,
        out_shape=(
            pltpu.HBM((2, 2, 2048, 128), jnp.bfloat16),
            pltpu.VMEM((4, 16, 128), jnp.bfloat16),
        ),
        in_specs=[SM, ANY, ANY],
        out_specs=(ANY, VM),
        scratch_shapes=[
            pltpu.VMEM((FIRST * UNIT, 128), jnp.bfloat16),
            pltpu.SemaphoreType.DMA((2, FIRST)),
        ],
        compiler_params=pltpu.CompilerParams(vmem_limit_bytes=4 * 2**20),
        name="store_first",
    )(arrived_len, in_hbm(first), terms[0])
    stay, long_out, leave = pl.pallas_call(
        final_kernel,
        out_shape=(
            jax.ShapeDtypeStruct((2, 2048), jnp.float32),
            jax.ShapeDtypeStruct((1, 2048), jnp.float32),
            jax.ShapeDtypeStruct((1, 2560), jnp.float32),
        ),
        in_specs=[SM] + [VM] * 7 + [ANY],
        out_specs=(VM,) * 3,
        scratch_shapes=[pltpu.VMEM((ROWS, 2048), jnp.float32)],
        compiler_params=params,
        name="final_rows",
    )(group_1, hidden, *terms, fresh_0, fresh_1, blocks)
    arrived = permute(leave, "replica", lambda i: (i + groups // 2) % groups)
    out_hidden, moved = pl.pallas_call(
        arrival_kernel,
        out_shape=(
            pltpu.HBM((3, 2048), jnp.float32),
            pltpu.HBM((2, 2, 2048, 128), jnp.bfloat16),
        ),
        in_specs=[SM, VM, VM, VM, VM, ANY],
        out_specs=(ANY, ANY),
        input_output_aliases={5: 1},
        scratch_shapes=[
            pltpu.VMEM((3, 2048), jnp.float32),
            pltpu.VMEM((4, 16, 128), jnp.bfloat16),
            pltpu.VMEM((4, UNIT, 128), jnp.bfloat16),
            pltpu.SemaphoreType.DMA((SECOND + 5,)),
        ],
        compiler_params=small,
        name="arrival",
    )(arrived_len, stay, arrived, blocks, in_vmem(second), stored_first)
    return (out_hidden, long_out, moved[None, :, :, :, None, :])


def solution(mesh):
    return jax.shard_map(
        local,
        mesh=mesh,
        in_specs=(
            P("replica", None),
            P("replica", None),
            P(None, None, "replica", None, "tensor", None),
            P(None, None, "replica", None, None, "tensor", None),
            P(),
            P(),
            P(),
            P(),
            P(),
            P(None, None, "tensor"),
            P(None, None, "tensor"),
            P(None, None, "tensor"),
            P(None, "tensor", None),
        ),
        out_specs=(
            P("replica", None),
            P("replica", None),
            P("replica", None, None, None, "tensor", None),
        ),
        check_vma=False,
    )
```

```python
import functools

import jax
import jax.numpy as jnp
import numpy as np
from jax import lax
from jax.experimental import pallas as pl
from jax.experimental.pallas import tpu as pltpu
from jax.sharding import PartitionSpec as P

EPSILON = 1e-06
ROPE_BASE = 1000000.0
NEGATIVE = -1e30
ROWS = 8
ANY = pl.BlockSpec(memory_space=pl.ANY)
VM = pl.BlockSpec(memory_space=pltpu.VMEM)
SM = pl.BlockSpec(memory_space=pltpu.SMEM)


def permute(value, axis, target):
    pairs = [(source, target(source)) for source in range(lax.axis_size(axis))]
    return lax.ppermute(value, axis, pairs)


def in_hbm(value):
    return pltpu.with_memory_space_constraint(value, pltpu.HBM)


def in_vmem(value):
    return pltpu.with_memory_space_constraint(value, pltpu.VMEM)


def row_of(count):
    return lax.broadcasted_iota(jnp.int32, (count, 1), 0)


def attention_step(
    layer, group_ref, lengths_ref, long_lengths_ref, hidden, gain_ref, q_gain_ref, k_gain_ref,
    cosine_ref, sine_ref, stored, state_ref, side_ref, fresh_ref, ready,
):
    wq, wk, wv, keys, long_keys, values, long_values = stored
    rows = hidden()
    scale = lax.rsqrt(jnp.mean(rows * rows, axis=-1, keepdims=True) + EPSILON)
    normed = (rows * scale * gain_ref[layer : layer + 1, :]).astype(jnp.bfloat16)
    ready(0, 1, 2)
    queries = jnp.dot(normed, wq[...], preferred_element_type=jnp.float32)
    new_keys = jnp.dot(normed, wk[...], preferred_element_type=jnp.float32)
    new_values = jnp.dot(normed, wv[...], preferred_element_type=jnp.float32).astype(jnp.bfloat16)

    def finish(heads, gain, cosine, sine):
        heads = heads * lax.rsqrt(jnp.mean(heads * heads, axis=-1, keepdims=True) + EPSILON) * gain
        return (heads * cosine + pltpu.roll(heads, 64, 1) * sine).astype(jnp.bfloat16)

    cosine, sine = cosine_ref[...], sine_ref[...]
    q_gain = q_gain_ref[layer : layer + 1, :]
    q0 = finish(queries[:, :128], q_gain, cosine, sine).astype(jnp.float32)
    q1 = finish(queries[:, 128:], q_gain, cosine, sine).astype(jnp.float32)
    key_new = finish(new_keys, k_gain_ref[layer : layer + 1, :], cosine, sine).astype(jnp.float32)
    value_new = new_values.astype(jnp.float32)
    fresh_ref[0:1, :] = key_new[2:3, :]
    fresh_ref[1:2, :] = value_new[2:3, :]
    both = jnp.concatenate([q0, q1], axis=0)
    query = both.astype(jnp.bfloat16)
    keys_twice = jnp.concatenate([key_new, key_new], axis=0)
    values_twice = jnp.concatenate([value_new, value_new], axis=0)
    factor = 128 ** (-0.5)
    own = jnp.sum(both * keys_twice, axis=-1, keepdims=True) * factor

    group = group_ref[0]
    parity = lax.rem(group, 2)
    which = lax.rem(row_of(16), 8)
    limit = jnp.ones((16, 1), jnp.int32)
    for r in range(3):
        limit = jnp.where(which == r, lengths_ref[group * 3 + r], limit)
    for r in range(2):
        limit = jnp.where(
            which == 3 + r, long_lengths_ref[group - parity + r] - parity * 2048, limit
        )
    scores = jnp.zeros((16, 2048), jnp.float32)
    for r in range(5):
        if r == 0:
            ready(3)
        if r == 3:
            ready(4)
        block = keys[r] if r < 3 else long_keys[r - 3]
        product = lax.dot_general(
            query, block, (((1,), (1,)), ((), ())), preferred_element_type=jnp.float32
        )
        scores = jnp.where(which == r, product, scores)
    places = lax.broadcasted_iota(jnp.int32, (16, 2048), 1)
    scores = jnp.where(places < limit, scores * factor, NEGATIVE)
    is_main = which < 3
    highest = jnp.max(scores, axis=-1, keepdims=True)
    highest = jnp.where(is_main, jnp.maximum(highest, own), highest)
    weights = jnp.exp(scores - highest)
    own_weight = jnp.where(is_main, jnp.exp(own - highest), 0.0)
    total = jnp.sum(weights, axis=-1, keepdims=True) + own_weight
    rounded = weights.astype(jnp.bfloat16)
    summed = own_weight.astype(jnp.bfloat16).astype(jnp.float32) * values_twice
    for r in range(5):
        if r == 0:
            ready(5)
        if r == 3:
            ready(6)
        block = values[r] if r < 3 else long_values[r - 3]
        product = jnp.dot(rounded, block, preferred_element_type=jnp.float32)
        summed = summed + jnp.where(which == r, product, 0.0)
    state_ref[:, 0:128] = summed
    lanes = lax.broadcasted_iota(jnp.int32, (16, 128), 1)
    state_ref[:, 128:256] = jnp.where(lanes < 64, highest, total)
    side_ref[:, 0:128] = jnp.broadcast_to(own, (16, 128))
    side_ref[:, 128:256] = values_twice


def parts_of(layer, cache_ref, long_ref, wq_ref, wk_ref, wv_ref):
    return (
        wq_ref.at[layer], wk_ref.at[layer], wv_ref.at[layer],
        cache_ref.at[layer, 0], long_ref.at[layer, 0, 0],
        cache_ref.at[layer, 1], long_ref.at[layer, 1, 0],
    )


def first_kernel(
    group_ref, lengths_ref, long_lengths_ref, tokens_ref, own_long_ref, far_long_ref, *rest
):
    tables, resident, held = rest[:5], rest[5:10], rest[10:12]
    state_ref, side_ref, fresh_ref, hidden_ref = rest[12:16]
    buffers, semaphores = rest[16:18], rest[18]
    sources = (held[0].at[0, 1], held[1].at[0, 1, 0])
    copies = [
        pltpu.make_async_copy(source, target, semaphores.at[i])
        for i, (source, target) in enumerate(zip(sources, buffers))
    ]
    for copy in copies:
        copy.start()

    def ready(*which):
        for i in which:
            if i >= 5:
                copies[i - 5].wait()

    def hidden():
        own = own_long_ref[...].astype(jnp.float32)
        far = far_long_ref[...].astype(jnp.float32)
        even = lax.rem(group_ref[0], 2) == 0
        hidden_ref[...] = jnp.zeros((ROWS, 2048), jnp.float32)
        hidden_ref[0:3, :] = tokens_ref[...].astype(jnp.float32)
        hidden_ref[3:4, :] = jnp.where(even, own, far)
        hidden_ref[4:5, :] = jnp.where(even, far, own)
        return hidden_ref[...]

    attention_step(
        0, group_ref, lengths_ref, long_lengths_ref, hidden, *tables, (*resident, *buffers),
        state_ref, side_ref, fresh_ref, ready,
    )


def total_of(p_ref, r1_ref, r2_ref, r3_ref):
    p, r1, r2, r3 = (ref[...].astype(jnp.float32) for ref in (p_ref, r1_ref, r2_ref, r3_ref))
    return (p + r1) + (r2 + r3)


def second_kernel(
    group_ref, lengths_ref, long_lengths_ref, before_ref, p_ref, r1_ref, r2_ref, r3_ref, *rest
):
    tables, stored = rest[:5], rest[5:12]
    state_ref, side_ref, fresh_ref, hidden_ref = rest[12:16]

    def hidden():
        summed = total_of(p_ref, r1_ref, r2_ref, r3_ref)
        rows = (before_ref[...] + summed).astype(jnp.bfloat16).astype(jnp.float32)
        hidden_ref[...] = rows
        return rows

    attention_step(
        1, group_ref, lengths_ref, long_lengths_ref, hidden, *tables, stored,
        state_ref, side_ref, fresh_ref, lambda *which: None,
    )


UNIT = 256
HEAD = 6
FIRST = 24
PER = 2048 // UNIT
SECOND = 4 * PER - FIRST


def plane_of(unit):
    return unit // (2 * PER), unit // PER % 2, pl.ds(unit % PER * UNIT, UNIT)


def runs(begin, end):
    out, at = [], begin
    while at < end:
        stop = min(end, at // PER * PER + PER)
        i, j, _ = plane_of(at)
        out.append((i, j, at % PER * UNIT, (stop - at) * UNIT, (at - begin) * UNIT))
        at = stop
    return out


def leaving_kernel(begin, end, cache_ref, out_ref, unused_ref, semaphores):
    del unused_ref
    copies = []
    for n, (i, j, place, size, at) in enumerate(runs(begin, end)):
        copies.append(
            pltpu.make_async_copy(
                cache_ref.at[i, j, 2, pl.ds(place, size)], out_ref.at[pl.ds(at, size)],
                semaphores.at[n],
            )
        )
    for copy in copies:
        copy.start()
    for copy in copies:
        copy.wait()


def store_kernel(length_ref, head_ref, first_ref, after_ref, stored_ref, blocks_ref, buffer, semaphores):
    del after_ref
    reads, writes = [], []
    for n in range(FIRST):
        i, j, rows = plane_of(n)
        piece = pl.ds(n * UNIT, UNIT)
        ref, at = (head_ref, n) if n < HEAD else (first_ref, n - HEAD)
        reads.append(
            pltpu.make_async_copy(
                ref.at[pl.ds(at * UNIT, UNIT)], buffer.at[piece], semaphores.at[0, n]
            )
        )
        writes.append(
            pltpu.make_async_copy(buffer.at[piece], stored_ref.at[i, j, rows], semaphores.at[1, n])
        )
    for copy in reads:
        copy.start()
    for read, write in zip(reads, writes):
        read.wait()
        write.start()
    start = length_ref[0] // 16 * 16
    for plane in range(4):
        at = jnp.minimum(plane * 2048 + start, FIRST * UNIT - 16)
        blocks_ref[plane] = buffer[pl.ds(pl.multiple_of(at, 16), 16), :]
    for copy in writes:
        copy.wait()


def arrival_kernel(
    length_ref, stay_ref, arrived_ref, blocks_ref, second_ref, stored_ref, out_ref, moved_ref,
    rows, blocks, patched, semaphores,
):
    del stored_ref
    length = length_ref[0]
    hit_unit = length // UNIT
    units = [(unit, *plane_of(unit)) for unit in range(FIRST, 4 * PER)]

    def straight(unit, i, j, place):
        return pltpu.make_async_copy(
            second_ref.at[pl.ds((unit - FIRST) * UNIT, UNIT)], moved_ref.at[i, j, place],
            semaphores.at[unit - FIRST],
        )

    def changed(unit, i, j, place):
        return pltpu.make_async_copy(
            patched.at[unit // PER], moved_ref.at[i, j, place], semaphores.at[unit - FIRST]
        )

    for unit in units:

        @pl.when(hit_unit != unit[0] % PER)
        def _():
            straight(*unit).start()

    fresh = [arrived_ref[0:1, 2048 + 128 * n : 2176 + 128 * n] for n in range(4)]
    start = pl.multiple_of(length // 16 * 16, 16)
    early = []
    for plane in range((FIRST + PER - 1) // PER):
        block = blocks_ref[plane].astype(jnp.float32)
        blocks[plane] = jnp.where(row_of(16) == length - start, fresh[plane], block).astype(
            jnp.bfloat16
        )
        write = pltpu.make_async_copy(
            blocks.at[plane], moved_ref.at[plane // 2, plane % 2, pl.ds(start, 16)],
            semaphores.at[SECOND + plane],
        )
        early.append((plane * PER + hit_unit < FIRST, write))
    for inside, write in early:
        pl.when(inside)(write.start)
    for plane in range(FIRST // PER, 4):
        at = jnp.maximum(plane * PER + hit_unit - FIRST, 0) * UNIT
        whole = second_ref[pl.ds(pl.multiple_of(at, UNIT), UNIT), :].astype(jnp.float32)
        patched[plane] = jnp.where(
            row_of(UNIT) == length - hit_unit * UNIT, fresh[plane], whole
        ).astype(jnp.bfloat16)
    for unit in units:

        @pl.when(hit_unit == unit[0] % PER)
        def _():
            changed(*unit).start()

    rows[0:2, :] = stay_ref[...]
    rows[2:3, :] = arrived_ref[0:1, 0:2048]
    out = pltpu.make_async_copy(rows, out_ref, semaphores.at[SECOND + 4])
    out.start()
    for unit in units:
        straight(*unit).wait()
    for inside, write in early:
        pl.when(inside)(write.wait)
    out.wait()


def fetch_kernel(layer, which, *refs):
    held, outputs, semaphores = refs[:5], refs[6 : 6 + len(which)], refs[-1]
    sources = parts_of(layer, *held)
    copies = [
        pltpu.make_async_copy(sources[i], output, semaphores.at[n])
        for n, (i, output) in enumerate(zip(which, outputs))
    ]
    for copy in copies:
        copy.start()
    for copy in copies:
        copy.wait()


def out_kernel(
    layer, state_ref, far_ref, side_ref, w_ref, after_ref, also_after_ref, out_ref, w, semaphore
):
    del after_ref, also_after_ref
    copy = pltpu.make_async_copy(w_ref.at[layer], w, semaphore)
    copy.start()
    is_main = lax.rem(row_of(16), 8) < 3
    here, far = state_ref[...], far_ref[...]
    m_here, l_here, acc_here = here[:, 128:129], here[:, 192:193], here[:, :128]
    m_far, l_far, acc_far = far[:, 128:129], far[:, 192:193], far[:, :128]
    own, value = side_ref[:, 0:1], side_ref[:, 128:256]
    highest = jnp.maximum(jnp.maximum(m_here, m_far), own)
    f_here, f_far = jnp.exp(m_here - highest), jnp.exp(m_far - highest)
    own_weight = jnp.exp(own - highest)
    total = (l_here * f_here + l_far * f_far) + own_weight
    own_rounded = own_weight.astype(jnp.bfloat16).astype(jnp.float32)
    summed = (acc_here * f_here + acc_far * f_far) + own_rounded * value
    total = jnp.where(is_main, l_here, total)
    summed = jnp.where(is_main, acc_here, summed)
    attended = summed / total
    attended = jnp.concatenate([attended[:8], attended[8:]], axis=1).astype(jnp.bfloat16)
    copy.wait()
    out_ref[...] = jnp.dot(attended, w[...], preferred_element_type=jnp.float32)


def final_kernel(
    group_ref, before_ref, p_ref, r1_ref, r2_ref, r3_ref, fresh0_ref, fresh1_ref, after_ref,
    stay_ref, long_ref, leave_ref, scratch,
):
    del after_ref
    scratch[...] = before_ref[...] + total_of(p_ref, r1_ref, r2_ref, r3_ref)
    stay_ref[...] = scratch[0:2, :]
    odd = lax.rem(group_ref[0], 2) == 1
    long_ref[...] = jnp.where(odd, scratch[4:5, :], scratch[3:4, :])
    leave_ref[0:1, 0:2048] = scratch[2:3, :]
    for i, ref in enumerate((fresh0_ref, fresh1_ref)):
        for j in range(2):
            leave_ref[0:1, 2048 + 128 * (2 * i + j) : 2176 + 128 * (2 * i + j)] = ref[j : j + 1, :]


def local(
    tokens, long_tokens, cache, long_cache, lengths, long_lengths, norm_gain, q_gain, k_gain,
    w_query, key_weight, value_weight, w_out,
):
    groups = lax.axis_size("replica")
    group = lax.axis_index("replica")
    parity = group % 2
    group_1 = group[None]
    cache = cache.reshape(2, 2, 3, 2048, 128)
    long_cache = long_cache.reshape(2, 2, 1, 2, 2048, 128)

    params = pltpu.CompilerParams(vmem_limit_bytes=16 * 2**20)
    small = pltpu.CompilerParams(vmem_limit_bytes=2 * 2**20)
    held = in_hbm(cache)

    def leaving(begin, count, name):
        return pl.pallas_call(
            functools.partial(leaving_kernel, begin, begin + count),
            out_shape=(
                pltpu.VMEM((count * UNIT, 128), jnp.bfloat16),
                pltpu.VMEM((8, 128), jnp.float32),
            ),
            in_specs=[ANY],
            out_specs=(ANY, ANY),
            scratch_shapes=[pltpu.SemaphoreType.DMA((4,))],
            compiler_params=small,
            name=name,
        )(held)

    leaving_head, _ = leaving(0, HEAD, "leaving_head")
    leaving_first, _ = leaving(HEAD, FIRST - HEAD, "leaving_first")
    leaving_second, _ = leaving(FIRST, SECOND, "leaving_second")
    head, first, second = (
        permute(piece, "replica", lambda i: (i + groups // 2) % groups)
        for piece in (leaving_head, leaving_first, leaving_second)
    )
    far_token = permute(long_tokens, "replica", lambda i: i ^ 1)

    places = jnp.concatenate(
        [
            lax.dynamic_slice_in_dim(lengths, group * 3, 3),
            lax.dynamic_slice_in_dim(long_lengths, group - parity, 2),
            jnp.zeros((3,), jnp.int32),
        ]
    ).astype(jnp.float32)
    inverse = np.float64(ROPE_BASE) ** (-2.0 * np.arange(64) / 128)
    inverse = jnp.asarray(np.concatenate([inverse, inverse]).astype(np.float32))
    sign = jnp.asarray(np.where(np.arange(128) < 64, -1.0, 1.0).astype(np.float32))
    angles = places[:, None] * inverse[None, :]
    cosine, sine = jnp.cos(angles), jnp.sin(angles) * sign

    out_shape = (
        jax.ShapeDtypeStruct((16, 256), jnp.float32),
        jax.ShapeDtypeStruct((16, 256), jnp.float32),
        jax.ShapeDtypeStruct((2, 128), jnp.float32),
        jax.ShapeDtypeStruct((ROWS, 2048), jnp.float32),
    )
    stored = (cache, long_cache, w_query, key_weight, value_weight)
    tables = (norm_gain, q_gain, k_gain, cosine, sine)

    def project_out(layer, state, side, *after):
        far = permute(state, "replica", lambda i: i ^ 1)
        part = pl.pallas_call(
            functools.partial(out_kernel, layer),
            out_shape=jax.ShapeDtypeStruct((ROWS, 2048), jnp.float32),
            in_specs=[VM, VM, VM, ANY, ANY, ANY],
            out_specs=VM,
            scratch_shapes=[pltpu.VMEM((256, 2048), jnp.bfloat16), pltpu.SemaphoreType.DMA(())],
            compiler_params=params,
            name=f"out_projection_{layer}",
        )(state, far, side, w_out, *after)
        part = (part + permute(part, "tensor", lambda i: i ^ 1)).astype(jnp.bfloat16)
        received = [permute(part, "tensor", lambda i, k=k: i ^ k) for k in (2, 4, 6)]
        return (part, *received)

    buffers = ((2048, 256), (2048, 128), (2048, 128)) + ((3, 2048, 128), (2, 2048, 128)) * 2

    def fetch(layer, which, after, name):
        return pl.pallas_call(
            functools.partial(fetch_kernel, layer, which),
            out_shape=tuple(pltpu.VMEM(buffers[i], jnp.bfloat16) for i in which),
            in_specs=[ANY] * 6,
            out_specs=(ANY,) * len(which),
            scratch_shapes=[pltpu.SemaphoreType.DMA((len(which),))],
            compiler_params=small,
            name=name,
        )(*map(in_hbm, stored), after)

    state, side, fresh_0, hidden = pl.pallas_call(
        first_kernel,
        out_shape=out_shape,
        in_specs=[SM] * 3 + [VM] * 13 + [ANY] * 2,
        out_specs=(VM,) * 4,
        scratch_shapes=[
            pltpu.VMEM((3, 2048, 128), jnp.bfloat16),
            pltpu.VMEM((2, 2048, 128), jnp.bfloat16),
            pltpu.SemaphoreType.DMA((2,)),
        ],
        compiler_params=params,
        name="attention_0",
    )(
        group_1, lengths, long_lengths, tokens, long_tokens, far_token, *tables,
        *fetch(0, (0, 1, 2, 3, 4), leaving_first, "fetch_0"), in_hbm(cache), in_hbm(long_cache),
    )
    resident = fetch(1, (0, 1, 2, 3, 4), state, "fetch_1_keys")
    terms = project_out(0, state, side, resident[1], head)
    resident = (*resident, *fetch(1, (5, 6), terms[0], "fetch_1_values"))
    state, side, fresh_1, hidden = pl.pallas_call(
        second_kernel,
        out_shape=out_shape,
        in_specs=[SM] * 3 + [VM] * 17,
        out_specs=(VM,) * 4,
        compiler_params=params,
        name="attention_1",
    )(group_1, lengths, long_lengths, hidden, *terms, *tables, *resident)
    terms = project_out(1, state, side, side, side)
    partner = (group + groups // 2) % groups
    arrived_len = lax.dynamic_slice_in_dim(lengths, partner * 3 + 2, 1)
    stored_first, blocks = pl.pallas_call(
        store_kernel,
        out_shape=(
            pltpu.HBM((2, 2, 2048, 128), jnp.bfloat16),
            pltpu.VMEM((4, 16, 128), jnp.bfloat16),
        ),
        in_specs=[SM, ANY, ANY, ANY],
        out_specs=(ANY, VM),
        scratch_shapes=[
            pltpu.VMEM((FIRST * UNIT, 128), jnp.bfloat16),
            pltpu.SemaphoreType.DMA((2, FIRST)),
        ],
        compiler_params=pltpu.CompilerParams(vmem_limit_bytes=4 * 2**20),
        name="store_first",
    )(arrived_len, head, in_hbm(first), terms[0])
    stay, long_out, leave = pl.pallas_call(
        final_kernel,
        out_shape=(
            jax.ShapeDtypeStruct((2, 2048), jnp.float32),
            jax.ShapeDtypeStruct((1, 2048), jnp.float32),
            jax.ShapeDtypeStruct((1, 2560), jnp.float32),
        ),
        in_specs=[SM] + [VM] * 7 + [ANY],
        out_specs=(VM,) * 3,
        scratch_shapes=[pltpu.VMEM((ROWS, 2048), jnp.float32)],
        compiler_params=params,
        name="final_rows",
    )(group_1, hidden, *terms, fresh_0, fresh_1, blocks)
    arrived = permute(leave, "replica", lambda i: (i + groups // 2) % groups)
    out_hidden, moved = pl.pallas_call(
        arrival_kernel,
        out_shape=(
            pltpu.HBM((3, 2048), jnp.float32),
            pltpu.HBM((2, 2, 2048, 128), jnp.bfloat16),
        ),
        in_specs=[SM, VM, VM, VM, VM, ANY],
        out_specs=(ANY, ANY),
        input_output_aliases={5: 1},
        scratch_shapes=[
            pltpu.VMEM((3, 2048), jnp.float32),
            pltpu.VMEM((4, 16, 128), jnp.bfloat16),
            pltpu.VMEM((4, UNIT, 128), jnp.bfloat16),
            pltpu.SemaphoreType.DMA((SECOND + 5,)),
        ],
        compiler_params=small,
        name="arrival",
    )(arrived_len, stay, arrived, blocks, in_vmem(second), stored_first)
    return (out_hidden, long_out, moved[None, :, :, :, None, :])


def solution(mesh):
    return jax.shard_map(
        local,
        mesh=mesh,
        in_specs=(
            P("replica", None),
            P("replica", None),
            P(None, None, "replica", None, "tensor", None),
            P(None, None, "replica", None, None, "tensor", None),
            P(),
            P(),
            P(),
            P(),
            P(),
            P(None, None, "tensor"),
            P(None, None, "tensor"),
            P(None, None, "tensor"),
            P(None, "tensor", None),
        ),
        out_specs=(
            P("replica", None),
            P("replica", None),
            P("replica", None, None, None, "tensor", None),
        ),
        check_vma=False,
    )
```

```python
import functools

import jax
import jax.numpy as jnp
import numpy as np
from jax import lax
from jax.experimental import pallas as pl
from jax.experimental.pallas import tpu as pltpu
from jax.sharding import PartitionSpec as P

EPSILON = 1e-06
ROPE_BASE = 1000000.0
NEGATIVE = -1e30
ROWS = 8
ANY = pl.BlockSpec(memory_space=pl.ANY)
VM = pl.BlockSpec(memory_space=pltpu.VMEM)
SM = pl.BlockSpec(memory_space=pltpu.SMEM)


def permute(value, axis, target):
    pairs = [(source, target(source)) for source in range(lax.axis_size(axis))]
    return lax.ppermute(value, axis, pairs)


def in_hbm(value):
    return pltpu.with_memory_space_constraint(value, pltpu.HBM)


def in_vmem(value):
    return pltpu.with_memory_space_constraint(value, pltpu.VMEM)


def row_of(count):
    return lax.broadcasted_iota(jnp.int32, (count, 1), 0)


def attention_step(
    layer, group_ref, lengths_ref, long_lengths_ref, hidden, gain_ref, q_gain_ref, k_gain_ref,
    cosine_ref, sine_ref, stored, state_ref, side_ref, fresh_ref, ready,
):
    wq, wk, wv, keys, long_keys, values, long_values = stored
    rows = hidden()
    scale = lax.rsqrt(jnp.mean(rows * rows, axis=-1, keepdims=True) + EPSILON)
    normed = (rows * scale * gain_ref[layer : layer + 1, :]).astype(jnp.bfloat16)
    ready(0, 1, 2)
    queries = jnp.dot(normed, wq[...], preferred_element_type=jnp.float32)
    new_keys = jnp.dot(normed, wk[...], preferred_element_type=jnp.float32)
    new_values = jnp.dot(normed, wv[...], preferred_element_type=jnp.float32).astype(jnp.bfloat16)

    def finish(heads, gain, cosine, sine):
        heads = heads * lax.rsqrt(jnp.mean(heads * heads, axis=-1, keepdims=True) + EPSILON) * gain
        return (heads * cosine + pltpu.roll(heads, 64, 1) * sine).astype(jnp.bfloat16)

    cosine, sine = cosine_ref[...], sine_ref[...]
    q_gain = q_gain_ref[layer : layer + 1, :]
    q0 = finish(queries[:, :128], q_gain, cosine, sine).astype(jnp.float32)
    q1 = finish(queries[:, 128:], q_gain, cosine, sine).astype(jnp.float32)
    key_new = finish(new_keys, k_gain_ref[layer : layer + 1, :], cosine, sine).astype(jnp.float32)
    value_new = new_values.astype(jnp.float32)
    fresh_ref[0:1, :] = key_new[2:3, :]
    fresh_ref[1:2, :] = value_new[2:3, :]
    both = jnp.concatenate([q0, q1], axis=0)
    query = both.astype(jnp.bfloat16)
    keys_twice = jnp.concatenate([key_new, key_new], axis=0)
    values_twice = jnp.concatenate([value_new, value_new], axis=0)
    factor = 128 ** (-0.5)
    own = jnp.sum(both * keys_twice, axis=-1, keepdims=True) * factor

    group = group_ref[0]
    parity = lax.rem(group, 2)
    which = lax.rem(row_of(16), 8)
    limit = jnp.ones((16, 1), jnp.int32)
    for r in range(3):
        limit = jnp.where(which == r, lengths_ref[group * 3 + r], limit)
    for r in range(2):
        limit = jnp.where(
            which == 3 + r, long_lengths_ref[group - parity + r] - parity * 2048, limit
        )
    scores = jnp.zeros((16, 2048), jnp.float32)
    for r in range(5):
        if r == 0:
            ready(3)
        if r == 3:
            ready(4)
        block = keys[r] if r < 3 else long_keys[r - 3]
        product = lax.dot_general(
            query, block, (((1,), (1,)), ((), ())), preferred_element_type=jnp.float32
        )
        scores = jnp.where(which == r, product, scores)
    places = lax.broadcasted_iota(jnp.int32, (16, 2048), 1)
    scores = jnp.where(places < limit, scores * factor, NEGATIVE)
    is_main = which < 3
    highest = jnp.max(scores, axis=-1, keepdims=True)
    highest = jnp.where(is_main, jnp.maximum(highest, own), highest)
    weights = jnp.exp(scores - highest)
    own_weight = jnp.where(is_main, jnp.exp(own - highest), 0.0)
    total = jnp.sum(weights, axis=-1, keepdims=True) + own_weight
    rounded = weights.astype(jnp.bfloat16)
    summed = own_weight.astype(jnp.bfloat16).astype(jnp.float32) * values_twice
    for r in range(5):
        if r == 0:
            ready(5)
        if r == 3:
            ready(6)
        block = values[r] if r < 3 else long_values[r - 3]
        product = jnp.dot(rounded, block, preferred_element_type=jnp.float32)
        summed = summed + jnp.where(which == r, product, 0.0)
    state_ref[:, 0:128] = summed
    lanes = lax.broadcasted_iota(jnp.int32, (16, 128), 1)
    state_ref[:, 128:256] = jnp.where(lanes < 64, highest, total)
    side_ref[:, 0:128] = jnp.broadcast_to(own, (16, 128))
    side_ref[:, 128:256] = values_twice


def parts_of(layer, cache_ref, long_ref, wq_ref, wk_ref, wv_ref):
    return (
        wq_ref.at[layer], wk_ref.at[layer], wv_ref.at[layer],
        cache_ref.at[layer, 0], long_ref.at[layer, 0, 0],
        cache_ref.at[layer, 1], long_ref.at[layer, 1, 0],
    )


def first_kernel(
    group_ref, lengths_ref, long_lengths_ref, tokens_ref, own_long_ref, far_long_ref, *rest
):
    tables, resident, held = rest[:5], rest[5:10], rest[10:12]
    state_ref, side_ref, fresh_ref, hidden_ref = rest[12:16]
    buffers, semaphores = rest[16:18], rest[18]
    sources = (held[0].at[0, 1], held[1].at[0, 1, 0])
    copies = [
        pltpu.make_async_copy(source, target, semaphores.at[i])
        for i, (source, target) in enumerate(zip(sources, buffers))
    ]
    for copy in copies:
        copy.start()

    def ready(*which):
        for i in which:
            if i >= 5:
                copies[i - 5].wait()

    def hidden():
        own = own_long_ref[...].astype(jnp.float32)
        far = far_long_ref[...].astype(jnp.float32)
        even = lax.rem(group_ref[0], 2) == 0
        hidden_ref[...] = jnp.zeros((ROWS, 2048), jnp.float32)
        hidden_ref[0:3, :] = tokens_ref[...].astype(jnp.float32)
        hidden_ref[3:4, :] = jnp.where(even, own, far)
        hidden_ref[4:5, :] = jnp.where(even, far, own)
        return hidden_ref[...]

    attention_step(
        0, group_ref, lengths_ref, long_lengths_ref, hidden, *tables, (*resident, *buffers),
        state_ref, side_ref, fresh_ref, ready,
    )


def total_of(p_ref, r1_ref, r2_ref, r3_ref):
    p, r1, r2, r3 = (ref[...].astype(jnp.float32) for ref in (p_ref, r1_ref, r2_ref, r3_ref))
    return (p + r1) + (r2 + r3)


def second_kernel(
    group_ref, lengths_ref, long_lengths_ref, before_ref, p_ref, r1_ref, r2_ref, r3_ref, *rest
):
    tables, stored = rest[:5], rest[5:12]
    state_ref, side_ref, fresh_ref, hidden_ref = rest[12:16]

    def hidden():
        summed = total_of(p_ref, r1_ref, r2_ref, r3_ref)
        rows = (before_ref[...] + summed).astype(jnp.bfloat16).astype(jnp.float32)
        hidden_ref[...] = rows
        return rows

    attention_step(
        1, group_ref, lengths_ref, long_lengths_ref, hidden, *tables, stored,
        state_ref, side_ref, fresh_ref, lambda *which: None,
    )


UNIT = 256
FIRST = 23
PER = 2048 // UNIT
SECOND = 4 * PER - FIRST


def plane_of(unit):
    return unit // (2 * PER), unit // PER % 2, pl.ds(unit % PER * UNIT, UNIT)


def runs(begin, end):
    out, at = [], begin
    while at < end:
        stop = min(end, at // PER * PER + PER)
        i, j, _ = plane_of(at)
        out.append((i, j, at % PER * UNIT, (stop - at) * UNIT, (at - begin) * UNIT))
        at = stop
    return out


def leaving_kernel(begin, end, cache_ref, out_ref, unused_ref, semaphores):
    del unused_ref
    copies = []
    for n, (i, j, place, size, at) in enumerate(runs(begin, end)):
        copies.append(
            pltpu.make_async_copy(
                cache_ref.at[i, j, 2, pl.ds(place, size)], out_ref.at[pl.ds(at, size)],
                semaphores.at[n],
            )
        )
    for copy in copies:
        copy.start()
    for copy in copies:
        copy.wait()


def store_kernel(
    length_ref, first_ref, after_ref, stored_ref, blocks_ref, place_ref, buffer, semaphores
):
    del after_ref
    place_ref[...] = jnp.full((8, 128), length_ref[0].astype(jnp.float32))
    reads, writes = [], []
    for n in range(FIRST):
        i, j, rows = plane_of(n)
        piece = pl.ds(n * UNIT, UNIT)
        reads.append(
            pltpu.make_async_copy(first_ref.at[piece], buffer.at[piece], semaphores.at[0, n])
        )
        writes.append(
            pltpu.make_async_copy(buffer.at[piece], stored_ref.at[i, j, rows], semaphores.at[1, n])
        )
    for copy in reads:
        copy.start()
    for read, write in zip(reads, writes):
        read.wait()
        write.start()
    start = length_ref[0] // 16 * 16
    for plane in range(4):
        at = jnp.minimum(plane * 2048 + start, FIRST * UNIT - 16)
        blocks_ref[plane] = buffer[pl.ds(pl.multiple_of(at, 16), 16), :]
    for copy in writes:
        copy.wait()


def arrival_kernel(
    place_ref, stay_ref, arrived_ref, blocks_ref, second_ref, stored_ref, out_ref, moved_ref,
    rows, blocks, patched, semaphores,
):
    del stored_ref
    length = jnp.max(place_ref[...]).astype(jnp.int32)
    hit_unit = length // UNIT
    units = [(unit, *plane_of(unit)) for unit in range(FIRST, 4 * PER)]

    def straight(unit, i, j, place):
        return pltpu.make_async_copy(
            second_ref.at[pl.ds((unit - FIRST) * UNIT, UNIT)], moved_ref.at[i, j, place],
            semaphores.at[unit - FIRST],
        )

    def changed(unit, i, j, place):
        return pltpu.make_async_copy(
            patched.at[unit // PER], moved_ref.at[i, j, place], semaphores.at[unit - FIRST]
        )

    for unit in units:

        @pl.when(hit_unit != unit[0] % PER)
        def _():
            straight(*unit).start()

    fresh = [arrived_ref[0:1, 2048 + 128 * n : 2176 + 128 * n] for n in range(4)]
    start = pl.multiple_of(length // 16 * 16, 16)
    early = []
    for plane in range((FIRST + PER - 1) // PER):
        block = blocks_ref[plane].astype(jnp.float32)
        blocks[plane] = jnp.where(row_of(16) == length - start, fresh[plane], block).astype(
            jnp.bfloat16
        )
        write = pltpu.make_async_copy(
            blocks.at[plane], moved_ref.at[plane // 2, plane % 2, pl.ds(start, 16)],
            semaphores.at[SECOND + plane],
        )
        early.append((plane * PER + hit_unit < FIRST, write))
    for inside, write in early:
        pl.when(inside)(write.start)
    for plane in range(FIRST // PER, 4):
        at = jnp.maximum(plane * PER + hit_unit - FIRST, 0) * UNIT
        whole = second_ref[pl.ds(pl.multiple_of(at, UNIT), UNIT), :].astype(jnp.float32)
        patched[plane] = jnp.where(
            row_of(UNIT) == length - hit_unit * UNIT, fresh[plane], whole
        ).astype(jnp.bfloat16)
    for unit in units:

        @pl.when(hit_unit == unit[0] % PER)
        def _():
            changed(*unit).start()

    rows[0:2, :] = stay_ref[...]
    rows[2:3, :] = arrived_ref[0:1, 0:2048]
    out = pltpu.make_async_copy(rows, out_ref, semaphores.at[SECOND + 4])
    out.start()
    for unit in units:
        straight(*unit).wait()
    for inside, write in early:
        pl.when(inside)(write.wait)
    out.wait()


def fetch_kernel(layer, which, *refs):
    held, outputs, semaphores = refs[:5], refs[6 : 6 + len(which)], refs[-1]
    sources = parts_of(layer, *held)
    copies = [
        pltpu.make_async_copy(sources[i], output, semaphores.at[n])
        for n, (i, output) in enumerate(zip(which, outputs))
    ]
    for copy in copies:
        copy.start()
    for copy in copies:
        copy.wait()


def out_kernel(layer, state_ref, far_ref, side_ref, w_ref, after_ref, out_ref, w, semaphore):
    del after_ref
    copy = pltpu.make_async_copy(w_ref.at[layer], w, semaphore)
    copy.start()
    is_main = lax.rem(row_of(16), 8) < 3
    here, far = state_ref[...], far_ref[...]
    m_here, l_here, acc_here = here[:, 128:129], here[:, 192:193], here[:, :128]
    m_far, l_far, acc_far = far[:, 128:129], far[:, 192:193], far[:, :128]
    own, value = side_ref[:, 0:1], side_ref[:, 128:256]
    highest = jnp.maximum(jnp.maximum(m_here, m_far), own)
    f_here, f_far = jnp.exp(m_here - highest), jnp.exp(m_far - highest)
    own_weight = jnp.exp(own - highest)
    total = (l_here * f_here + l_far * f_far) + own_weight
    own_rounded = own_weight.astype(jnp.bfloat16).astype(jnp.float32)
    summed = (acc_here * f_here + acc_far * f_far) + own_rounded * value
    total = jnp.where(is_main, l_here, total)
    summed = jnp.where(is_main, acc_here, summed)
    attended = summed / total
    attended = jnp.concatenate([attended[:8], attended[8:]], axis=1).astype(jnp.bfloat16)
    copy.wait()
    out_ref[...] = jnp.dot(attended, w[...], preferred_element_type=jnp.float32)


def final_kernel(
    group_ref, before_ref, p_ref, r1_ref, r2_ref, r3_ref, fresh0_ref, fresh1_ref, after_ref,
    stay_ref, long_ref, leave_ref, scratch,
):
    del after_ref
    scratch[...] = before_ref[...] + total_of(p_ref, r1_ref, r2_ref, r3_ref)
    stay_ref[...] = scratch[0:2, :]
    odd = lax.rem(group_ref[0], 2) == 1
    long_ref[...] = jnp.where(odd, scratch[4:5, :], scratch[3:4, :])
    leave_ref[0:1, 0:2048] = scratch[2:3, :]
    for i, ref in enumerate((fresh0_ref, fresh1_ref)):
        for j in range(2):
            leave_ref[0:1, 2048 + 128 * (2 * i + j) : 2176 + 128 * (2 * i + j)] = ref[j : j + 1, :]


def local(
    tokens, long_tokens, cache, long_cache, lengths, long_lengths, norm_gain, q_gain, k_gain,
    w_query, key_weight, value_weight, w_out,
):
    groups = lax.axis_size("replica")
    group = lax.axis_index("replica")
    parity = group % 2
    group_1 = group[None]
    cache = cache.reshape(2, 2, 3, 2048, 128)
    long_cache = long_cache.reshape(2, 2, 1, 2, 2048, 128)

    params = pltpu.CompilerParams(vmem_limit_bytes=16 * 2**20)
    small = pltpu.CompilerParams(vmem_limit_bytes=2 * 2**20)
    held = in_hbm(cache)

    def leaving(begin, count, name):
        return pl.pallas_call(
            functools.partial(leaving_kernel, begin, begin + count),
            out_shape=(
                pltpu.VMEM((count * UNIT, 128), jnp.bfloat16),
                pltpu.VMEM((8, 128), jnp.float32),
            ),
            in_specs=[ANY],
            out_specs=(ANY, ANY),
            scratch_shapes=[pltpu.SemaphoreType.DMA((4,))],
            compiler_params=small,
            name=name,
        )(held)

    leaving_first, _ = leaving(0, FIRST, "leaving_first")
    leaving_second, _ = leaving(FIRST, SECOND, "leaving_second")
    first, second = (
        permute(piece, "replica", lambda i: (i + groups // 2) % groups)
        for piece in (leaving_first, leaving_second)
    )
    far_token = permute(long_tokens, "replica", lambda i: i ^ 1)

    places = jnp.concatenate(
        [
            lax.dynamic_slice_in_dim(lengths, group * 3, 3),
            lax.dynamic_slice_in_dim(long_lengths, group - parity, 2),
            jnp.zeros((3,), jnp.int32),
        ]
    ).astype(jnp.float32)
    inverse = np.float64(ROPE_BASE) ** (-2.0 * np.arange(64) / 128)
    inverse = jnp.asarray(np.concatenate([inverse, inverse]).astype(np.float32))
    sign = jnp.asarray(np.where(np.arange(128) < 64, -1.0, 1.0).astype(np.float32))
    angles = places[:, None] * inverse[None, :]
    cosine, sine = jnp.cos(angles), jnp.sin(angles) * sign

    out_shape = (
        jax.ShapeDtypeStruct((16, 256), jnp.float32),
        jax.ShapeDtypeStruct((16, 256), jnp.float32),
        jax.ShapeDtypeStruct((2, 128), jnp.float32),
        jax.ShapeDtypeStruct((ROWS, 2048), jnp.float32),
    )
    stored = (cache, long_cache, w_query, key_weight, value_weight)
    tables = (norm_gain, q_gain, k_gain, cosine, sine)

    def project_out(layer, state, side, after):
        far = permute(state, "replica", lambda i: i ^ 1)
        part = pl.pallas_call(
            functools.partial(out_kernel, layer),
            out_shape=jax.ShapeDtypeStruct((ROWS, 2048), jnp.float32),
            in_specs=[VM, VM, VM, ANY, ANY],
            out_specs=VM,
            scratch_shapes=[pltpu.VMEM((256, 2048), jnp.bfloat16), pltpu.SemaphoreType.DMA(())],
            compiler_params=params,
            name=f"out_projection_{layer}",
        )(state, far, side, w_out, after)
        part = (part + permute(part, "tensor", lambda i: i ^ 1)).astype(jnp.bfloat16)
        received = [permute(part, "tensor", lambda i, k=k: i ^ k) for k in (2, 4, 6)]
        return (part, *received)

    buffers = ((2048, 256), (2048, 128), (2048, 128)) + ((3, 2048, 128), (2, 2048, 128)) * 2

    def fetch(layer, which, after, name):
        return pl.pallas_call(
            functools.partial(fetch_kernel, layer, which),
            out_shape=tuple(pltpu.VMEM(buffers[i], jnp.bfloat16) for i in which),
            in_specs=[ANY] * 6,
            out_specs=(ANY,) * len(which),
            scratch_shapes=[pltpu.SemaphoreType.DMA((len(which),))],
            compiler_params=small,
            name=name,
        )(*map(in_hbm, stored), after)

    state, side, fresh_0, hidden = pl.pallas_call(
        first_kernel,
        out_shape=out_shape,
        in_specs=[SM] * 3 + [VM] * 13 + [ANY] * 2,
        out_specs=(VM,) * 4,
        scratch_shapes=[
            pltpu.VMEM((3, 2048, 128), jnp.bfloat16),
            pltpu.VMEM((2, 2048, 128), jnp.bfloat16),
            pltpu.SemaphoreType.DMA((2,)),
        ],
        compiler_params=params,
        name="attention_0",
    )(
        group_1, lengths, long_lengths, tokens, long_tokens, far_token, *tables,
        *fetch(0, (0, 1, 2, 3, 4), leaving_first, "fetch_0"), in_hbm(cache), in_hbm(long_cache),
    )
    resident = fetch(1, (0, 1, 2, 3, 4), state, "fetch_1_keys")
    terms = project_out(0, state, side, resident[1])
    resident = (*resident, *fetch(1, (5, 6), terms[0], "fetch_1_values"))
    state, side, fresh_1, hidden = pl.pallas_call(
        second_kernel,
        out_shape=out_shape,
        in_specs=[SM] * 3 + [VM] * 17,
        out_specs=(VM,) * 4,
        compiler_params=params,
        name="attention_1",
    )(group_1, lengths, long_lengths, hidden, *terms, *tables, *resident)
    terms = project_out(1, state, side, side)
    partner = (group + groups // 2) % groups
    arrived_len = lax.dynamic_slice_in_dim(lengths, partner * 3 + 2, 1)
    stored_first, blocks, place = pl.pallas_call(
        store_kernel,
        out_shape=(
            pltpu.HBM((2, 2, 2048, 128), jnp.bfloat16),
            pltpu.VMEM((4, 16, 128), jnp.bfloat16),
            pltpu.VMEM((8, 128), jnp.float32),
        ),
        in_specs=[SM, ANY, ANY],
        out_specs=(ANY, VM, VM),
        scratch_shapes=[
            pltpu.VMEM((FIRST * UNIT, 128), jnp.bfloat16),
            pltpu.SemaphoreType.DMA((2, FIRST)),
        ],
        compiler_params=pltpu.CompilerParams(vmem_limit_bytes=4 * 2**20),
        name="store_first",
    )(arrived_len, in_hbm(first), terms[0])
    stay, long_out, leave = pl.pallas_call(
        final_kernel,
        out_shape=(
            jax.ShapeDtypeStruct((2, 2048), jnp.float32),
            jax.ShapeDtypeStruct((1, 2048), jnp.float32),
            jax.ShapeDtypeStruct((1, 2560), jnp.float32),
        ),
        in_specs=[SM] + [VM] * 7 + [ANY],
        out_specs=(VM,) * 3,
        scratch_shapes=[pltpu.VMEM((ROWS, 2048), jnp.float32)],
        compiler_params=params,
        name="final_rows",
    )(group_1, hidden, *terms, fresh_0, fresh_1, blocks)
    arrived = permute(leave, "replica", lambda i: (i + groups // 2) % groups)
    out_hidden, moved = pl.pallas_call(
        arrival_kernel,
        out_shape=(
            pltpu.HBM((3, 2048), jnp.float32),
            pltpu.HBM((2, 2, 2048, 128), jnp.bfloat16),
        ),
        in_specs=[VM, VM, VM, VM, VM, ANY],
        out_specs=(ANY, ANY),
        input_output_aliases={5: 1},
        scratch_shapes=[
            pltpu.VMEM((3, 2048), jnp.float32),
            pltpu.VMEM((4, 16, 128), jnp.bfloat16),
            pltpu.VMEM((4, UNIT, 128), jnp.bfloat16),
            pltpu.SemaphoreType.DMA((SECOND + 5,)),
        ],
        compiler_params=small,
        name="arrival",
    )(place, stay, arrived, blocks, in_vmem(second), stored_first)
    return (out_hidden, long_out, moved[None, :, :, :, None, :])


def solution(mesh):
    return jax.shard_map(
        local,
        mesh=mesh,
        in_specs=(
            P("replica", None),
            P("replica", None),
            P(None, None, "replica", None, "tensor", None),
            P(None, None, "replica", None, None, "tensor", None),
            P(),
            P(),
            P(),
            P(),
            P(),
            P(None, None, "tensor"),
            P(None, None, "tensor"),
            P(None, None, "tensor"),
            P(None, "tensor", None),
        ),
        out_specs=(
            P("replica", None),
            P("replica", None),
            P("replica", None, None, None, "tensor", None),
        ),
        check_vma=False,
    )
```

```python
import functools

import jax
import jax.numpy as jnp
import numpy as np
from jax import lax
from jax.experimental import pallas as pl
from jax.experimental.pallas import tpu as pltpu
from jax.sharding import PartitionSpec as P

EPSILON = 1e-06
ROPE_BASE = 1000000.0
NEGATIVE = -1e30
ROWS = 8
ANY = pl.BlockSpec(memory_space=pl.ANY)
VM = pl.BlockSpec(memory_space=pltpu.VMEM)
SM = pl.BlockSpec(memory_space=pltpu.SMEM)


def permute(value, axis, target):
    pairs = [(source, target(source)) for source in range(lax.axis_size(axis))]
    return lax.ppermute(value, axis, pairs)


def in_hbm(value):
    return pltpu.with_memory_space_constraint(value, pltpu.HBM)


def in_vmem(value):
    return pltpu.with_memory_space_constraint(value, pltpu.VMEM)


def row_of(count):
    return lax.broadcasted_iota(jnp.int32, (count, 1), 0)


def attention_step(
    layer, group_ref, lengths_ref, long_lengths_ref, hidden, gain_ref, q_gain_ref, k_gain_ref,
    cosine_ref, sine_ref, stored, state_ref, side_ref, fresh_ref, ready,
):
    wq, wk, wv, keys, long_keys, values, long_values = stored
    rows = hidden()
    scale = lax.rsqrt(jnp.mean(rows * rows, axis=-1, keepdims=True) + EPSILON)
    normed = (rows * scale * gain_ref[layer : layer + 1, :]).astype(jnp.bfloat16)
    ready(0, 1, 2)
    queries = jnp.dot(normed, wq[...], preferred_element_type=jnp.float32)
    new_keys = jnp.dot(normed, wk[...], preferred_element_type=jnp.float32)
    new_values = jnp.dot(normed, wv[...], preferred_element_type=jnp.float32).astype(jnp.bfloat16)

    def finish(heads, gain, cosine, sine):
        heads = heads * lax.rsqrt(jnp.mean(heads * heads, axis=-1, keepdims=True) + EPSILON) * gain
        return (heads * cosine + pltpu.roll(heads, 64, 1) * sine).astype(jnp.bfloat16)

    cosine, sine = cosine_ref[...], sine_ref[...]
    q_gain = q_gain_ref[layer : layer + 1, :]
    q0 = finish(queries[:, :128], q_gain, cosine, sine).astype(jnp.float32)
    q1 = finish(queries[:, 128:], q_gain, cosine, sine).astype(jnp.float32)
    key_new = finish(new_keys, k_gain_ref[layer : layer + 1, :], cosine, sine).astype(jnp.float32)
    value_new = new_values.astype(jnp.float32)
    fresh_ref[0:1, :] = key_new[2:3, :]
    fresh_ref[1:2, :] = value_new[2:3, :]
    both = jnp.concatenate([q0, q1], axis=0)
    query = both.astype(jnp.bfloat16)
    keys_twice = jnp.concatenate([key_new, key_new], axis=0)
    values_twice = jnp.concatenate([value_new, value_new], axis=0)
    factor = 128 ** (-0.5)
    own = jnp.sum(both * keys_twice, axis=-1, keepdims=True) * factor

    group = group_ref[0]
    parity = lax.rem(group, 2)
    which = lax.rem(row_of(16), 8)
    limit = jnp.ones((16, 1), jnp.int32)
    for r in range(3):
        limit = jnp.where(which == r, lengths_ref[group * 3 + r], limit)
    for r in range(2):
        limit = jnp.where(
            which == 3 + r, long_lengths_ref[group - parity + r] - parity * 2048, limit
        )
    scores = jnp.zeros((16, 2048), jnp.float32)
    for r in range(5):
        if r == 0:
            ready(3)
        if r == 3:
            ready(4)
        block = keys[r] if r < 3 else long_keys[r - 3]
        product = lax.dot_general(
            query, block, (((1,), (1,)), ((), ())), preferred_element_type=jnp.float32
        )
        scores = jnp.where(which == r, product, scores)
    places = lax.broadcasted_iota(jnp.int32, (16, 2048), 1)
    scores = jnp.where(places < limit, scores * factor, NEGATIVE)
    is_main = which < 3
    highest = jnp.max(scores, axis=-1, keepdims=True)
    highest = jnp.where(is_main, jnp.maximum(highest, own), highest)
    weights = jnp.exp(scores - highest)
    own_weight = jnp.where(is_main, jnp.exp(own - highest), 0.0)
    total = jnp.sum(weights, axis=-1, keepdims=True) + own_weight
    rounded = weights.astype(jnp.bfloat16)
    summed = own_weight.astype(jnp.bfloat16).astype(jnp.float32) * values_twice
    for r in range(5):
        if r == 0:
            ready(5)
        if r == 3:
            ready(6)
        block = values[r] if r < 3 else long_values[r - 3]
        product = jnp.dot(rounded, block, preferred_element_type=jnp.float32)
        summed = summed + jnp.where(which == r, product, 0.0)
    state_ref[:, 0:128] = summed
    lanes = lax.broadcasted_iota(jnp.int32, (16, 128), 1)
    state_ref[:, 128:256] = jnp.where(lanes < 64, highest, total)
    side_ref[:, 0:128] = jnp.broadcast_to(own, (16, 128))
    side_ref[:, 128:256] = values_twice


def parts_of(layer, cache_ref, long_ref, wq_ref, wk_ref, wv_ref):
    return (
        wq_ref.at[layer], wk_ref.at[layer], wv_ref.at[layer],
        cache_ref.at[layer, 0], long_ref.at[layer, 0, 0],
        cache_ref.at[layer, 1], long_ref.at[layer, 1, 0],
    )


def first_kernel(
    group_ref, lengths_ref, long_lengths_ref, tokens_ref, own_long_ref, far_long_ref, *rest
):
    tables, resident, held = rest[:5], rest[5:10], rest[10:12]
    state_ref, side_ref, fresh_ref, hidden_ref = rest[12:16]
    buffers, semaphores = rest[16:18], rest[18]
    sources = (held[0].at[0, 1], held[1].at[0, 1, 0])
    copies = [
        pltpu.make_async_copy(source, target, semaphores.at[i])
        for i, (source, target) in enumerate(zip(sources, buffers))
    ]
    for copy in copies:
        copy.start()

    def ready(*which):
        for i in which:
            if i >= 5:
                copies[i - 5].wait()

    def hidden():
        own = own_long_ref[...].astype(jnp.float32)
        far = far_long_ref[...].astype(jnp.float32)
        even = lax.rem(group_ref[0], 2) == 0
        hidden_ref[...] = jnp.zeros((ROWS, 2048), jnp.float32)
        hidden_ref[0:3, :] = tokens_ref[...].astype(jnp.float32)
        hidden_ref[3:4, :] = jnp.where(even, own, far)
        hidden_ref[4:5, :] = jnp.where(even, far, own)
        return hidden_ref[...]

    attention_step(
        0, group_ref, lengths_ref, long_lengths_ref, hidden, *tables, (*resident, *buffers),
        state_ref, side_ref, fresh_ref, ready,
    )


def total_of(p_ref, r1_ref, r2_ref, r3_ref):
    p, r1, r2, r3 = (ref[...].astype(jnp.float32) for ref in (p_ref, r1_ref, r2_ref, r3_ref))
    return (p + r1) + (r2 + r3)


def second_kernel(
    group_ref, lengths_ref, long_lengths_ref, before_ref, p_ref, r1_ref, r2_ref, r3_ref, *rest
):
    tables, stored = rest[:5], rest[5:12]
    state_ref, side_ref, fresh_ref, hidden_ref = rest[12:16]

    def hidden():
        summed = total_of(p_ref, r1_ref, r2_ref, r3_ref)
        rows = (before_ref[...] + summed).astype(jnp.bfloat16).astype(jnp.float32)
        hidden_ref[...] = rows
        return rows

    attention_step(
        1, group_ref, lengths_ref, long_lengths_ref, hidden, *tables, stored,
        state_ref, side_ref, fresh_ref, lambda *which: None,
    )


UNIT = 256
FIRST = 23
PER = 2048 // UNIT
SECOND = 4 * PER - FIRST


def plane_of(unit):
    return unit // (2 * PER), unit // PER % 2, pl.ds(unit % PER * UNIT, UNIT)


def runs(begin, end):
    out, at = [], begin
    while at < end:
        stop = min(end, at // PER * PER + PER)
        i, j, _ = plane_of(at)
        out.append((i, j, at % PER * UNIT, (stop - at) * UNIT, (at - begin) * UNIT))
        at = stop
    return out


def leaving_kernel(begin, end, cache_ref, out_ref, unused_ref, semaphores):
    del unused_ref
    copies = []
    for n, (i, j, place, size, at) in enumerate(runs(begin, end)):
        copies.append(
            pltpu.make_async_copy(
                cache_ref.at[i, j, 2, pl.ds(place, size)], out_ref.at[pl.ds(at, size)],
                semaphores.at[n],
            )
        )
    for copy in copies:
        copy.start()
    for copy in copies:
        copy.wait()


def leaving_second_kernel(begin, end, cache_ref, out_ref, buffer, semaphores):
    copies = []
    for n, (i, j, place, size, at) in enumerate(runs(begin, end)):
        piece = pl.ds(at, size)
        copies.append(
            (
                pltpu.make_async_copy(
                    cache_ref.at[i, j, 2, pl.ds(place, size)], buffer.at[piece], semaphores.at[0, n]
                ),
                pltpu.make_async_copy(buffer.at[piece], out_ref.at[piece], semaphores.at[1, n]),
            )
        )
    for read, _ in copies:
        read.start()
    for read, write in copies:
        read.wait()
        write.start()
    for _, write in copies:
        write.wait()


def store_kernel(
    length_ref, first_ref, after_ref, stored_ref, blocks_ref, place_ref, buffer, semaphores
):
    del after_ref
    place_ref[...] = jnp.full((8, 128), length_ref[0].astype(jnp.float32))
    reads, writes = [], []
    for n in range(FIRST):
        i, j, rows = plane_of(n)
        piece = pl.ds(n * UNIT, UNIT)
        reads.append(
            pltpu.make_async_copy(first_ref.at[piece], buffer.at[piece], semaphores.at[0, n])
        )
        writes.append(
            pltpu.make_async_copy(buffer.at[piece], stored_ref.at[i, j, rows], semaphores.at[1, n])
        )
    for copy in reads:
        copy.start()
    for read, write in zip(reads, writes):
        read.wait()
        write.start()
    start = length_ref[0] // 16 * 16
    for plane in range(4):
        at = jnp.minimum(plane * 2048 + start, FIRST * UNIT - 16)
        blocks_ref[plane] = buffer[pl.ds(pl.multiple_of(at, 16), 16), :]
    for copy in writes:
        copy.wait()


def arrival_kernel(
    place_ref, stay_ref, arrived_ref, blocks_ref, second_ref, stored_ref, out_ref, moved_ref,
    rows, blocks, patched, semaphores,
):
    del stored_ref
    length = jnp.max(place_ref[...]).astype(jnp.int32)
    hit_unit = length // UNIT
    units = [(unit, *plane_of(unit)) for unit in range(FIRST, 4 * PER)]

    def straight(unit, i, j, place):
        return pltpu.make_async_copy(
            second_ref.at[pl.ds((unit - FIRST) * UNIT, UNIT)], moved_ref.at[i, j, place],
            semaphores.at[unit - FIRST],
        )

    def changed(unit, i, j, place):
        return pltpu.make_async_copy(
            patched.at[unit // PER], moved_ref.at[i, j, place], semaphores.at[unit - FIRST]
        )

    for unit in units:

        @pl.when(hit_unit != unit[0] % PER)
        def _():
            straight(*unit).start()

    fresh = [arrived_ref[0:1, 2048 + 128 * n : 2176 + 128 * n] for n in range(4)]
    start = pl.multiple_of(length // 16 * 16, 16)
    early = []
    for plane in range((FIRST + PER - 1) // PER):
        block = blocks_ref[plane].astype(jnp.float32)
        blocks[plane] = jnp.where(row_of(16) == length - start, fresh[plane], block).astype(
            jnp.bfloat16
        )
        write = pltpu.make_async_copy(
            blocks.at[plane], moved_ref.at[plane // 2, plane % 2, pl.ds(start, 16)],
            semaphores.at[SECOND + plane],
        )
        early.append((plane * PER + hit_unit < FIRST, write))
    for inside, write in early:
        pl.when(inside)(write.start)
    for plane in range(FIRST // PER, 4):
        at = jnp.maximum(plane * PER + hit_unit - FIRST, 0) * UNIT
        whole = second_ref[pl.ds(pl.multiple_of(at, UNIT), UNIT), :].astype(jnp.float32)
        patched[plane] = jnp.where(
            row_of(UNIT) == length - hit_unit * UNIT, fresh[plane], whole
        ).astype(jnp.bfloat16)
    for unit in units:

        @pl.when(hit_unit == unit[0] % PER)
        def _():
            changed(*unit).start()

    rows[0:2, :] = stay_ref[...]
    rows[2:3, :] = arrived_ref[0:1, 0:2048]
    out = pltpu.make_async_copy(rows, out_ref, semaphores.at[SECOND + 4])
    out.start()
    for unit in units:
        straight(*unit).wait()
    for inside, write in early:
        pl.when(inside)(write.wait)
    out.wait()


def fetch_kernel(layer, which, *refs):
    held, outputs, semaphores = refs[:5], refs[6 : 6 + len(which)], refs[-1]
    sources = parts_of(layer, *held)
    copies = [
        pltpu.make_async_copy(sources[i], output, semaphores.at[n])
        for n, (i, output) in enumerate(zip(which, outputs))
    ]
    for copy in copies:
        copy.start()
    for copy in copies:
        copy.wait()


def out_kernel(layer, state_ref, far_ref, side_ref, w_ref, after_ref, out_ref, w, semaphore):
    del after_ref
    copy = pltpu.make_async_copy(w_ref.at[layer], w, semaphore)
    copy.start()
    is_main = lax.rem(row_of(16), 8) < 3
    here, far = state_ref[...], far_ref[...]
    m_here, l_here, acc_here = here[:, 128:129], here[:, 192:193], here[:, :128]
    m_far, l_far, acc_far = far[:, 128:129], far[:, 192:193], far[:, :128]
    own, value = side_ref[:, 0:1], side_ref[:, 128:256]
    highest = jnp.maximum(jnp.maximum(m_here, m_far), own)
    f_here, f_far = jnp.exp(m_here - highest), jnp.exp(m_far - highest)
    own_weight = jnp.exp(own - highest)
    total = (l_here * f_here + l_far * f_far) + own_weight
    own_rounded = own_weight.astype(jnp.bfloat16).astype(jnp.float32)
    summed = (acc_here * f_here + acc_far * f_far) + own_rounded * value
    total = jnp.where(is_main, l_here, total)
    summed = jnp.where(is_main, acc_here, summed)
    attended = summed / total
    attended = jnp.concatenate([attended[:8], attended[8:]], axis=1).astype(jnp.bfloat16)
    copy.wait()
    out_ref[...] = jnp.dot(attended, w[...], preferred_element_type=jnp.float32)


def final_kernel(
    group_ref, before_ref, p_ref, r1_ref, r2_ref, r3_ref, fresh0_ref, fresh1_ref, after_ref,
    stay_ref, long_ref, leave_ref, scratch,
):
    del after_ref
    scratch[...] = before_ref[...] + total_of(p_ref, r1_ref, r2_ref, r3_ref)
    stay_ref[...] = scratch[0:2, :]
    odd = lax.rem(group_ref[0], 2) == 1
    long_ref[...] = jnp.where(odd, scratch[4:5, :], scratch[3:4, :])
    leave_ref[0:1, 0:2048] = scratch[2:3, :]
    for i, ref in enumerate((fresh0_ref, fresh1_ref)):
        for j in range(2):
            leave_ref[0:1, 2048 + 128 * (2 * i + j) : 2176 + 128 * (2 * i + j)] = ref[j : j + 1, :]


def local(
    tokens, long_tokens, cache, long_cache, lengths, long_lengths, norm_gain, q_gain, k_gain,
    w_query, key_weight, value_weight, w_out,
):
    groups = lax.axis_size("replica")
    group = lax.axis_index("replica")
    parity = group % 2
    group_1 = group[None]
    cache = cache.reshape(2, 2, 3, 2048, 128)
    long_cache = long_cache.reshape(2, 2, 1, 2, 2048, 128)

    params = pltpu.CompilerParams(vmem_limit_bytes=16 * 2**20)
    small = pltpu.CompilerParams(vmem_limit_bytes=2 * 2**20)
    held = in_hbm(cache)

    def leaving(begin, count, name):
        return pl.pallas_call(
            functools.partial(leaving_kernel, begin, begin + count),
            out_shape=(
                pltpu.VMEM((count * UNIT, 128), jnp.bfloat16),
                pltpu.VMEM((8, 128), jnp.float32),
            ),
            in_specs=[ANY],
            out_specs=(ANY, ANY),
            scratch_shapes=[pltpu.SemaphoreType.DMA((4,))],
            compiler_params=small,
            name=name,
        )(held)

    leaving_first, _ = leaving(0, FIRST, "leaving_first")
    leaving_second = pl.pallas_call(
        functools.partial(leaving_second_kernel, FIRST, 4 * PER),
        out_shape=pltpu.HBM((SECOND * UNIT, 128), jnp.bfloat16),
        in_specs=[ANY],
        out_specs=ANY,
        scratch_shapes=[
            pltpu.VMEM((SECOND * UNIT, 128), jnp.bfloat16),
            pltpu.SemaphoreType.DMA((2, 4)),
        ],
        compiler_params=small,
        name="leaving_second",
    )(held)
    first, second = (
        permute(piece, "replica", lambda i: (i + groups // 2) % groups)
        for piece in (leaving_first, leaving_second)
    )
    far_token = permute(long_tokens, "replica", lambda i: i ^ 1)

    places = jnp.concatenate(
        [
            lax.dynamic_slice_in_dim(lengths, group * 3, 3),
            lax.dynamic_slice_in_dim(long_lengths, group - parity, 2),
            jnp.zeros((3,), jnp.int32),
        ]
    ).astype(jnp.float32)
    inverse = np.float64(ROPE_BASE) ** (-2.0 * np.arange(64) / 128)
    inverse = jnp.asarray(np.concatenate([inverse, inverse]).astype(np.float32))
    sign = jnp.asarray(np.where(np.arange(128) < 64, -1.0, 1.0).astype(np.float32))
    angles = places[:, None] * inverse[None, :]
    cosine, sine = jnp.cos(angles), jnp.sin(angles) * sign

    out_shape = (
        jax.ShapeDtypeStruct((16, 256), jnp.float32),
        jax.ShapeDtypeStruct((16, 256), jnp.float32),
        jax.ShapeDtypeStruct((2, 128), jnp.float32),
        jax.ShapeDtypeStruct((ROWS, 2048), jnp.float32),
    )
    stored = (cache, long_cache, w_query, key_weight, value_weight)
    tables = (norm_gain, q_gain, k_gain, cosine, sine)

    def project_out(layer, state, side, after):
        far = permute(state, "replica", lambda i: i ^ 1)
        part = pl.pallas_call(
            functools.partial(out_kernel, layer),
            out_shape=jax.ShapeDtypeStruct((ROWS, 2048), jnp.float32),
            in_specs=[VM, VM, VM, ANY, ANY],
            out_specs=VM,
            scratch_shapes=[pltpu.VMEM((256, 2048), jnp.bfloat16), pltpu.SemaphoreType.DMA(())],
            compiler_params=params,
            name=f"out_projection_{layer}",
        )(state, far, side, w_out, after)
        part = (part + permute(part, "tensor", lambda i: i ^ 1)).astype(jnp.bfloat16)
        received = [permute(part, "tensor", lambda i, k=k: i ^ k) for k in (2, 4, 6)]
        return (part, *received)

    buffers = ((2048, 256), (2048, 128), (2048, 128)) + ((3, 2048, 128), (2, 2048, 128)) * 2

    def fetch(layer, which, after, name):
        return pl.pallas_call(
            functools.partial(fetch_kernel, layer, which),
            out_shape=tuple(pltpu.VMEM(buffers[i], jnp.bfloat16) for i in which),
            in_specs=[ANY] * 6,
            out_specs=(ANY,) * len(which),
            scratch_shapes=[pltpu.SemaphoreType.DMA((len(which),))],
            compiler_params=small,
            name=name,
        )(*map(in_hbm, stored), after)

    state, side, fresh_0, hidden = pl.pallas_call(
        first_kernel,
        out_shape=out_shape,
        in_specs=[SM] * 3 + [VM] * 13 + [ANY] * 2,
        out_specs=(VM,) * 4,
        scratch_shapes=[
            pltpu.VMEM((3, 2048, 128), jnp.bfloat16),
            pltpu.VMEM((2, 2048, 128), jnp.bfloat16),
            pltpu.SemaphoreType.DMA((2,)),
        ],
        compiler_params=params,
        name="attention_0",
    )(
        group_1, lengths, long_lengths, tokens, long_tokens, far_token, *tables,
        *fetch(0, (0, 1, 2, 3, 4), leaving_first, "fetch_0"), in_hbm(cache), in_hbm(long_cache),
    )
    resident = fetch(1, (0, 1, 2, 3, 4), state, "fetch_1_keys")
    terms = project_out(0, state, side, resident[1])
    resident = (*resident, *fetch(1, (5, 6), terms[0], "fetch_1_values"))
    state, side, fresh_1, hidden = pl.pallas_call(
        second_kernel,
        out_shape=out_shape,
        in_specs=[SM] * 3 + [VM] * 17,
        out_specs=(VM,) * 4,
        compiler_params=params,
        name="attention_1",
    )(group_1, lengths, long_lengths, hidden, *terms, *tables, *resident)
    terms = project_out(1, state, side, side)
    partner = (group + groups // 2) % groups
    arrived_len = lax.dynamic_slice_in_dim(lengths, partner * 3 + 2, 1)
    stored_first, blocks, place = pl.pallas_call(
        store_kernel,
        out_shape=(
            pltpu.HBM((2, 2, 2048, 128), jnp.bfloat16),
            pltpu.VMEM((4, 16, 128), jnp.bfloat16),
            pltpu.VMEM((8, 128), jnp.float32),
        ),
        in_specs=[SM, ANY, ANY],
        out_specs=(ANY, VM, VM),
        scratch_shapes=[
            pltpu.VMEM((FIRST * UNIT, 128), jnp.bfloat16),
            pltpu.SemaphoreType.DMA((2, FIRST)),
        ],
        compiler_params=pltpu.CompilerParams(vmem_limit_bytes=4 * 2**20),
        name="store_first",
    )(arrived_len, in_vmem(first), terms[0])
    stay, long_out, leave = pl.pallas_call(
        final_kernel,
        out_shape=(
            jax.ShapeDtypeStruct((2, 2048), jnp.float32),
            jax.ShapeDtypeStruct((1, 2048), jnp.float32),
            jax.ShapeDtypeStruct((1, 2560), jnp.float32),
        ),
        in_specs=[SM] + [VM] * 7 + [ANY],
        out_specs=(VM,) * 3,
        scratch_shapes=[pltpu.VMEM((ROWS, 2048), jnp.float32)],
        compiler_params=params,
        name="final_rows",
    )(group_1, hidden, *terms, fresh_0, fresh_1, blocks)
    arrived = permute(leave, "replica", lambda i: (i + groups // 2) % groups)
    out_hidden, moved = pl.pallas_call(
        arrival_kernel,
        out_shape=(
            pltpu.HBM((3, 2048), jnp.float32),
            pltpu.HBM((2, 2, 2048, 128), jnp.bfloat16),
        ),
        in_specs=[VM, VM, VM, VM, VM, ANY],
        out_specs=(ANY, ANY),
        input_output_aliases={5: 1},
        scratch_shapes=[
            pltpu.VMEM((3, 2048), jnp.float32),
            pltpu.VMEM((4, 16, 128), jnp.bfloat16),
            pltpu.VMEM((4, UNIT, 128), jnp.bfloat16),
            pltpu.SemaphoreType.DMA((SECOND + 5,)),
        ],
        compiler_params=small,
        name="arrival",
    )(place, stay, arrived, blocks, in_vmem(second), stored_first)
    return (out_hidden, long_out, moved[None, :, :, :, None, :])


def solution(mesh):
    return jax.shard_map(
        local,
        mesh=mesh,
        in_specs=(
            P("replica", None),
            P("replica", None),
            P(None, None, "replica", None, "tensor", None),
            P(None, None, "replica", None, None, "tensor", None),
            P(),
            P(),
            P(),
            P(),
            P(),
            P(None, None, "tensor"),
            P(None, None, "tensor"),
            P(None, None, "tensor"),
            P(None, "tensor", None),
        ),
        out_specs=(
            P("replica", None),
            P("replica", None),
            P("replica", None, None, None, "tensor", None),
        ),
        check_vma=False,
    )
```

```python
import functools

import jax
import jax.numpy as jnp
import numpy as np
from jax import lax
from jax.experimental import pallas as pl
from jax.experimental.pallas import tpu as pltpu
from jax.sharding import PartitionSpec as P

EPSILON = 1e-06
ROPE_BASE = 1000000.0
NEGATIVE = -1e30
ROWS = 8
ANY = pl.BlockSpec(memory_space=pl.ANY)
VM = pl.BlockSpec(memory_space=pltpu.VMEM)
SM = pl.BlockSpec(memory_space=pltpu.SMEM)


def permute(value, axis, target):
    pairs = [(source, target(source)) for source in range(lax.axis_size(axis))]
    return lax.ppermute(value, axis, pairs)


def in_hbm(value):
    return pltpu.with_memory_space_constraint(value, pltpu.HBM)


def in_vmem(value):
    return pltpu.with_memory_space_constraint(value, pltpu.VMEM)


def row_of(count):
    return lax.broadcasted_iota(jnp.int32, (count, 1), 0)


def attention_step(
    layer, group_ref, lengths_ref, long_lengths_ref, hidden, gain_ref, q_gain_ref, k_gain_ref,
    cosine_ref, sine_ref, stored, state_ref, side_ref, fresh_ref, ready,
):
    wq, wk, wv, keys, long_keys, values, long_values = stored
    rows = hidden()
    scale = lax.rsqrt(jnp.mean(rows * rows, axis=-1, keepdims=True) + EPSILON)
    normed = (rows * scale * gain_ref[layer : layer + 1, :]).astype(jnp.bfloat16)
    ready(0, 1, 2)
    queries = jnp.dot(normed, wq[...], preferred_element_type=jnp.float32)
    new_keys = jnp.dot(normed, wk[...], preferred_element_type=jnp.float32)
    new_values = jnp.dot(normed, wv[...], preferred_element_type=jnp.float32).astype(jnp.bfloat16)

    def finish(heads, gain, cosine, sine):
        heads = heads * lax.rsqrt(jnp.mean(heads * heads, axis=-1, keepdims=True) + EPSILON) * gain
        return (heads * cosine + pltpu.roll(heads, 64, 1) * sine).astype(jnp.bfloat16)

    cosine, sine = cosine_ref[...], sine_ref[...]
    q_gain = q_gain_ref[layer : layer + 1, :]
    q0 = finish(queries[:, :128], q_gain, cosine, sine).astype(jnp.float32)
    q1 = finish(queries[:, 128:], q_gain, cosine, sine).astype(jnp.float32)
    key_new = finish(new_keys, k_gain_ref[layer : layer + 1, :], cosine, sine).astype(jnp.float32)
    value_new = new_values.astype(jnp.float32)
    fresh_ref[0:1, :] = key_new[2:3, :]
    fresh_ref[1:2, :] = value_new[2:3, :]
    both = jnp.concatenate([q0, q1], axis=0)
    query = both.astype(jnp.bfloat16)
    keys_twice = jnp.concatenate([key_new, key_new], axis=0)
    values_twice = jnp.concatenate([value_new, value_new], axis=0)
    factor = 128 ** (-0.5)
    own = jnp.sum(both * keys_twice, axis=-1, keepdims=True) * factor

    group = group_ref[0]
    parity = lax.rem(group, 2)
    which = lax.rem(row_of(16), 8)
    limit = jnp.ones((16, 1), jnp.int32)
    for r in range(3):
        limit = jnp.where(which == r, lengths_ref[group * 3 + r], limit)
    for r in range(2):
        limit = jnp.where(
            which == 3 + r, long_lengths_ref[group - parity + r] - parity * 2048, limit
        )
    scores = jnp.zeros((16, 2048), jnp.float32)
    for r in range(5):
        if r == 0:
            ready(3)
        if r == 3:
            ready(4)
        block = keys[r] if r < 3 else long_keys[r - 3]
        product = lax.dot_general(
            query, block, (((1,), (1,)), ((), ())), preferred_element_type=jnp.float32
        )
        scores = jnp.where(which == r, product, scores)
    places = lax.broadcasted_iota(jnp.int32, (16, 2048), 1)
    scores = jnp.where(places < limit, scores * factor, NEGATIVE)
    is_main = which < 3
    highest = jnp.max(scores, axis=-1, keepdims=True)
    highest = jnp.where(is_main, jnp.maximum(highest, own), highest)
    weights = jnp.exp(scores - highest)
    own_weight = jnp.where(is_main, jnp.exp(own - highest), 0.0)
    total = jnp.sum(weights, axis=-1, keepdims=True) + own_weight
    rounded = weights.astype(jnp.bfloat16)
    summed = own_weight.astype(jnp.bfloat16).astype(jnp.float32) * values_twice
    for r in range(5):
        if r == 0:
            ready(5)
        if r == 3:
            ready(6)
        block = values[r] if r < 3 else long_values[r - 3]
        product = jnp.dot(rounded, block, preferred_element_type=jnp.float32)
        summed = summed + jnp.where(which == r, product, 0.0)
    state_ref[:, 0:128] = summed
    lanes = lax.broadcasted_iota(jnp.int32, (16, 128), 1)
    state_ref[:, 128:256] = jnp.where(lanes < 64, highest, total)
    side_ref[:, 0:128] = jnp.broadcast_to(own, (16, 128))
    side_ref[:, 128:256] = values_twice


def parts_of(layer, cache_ref, long_ref, wq_ref, wk_ref, wv_ref):
    return (
        wq_ref.at[layer], wk_ref.at[layer], wv_ref.at[layer],
        cache_ref.at[layer, 0], long_ref.at[layer, 0, 0],
        cache_ref.at[layer, 1], long_ref.at[layer, 1, 0],
    )


def first_kernel(
    group_ref, lengths_ref, long_lengths_ref, tokens_ref, own_long_ref, far_long_ref, *rest
):
    tables, resident, held = rest[:5], rest[5:10], rest[10:12]
    state_ref, side_ref, fresh_ref, hidden_ref = rest[12:16]
    buffers, semaphores = rest[16:18], rest[18]
    sources = (held[0].at[0, 1], held[1].at[0, 1, 0])
    copies = [
        pltpu.make_async_copy(source, target, semaphores.at[i])
        for i, (source, target) in enumerate(zip(sources, buffers))
    ]
    for copy in copies:
        copy.start()

    def ready(*which):
        for i in which:
            if i >= 5:
                copies[i - 5].wait()

    def hidden():
        own = own_long_ref[...].astype(jnp.float32)
        far = far_long_ref[...].astype(jnp.float32)
        even = lax.rem(group_ref[0], 2) == 0
        hidden_ref[...] = jnp.zeros((ROWS, 2048), jnp.float32)
        hidden_ref[0:3, :] = tokens_ref[...].astype(jnp.float32)
        hidden_ref[3:4, :] = jnp.where(even, own, far)
        hidden_ref[4:5, :] = jnp.where(even, far, own)
        return hidden_ref[...]

    attention_step(
        0, group_ref, lengths_ref, long_lengths_ref, hidden, *tables, (*resident, *buffers),
        state_ref, side_ref, fresh_ref, ready,
    )


def total_of(p_ref, r1_ref, r2_ref, r3_ref):
    p, r1, r2, r3 = (ref[...].astype(jnp.float32) for ref in (p_ref, r1_ref, r2_ref, r3_ref))
    return (p + r1) + (r2 + r3)


def second_kernel(
    group_ref, lengths_ref, long_lengths_ref, before_ref, p_ref, r1_ref, r2_ref, r3_ref, *rest
):
    tables, stored = rest[:5], rest[5:12]
    state_ref, side_ref, fresh_ref, hidden_ref = rest[12:16]

    def hidden():
        summed = total_of(p_ref, r1_ref, r2_ref, r3_ref)
        rows = (before_ref[...] + summed).astype(jnp.bfloat16).astype(jnp.float32)
        hidden_ref[...] = rows
        return rows

    attention_step(
        1, group_ref, lengths_ref, long_lengths_ref, hidden, *tables, stored,
        state_ref, side_ref, fresh_ref, lambda *which: None,
    )


UNIT = 256
FIRST = 23
PER = 2048 // UNIT
SECOND = 4 * PER - FIRST


def plane_of(unit):
    return unit // (2 * PER), unit // PER % 2, pl.ds(unit % PER * UNIT, UNIT)


def runs(begin, end):
    out, at = [], begin
    while at < end:
        stop = min(end, at // PER * PER + PER)
        i, j, _ = plane_of(at)
        out.append((i, j, at % PER * UNIT, (stop - at) * UNIT, (at - begin) * UNIT))
        at = stop
    return out


def leaving_kernel(begin, end, cache_ref, out_ref, unused_ref, semaphores):
    del unused_ref
    copies = []
    for n, (i, j, place, size, at) in enumerate(runs(begin, end)):
        copies.append(
            pltpu.make_async_copy(
                cache_ref.at[i, j, 2, pl.ds(place, size)], out_ref.at[pl.ds(at, size)],
                semaphores.at[n],
            )
        )
    for copy in copies:
        copy.start()
    for copy in copies:
        copy.wait()


def store_kernel(
    length_ref, first_ref, after_ref, stored_ref, blocks_ref, place_ref, buffer, semaphores
):
    del after_ref
    place_ref[...] = jnp.full((8, 128), length_ref[0].astype(jnp.float32))
    reads, writes = [], []
    for n in range(FIRST):
        i, j, rows = plane_of(n)
        piece = pl.ds(n * UNIT, UNIT)
        reads.append(
            pltpu.make_async_copy(first_ref.at[piece], buffer.at[piece], semaphores.at[0, n])
        )
        writes.append(
            pltpu.make_async_copy(buffer.at[piece], stored_ref.at[i, j, rows], semaphores.at[1, n])
        )
    for copy in reads:
        copy.start()
    for read, write in zip(reads, writes):
        read.wait()
        write.start()
    start = length_ref[0] // 16 * 16
    for plane in range(4):
        at = jnp.minimum(plane * 2048 + start, FIRST * UNIT - 16)
        blocks_ref[plane] = buffer[pl.ds(pl.multiple_of(at, 16), 16), :]
    for copy in writes:
        copy.wait()


def arrival_kernel(
    place_ref, stay_ref, arrived_ref, blocks_ref, second_ref, stored_ref, out_ref, moved_ref,
    rows, blocks, patched, semaphores,
):
    del stored_ref
    rows[0:2, :] = stay_ref[...]
    rows[2:3, :] = arrived_ref[0:1, 0:2048]
    out = pltpu.make_async_copy(rows, out_ref, semaphores.at[SECOND + 4])
    out.start()
    length = jnp.max(place_ref[...]).astype(jnp.int32)
    hit_unit = length // UNIT
    units = [(unit, *plane_of(unit)) for unit in range(FIRST, 4 * PER)]

    def straight(unit, i, j, place):
        return pltpu.make_async_copy(
            second_ref.at[pl.ds((unit - FIRST) * UNIT, UNIT)], moved_ref.at[i, j, place],
            semaphores.at[unit - FIRST],
        )

    def changed(unit, i, j, place):
        return pltpu.make_async_copy(
            patched.at[unit // PER], moved_ref.at[i, j, place], semaphores.at[unit - FIRST]
        )

    for unit in units:

        @pl.when(hit_unit != unit[0] % PER)
        def _():
            straight(*unit).start()

    fresh = [arrived_ref[0:1, 2048 + 128 * n : 2176 + 128 * n] for n in range(4)]
    start = pl.multiple_of(length // 16 * 16, 16)
    early = []
    for plane in range((FIRST + PER - 1) // PER):
        block = blocks_ref[plane].astype(jnp.float32)
        blocks[plane] = jnp.where(row_of(16) == length - start, fresh[plane], block).astype(
            jnp.bfloat16
        )
        write = pltpu.make_async_copy(
            blocks.at[plane], moved_ref.at[plane // 2, plane % 2, pl.ds(start, 16)],
            semaphores.at[SECOND + plane],
        )
        early.append((plane * PER + hit_unit < FIRST, write))
    for inside, write in early:
        pl.when(inside)(write.start)
    for plane in range(FIRST // PER, 4):
        at = jnp.maximum(plane * PER + hit_unit - FIRST, 0) * UNIT
        whole = second_ref[pl.ds(pl.multiple_of(at, UNIT), UNIT), :].astype(jnp.float32)
        patched[plane] = jnp.where(
            row_of(UNIT) == length - hit_unit * UNIT, fresh[plane], whole
        ).astype(jnp.bfloat16)
    for unit in units:

        @pl.when(hit_unit == unit[0] % PER)
        def _():
            changed(*unit).start()

    for unit in units:
        straight(*unit).wait()
    for inside, write in early:
        pl.when(inside)(write.wait)
    out.wait()


def fetch_kernel(layer, which, *refs):
    held, outputs, semaphores = refs[:5], refs[6 : 6 + len(which)], refs[-1]
    sources = parts_of(layer, *held)
    copies = [
        pltpu.make_async_copy(sources[i], output, semaphores.at[n])
        for n, (i, output) in enumerate(zip(which, outputs))
    ]
    for copy in copies:
        copy.start()
    for copy in copies:
        copy.wait()


def out_kernel(layer, state_ref, far_ref, side_ref, w_ref, after_ref, out_ref, w, semaphore):
    del after_ref
    copy = pltpu.make_async_copy(w_ref.at[layer], w, semaphore)
    copy.start()
    is_main = lax.rem(row_of(16), 8) < 3
    here, far = state_ref[...], far_ref[...]
    m_here, l_here, acc_here = here[:, 128:129], here[:, 192:193], here[:, :128]
    m_far, l_far, acc_far = far[:, 128:129], far[:, 192:193], far[:, :128]
    own, value = side_ref[:, 0:1], side_ref[:, 128:256]
    highest = jnp.maximum(jnp.maximum(m_here, m_far), own)
    f_here, f_far = jnp.exp(m_here - highest), jnp.exp(m_far - highest)
    own_weight = jnp.exp(own - highest)
    total = (l_here * f_here + l_far * f_far) + own_weight
    own_rounded = own_weight.astype(jnp.bfloat16).astype(jnp.float32)
    summed = (acc_here * f_here + acc_far * f_far) + own_rounded * value
    total = jnp.where(is_main, l_here, total)
    summed = jnp.where(is_main, acc_here, summed)
    attended = summed / total
    attended = jnp.concatenate([attended[:8], attended[8:]], axis=1).astype(jnp.bfloat16)
    copy.wait()
    out_ref[...] = jnp.dot(attended, w[...], preferred_element_type=jnp.float32)


def final_kernel(
    group_ref, before_ref, p_ref, r1_ref, r2_ref, r3_ref, fresh0_ref, fresh1_ref, after_ref,
    stay_ref, long_ref, leave_ref, scratch,
):
    del after_ref
    scratch[...] = before_ref[...] + total_of(p_ref, r1_ref, r2_ref, r3_ref)
    stay_ref[...] = scratch[0:2, :]
    odd = lax.rem(group_ref[0], 2) == 1
    long_ref[...] = jnp.where(odd, scratch[4:5, :], scratch[3:4, :])
    leave_ref[0:1, 0:2048] = scratch[2:3, :]
    for i, ref in enumerate((fresh0_ref, fresh1_ref)):
        for j in range(2):
            leave_ref[0:1, 2048 + 128 * (2 * i + j) : 2176 + 128 * (2 * i + j)] = ref[j : j + 1, :]


def local(
    tokens, long_tokens, cache, long_cache, lengths, long_lengths, norm_gain, q_gain, k_gain,
    w_query, key_weight, value_weight, w_out,
):
    groups = lax.axis_size("replica")
    group = lax.axis_index("replica")
    parity = group % 2
    group_1 = group[None]
    cache = cache.reshape(2, 2, 3, 2048, 128)
    long_cache = long_cache.reshape(2, 2, 1, 2, 2048, 128)

    params = pltpu.CompilerParams(vmem_limit_bytes=16 * 2**20)
    small = pltpu.CompilerParams(vmem_limit_bytes=2 * 2**20)
    held = in_hbm(cache)

    def leaving(begin, count, name):
        return pl.pallas_call(
            functools.partial(leaving_kernel, begin, begin + count),
            out_shape=(
                pltpu.VMEM((count * UNIT, 128), jnp.bfloat16),
                pltpu.VMEM((8, 128), jnp.float32),
            ),
            in_specs=[ANY],
            out_specs=(ANY, ANY),
            scratch_shapes=[pltpu.SemaphoreType.DMA((4,))],
            compiler_params=small,
            name=name,
        )(held)

    leaving_first, _ = leaving(0, FIRST, "leaving_first")
    leaving_second, _ = leaving(FIRST, SECOND, "leaving_second")
    first, second = (
        permute(piece, "replica", lambda i: (i + groups // 2) % groups)
        for piece in (leaving_first, leaving_second)
    )
    far_token = permute(long_tokens, "replica", lambda i: i ^ 1)

    places = jnp.concatenate(
        [
            lax.dynamic_slice_in_dim(lengths, group * 3, 3),
            lax.dynamic_slice_in_dim(long_lengths, group - parity, 2),
            jnp.zeros((3,), jnp.int32),
        ]
    ).astype(jnp.float32)
    inverse = np.float64(ROPE_BASE) ** (-2.0 * np.arange(64) / 128)
    inverse = jnp.asarray(np.concatenate([inverse, inverse]).astype(np.float32))
    sign = jnp.asarray(np.where(np.arange(128) < 64, -1.0, 1.0).astype(np.float32))
    angles = places[:, None] * inverse[None, :]
    cosine, sine = jnp.cos(angles), jnp.sin(angles) * sign

    out_shape = (
        jax.ShapeDtypeStruct((16, 256), jnp.float32),
        jax.ShapeDtypeStruct((16, 256), jnp.float32),
        jax.ShapeDtypeStruct((2, 128), jnp.float32),
        jax.ShapeDtypeStruct((ROWS, 2048), jnp.float32),
    )
    stored = (cache, long_cache, w_query, key_weight, value_weight)
    tables = (norm_gain, q_gain, k_gain, cosine, sine)

    def project_out(layer, state, side, after):
        far = permute(state, "replica", lambda i: i ^ 1)
        part = pl.pallas_call(
            functools.partial(out_kernel, layer),
            out_shape=jax.ShapeDtypeStruct((ROWS, 2048), jnp.float32),
            in_specs=[VM, VM, VM, ANY, ANY],
            out_specs=VM,
            scratch_shapes=[pltpu.VMEM((256, 2048), jnp.bfloat16), pltpu.SemaphoreType.DMA(())],
            compiler_params=params,
            name=f"out_projection_{layer}",
        )(state, far, side, w_out, after)
        part = (part + permute(part, "tensor", lambda i: i ^ 1)).astype(jnp.bfloat16)
        received = [permute(part, "tensor", lambda i, k=k: i ^ k) for k in (2, 4, 6)]
        return (part, *received)

    buffers = ((2048, 256), (2048, 128), (2048, 128)) + ((3, 2048, 128), (2, 2048, 128)) * 2

    def fetch(layer, which, after, name):
        return pl.pallas_call(
            functools.partial(fetch_kernel, layer, which),
            out_shape=tuple(pltpu.VMEM(buffers[i], jnp.bfloat16) for i in which),
            in_specs=[ANY] * 6,
            out_specs=(ANY,) * len(which),
            scratch_shapes=[pltpu.SemaphoreType.DMA((len(which),))],
            compiler_params=small,
            name=name,
        )(*map(in_hbm, stored), after)

    state, side, fresh_0, hidden = pl.pallas_call(
        first_kernel,
        out_shape=out_shape,
        in_specs=[SM] * 3 + [VM] * 13 + [ANY] * 2,
        out_specs=(VM,) * 4,
        scratch_shapes=[
            pltpu.VMEM((3, 2048, 128), jnp.bfloat16),
            pltpu.VMEM((2, 2048, 128), jnp.bfloat16),
            pltpu.SemaphoreType.DMA((2,)),
        ],
        compiler_params=params,
        name="attention_0",
    )(
        group_1, lengths, long_lengths, tokens, long_tokens, far_token, *tables,
        *fetch(0, (0, 1, 2, 3, 4), leaving_first, "fetch_0"), in_hbm(cache), in_hbm(long_cache),
    )
    resident = fetch(1, (0, 1, 2, 3, 4), state, "fetch_1_keys")
    terms = project_out(0, state, side, resident[1])
    resident = (*resident, *fetch(1, (5, 6), terms[0], "fetch_1_values"))
    state, side, fresh_1, hidden = pl.pallas_call(
        second_kernel,
        out_shape=out_shape,
        in_specs=[SM] * 3 + [VM] * 17,
        out_specs=(VM,) * 4,
        compiler_params=params,
        name="attention_1",
    )(group_1, lengths, long_lengths, hidden, *terms, *tables, *resident)
    terms = project_out(1, state, side, side)
    partner = (group + groups // 2) % groups
    arrived_len = lax.dynamic_slice_in_dim(lengths, partner * 3 + 2, 1)
    stored_first, blocks, place = pl.pallas_call(
        store_kernel,
        out_shape=(
            pltpu.HBM((2, 2, 2048, 128), jnp.bfloat16),
            pltpu.VMEM((4, 16, 128), jnp.bfloat16),
            pltpu.VMEM((8, 128), jnp.float32),
        ),
        in_specs=[SM, ANY, ANY],
        out_specs=(ANY, VM, VM),
        scratch_shapes=[
            pltpu.VMEM((FIRST * UNIT, 128), jnp.bfloat16),
            pltpu.SemaphoreType.DMA((2, FIRST)),
        ],
        compiler_params=pltpu.CompilerParams(vmem_limit_bytes=4 * 2**20),
        name="store_first",
    )(arrived_len, in_hbm(first), terms[0])
    stay, long_out, leave = pl.pallas_call(
        final_kernel,
        out_shape=(
            jax.ShapeDtypeStruct((2, 2048), jnp.float32),
            jax.ShapeDtypeStruct((1, 2048), jnp.float32),
            jax.ShapeDtypeStruct((1, 2560), jnp.float32),
        ),
        in_specs=[SM] + [VM] * 7 + [ANY],
        out_specs=(VM,) * 3,
        scratch_shapes=[pltpu.VMEM((ROWS, 2048), jnp.float32)],
        compiler_params=params,
        name="final_rows",
    )(group_1, hidden, *terms, fresh_0, fresh_1, blocks)
    arrived = permute(leave, "replica", lambda i: (i + groups // 2) % groups)
    out_hidden, moved = pl.pallas_call(
        arrival_kernel,
        out_shape=(
            pltpu.HBM((3, 2048), jnp.float32),
            pltpu.HBM((2, 2, 2048, 128), jnp.bfloat16),
        ),
        in_specs=[VM, VM, VM, VM, VM, ANY],
        out_specs=(ANY, ANY),
        input_output_aliases={5: 1},
        scratch_shapes=[
            pltpu.VMEM((3, 2048), jnp.float32),
            pltpu.VMEM((4, 16, 128), jnp.bfloat16),
            pltpu.VMEM((4, UNIT, 128), jnp.bfloat16),
            pltpu.SemaphoreType.DMA((SECOND + 5,)),
        ],
        compiler_params=small,
        name="arrival",
    )(place, stay, arrived, blocks, in_vmem(second), stored_first)
    return (out_hidden, long_out, moved[None, :, :, :, None, :])


def solution(mesh):
    return jax.shard_map(
        local,
        mesh=mesh,
        in_specs=(
            P("replica", None),
            P("replica", None),
            P(None, None, "replica", None, "tensor", None),
            P(None, None, "replica", None, None, "tensor", None),
            P(),
            P(),
            P(),
            P(),
            P(),
            P(None, None, "tensor"),
            P(None, None, "tensor"),
            P(None, None, "tensor"),
            P(None, "tensor", None),
        ),
        out_specs=(
            P("replica", None),
            P("replica", None),
            P("replica", None, None, None, "tensor", None),
        ),
        check_vma=False,
    )
```

```python
import functools

import jax
import jax.numpy as jnp
import numpy as np
from jax import lax
from jax.experimental import pallas as pl
from jax.experimental.pallas import tpu as pltpu
from jax.sharding import PartitionSpec as P

EPSILON = 1e-06
ROPE_BASE = 1000000.0
NEGATIVE = -1e30
ROWS = 8
ANY = pl.BlockSpec(memory_space=pl.ANY)
VM = pl.BlockSpec(memory_space=pltpu.VMEM)
SM = pl.BlockSpec(memory_space=pltpu.SMEM)


def permute(value, axis, target):
    pairs = [(source, target(source)) for source in range(lax.axis_size(axis))]
    return lax.ppermute(value, axis, pairs)


def in_hbm(value):
    return pltpu.with_memory_space_constraint(value, pltpu.HBM)


def in_vmem(value):
    return pltpu.with_memory_space_constraint(value, pltpu.VMEM)


def row_of(count):
    return lax.broadcasted_iota(jnp.int32, (count, 1), 0)


def attention_step(
    layer, group_ref, lengths_ref, long_lengths_ref, hidden, gain_ref, q_gain_ref, k_gain_ref,
    cosine_ref, sine_ref, stored, state_ref, side_ref, fresh_ref, ready,
):
    wq, wk, wv, keys, long_keys, values, long_values = stored
    rows = hidden()
    scale = lax.rsqrt(jnp.mean(rows * rows, axis=-1, keepdims=True) + EPSILON)
    normed = (rows * scale * gain_ref[layer : layer + 1, :]).astype(jnp.bfloat16)
    ready(0, 1, 2)
    queries = jnp.dot(normed, wq[...], preferred_element_type=jnp.float32)
    new_keys = jnp.dot(normed, wk[...], preferred_element_type=jnp.float32)
    new_values = jnp.dot(normed, wv[...], preferred_element_type=jnp.float32).astype(jnp.bfloat16)

    def finish(heads, gain, cosine, sine):
        heads = heads * lax.rsqrt(jnp.mean(heads * heads, axis=-1, keepdims=True) + EPSILON) * gain
        return (heads * cosine + pltpu.roll(heads, 64, 1) * sine).astype(jnp.bfloat16)

    cosine, sine = cosine_ref[...], sine_ref[...]
    q_gain = q_gain_ref[layer : layer + 1, :]
    q0 = finish(queries[:, :128], q_gain, cosine, sine).astype(jnp.float32)
    q1 = finish(queries[:, 128:], q_gain, cosine, sine).astype(jnp.float32)
    key_new = finish(new_keys, k_gain_ref[layer : layer + 1, :], cosine, sine).astype(jnp.float32)
    value_new = new_values.astype(jnp.float32)
    fresh_ref[0:1, :] = key_new[2:3, :]
    fresh_ref[1:2, :] = value_new[2:3, :]
    both = jnp.concatenate([q0, q1], axis=0)
    query = both.astype(jnp.bfloat16)
    keys_twice = jnp.concatenate([key_new, key_new], axis=0)
    values_twice = jnp.concatenate([value_new, value_new], axis=0)
    factor = 128 ** (-0.5)
    own = jnp.sum(both * keys_twice, axis=-1, keepdims=True) * factor

    group = group_ref[0]
    parity = lax.rem(group, 2)
    which = lax.rem(row_of(16), 8)
    limit = jnp.ones((16, 1), jnp.int32)
    for r in range(3):
        limit = jnp.where(which == r, lengths_ref[group * 3 + r], limit)
    for r in range(2):
        limit = jnp.where(
            which == 3 + r, long_lengths_ref[group - parity + r] - parity * 2048, limit
        )
    scores = jnp.zeros((16, 2048), jnp.float32)
    for r in range(5):
        if r == 0:
            ready(3)
        if r == 3:
            ready(4)
        block = keys[r] if r < 3 else long_keys[r - 3]
        product = lax.dot_general(
            query, block, (((1,), (1,)), ((), ())), preferred_element_type=jnp.float32
        )
        scores = jnp.where(which == r, product, scores)
    places = lax.broadcasted_iota(jnp.int32, (16, 2048), 1)
    scores = jnp.where(places < limit, scores * factor, NEGATIVE)
    is_main = which < 3
    highest = jnp.max(scores, axis=-1, keepdims=True)
    highest = jnp.where(is_main, jnp.maximum(highest, own), highest)
    weights = jnp.exp(scores - highest)
    own_weight = jnp.where(is_main, jnp.exp(own - highest), 0.0)
    total = jnp.sum(weights, axis=-1, keepdims=True) + own_weight
    rounded = weights.astype(jnp.bfloat16)
    summed = own_weight.astype(jnp.bfloat16).astype(jnp.float32) * values_twice
    for r in range(5):
        if r == 0:
            ready(5)
        if r == 3:
            ready(6)
        block = values[r] if r < 3 else long_values[r - 3]
        product = jnp.dot(rounded, block, preferred_element_type=jnp.float32)
        summed = summed + jnp.where(which == r, product, 0.0)
    state_ref[:, 0:128] = summed
    lanes = lax.broadcasted_iota(jnp.int32, (16, 128), 1)
    state_ref[:, 128:256] = jnp.where(lanes < 64, highest, total)
    side_ref[:, 0:128] = jnp.broadcast_to(own, (16, 128))
    side_ref[:, 128:256] = values_twice


def parts_of(layer, cache_ref, long_ref, wq_ref, wk_ref, wv_ref):
    return (
        wq_ref.at[layer], wk_ref.at[layer], wv_ref.at[layer],
        cache_ref.at[layer, 0], long_ref.at[layer, 0, 0],
        cache_ref.at[layer, 1], long_ref.at[layer, 1, 0],
    )


def first_kernel(
    group_ref, lengths_ref, long_lengths_ref, tokens_ref, own_long_ref, far_long_ref, *rest
):
    tables, resident, held = rest[:5], rest[5:10], rest[10:12]
    state_ref, side_ref, fresh_ref, hidden_ref = rest[12:16]
    buffers, semaphores = rest[16:18], rest[18]
    sources = (held[0].at[0, 1], held[1].at[0, 1, 0])
    copies = [
        pltpu.make_async_copy(source, target, semaphores.at[i])
        for i, (source, target) in enumerate(zip(sources, buffers))
    ]
    for copy in copies:
        copy.start()

    def ready(*which):
        for i in which:
            if i >= 5:
                copies[i - 5].wait()

    def hidden():
        own = own_long_ref[...].astype(jnp.float32)
        far = far_long_ref[...].astype(jnp.float32)
        even = lax.rem(group_ref[0], 2) == 0
        hidden_ref[...] = jnp.zeros((ROWS, 2048), jnp.float32)
        hidden_ref[0:3, :] = tokens_ref[...].astype(jnp.float32)
        hidden_ref[3:4, :] = jnp.where(even, own, far)
        hidden_ref[4:5, :] = jnp.where(even, far, own)
        return hidden_ref[...]

    attention_step(
        0, group_ref, lengths_ref, long_lengths_ref, hidden, *tables, (*resident, *buffers),
        state_ref, side_ref, fresh_ref, ready,
    )


def total_of(p_ref, r1_ref, r2_ref, r3_ref):
    p, r1, r2, r3 = (ref[...].astype(jnp.float32) for ref in (p_ref, r1_ref, r2_ref, r3_ref))
    return (p + r1) + (r2 + r3)


def second_kernel(
    group_ref, lengths_ref, long_lengths_ref, before_ref, p_ref, r1_ref, r2_ref, r3_ref, *rest
):
    tables, stored = rest[:5], rest[5:12]
    state_ref, side_ref, fresh_ref, hidden_ref = rest[12:16]

    def hidden():
        summed = total_of(p_ref, r1_ref, r2_ref, r3_ref)
        rows = (before_ref[...] + summed).astype(jnp.bfloat16).astype(jnp.float32)
        hidden_ref[...] = rows
        return rows

    attention_step(
        1, group_ref, lengths_ref, long_lengths_ref, hidden, *tables, stored,
        state_ref, side_ref, fresh_ref, lambda *which: None,
    )


UNIT = 256
FIRST = 23
PER = 2048 // UNIT
SECOND = 4 * PER - FIRST


def plane_of(unit):
    return unit // (2 * PER), unit // PER % 2, pl.ds(unit % PER * UNIT, UNIT)


def runs(begin, end):
    out, at = [], begin
    while at < end:
        stop = min(end, at // PER * PER + PER)
        i, j, _ = plane_of(at)
        out.append((i, j, at % PER * UNIT, (stop - at) * UNIT, (at - begin) * UNIT))
        at = stop
    return out


def leaving_kernel(begin, end, cache_ref, out_ref, unused_ref, semaphores):
    del unused_ref
    copies = []
    for n, (i, j, place, size, at) in enumerate(runs(begin, end)):
        copies.append(
            pltpu.make_async_copy(
                cache_ref.at[i, j, 2, pl.ds(place, size)], out_ref.at[pl.ds(at, size)],
                semaphores.at[n],
            )
        )
    for copy in copies:
        copy.start()
    for copy in copies:
        copy.wait()


def store_kernel(
    length_ref, first_ref, after_ref, stored_ref, blocks_ref, place_ref, buffer, semaphores
):
    del after_ref
    place_ref[...] = jnp.full((8, 128), length_ref[0].astype(jnp.float32))
    reads, writes = [], []
    for n in range(FIRST):
        i, j, rows = plane_of(n)
        piece = pl.ds(n * UNIT, UNIT)
        reads.append(
            pltpu.make_async_copy(first_ref.at[piece], buffer.at[piece], semaphores.at[0, n])
        )
        writes.append(
            pltpu.make_async_copy(buffer.at[piece], stored_ref.at[i, j, rows], semaphores.at[1, n])
        )
    for copy in reads:
        copy.start()
    for read, write in zip(reads, writes):
        read.wait()
        write.start()
    start = length_ref[0] // 16 * 16
    for plane in range(4):
        at = jnp.minimum(plane * 2048 + start, FIRST * UNIT - 16)
        blocks_ref[plane] = buffer[pl.ds(pl.multiple_of(at, 16), 16), :]
    for copy in writes:
        copy.wait()


def arrival_kernel(
    place_ref, stay_ref, arrived_ref, blocks_ref, second_ref, stored_ref, out_ref, moved_ref,
    rows, blocks, patched, semaphores,
):
    del stored_ref
    length = jnp.max(place_ref[...]).astype(jnp.int32)
    hit_unit = length // UNIT
    units = [(unit, *plane_of(unit)) for unit in range(FIRST, 4 * PER)]

    def straight(unit, i, j, place):
        return pltpu.make_async_copy(
            second_ref.at[pl.ds((unit - FIRST) * UNIT, UNIT)], moved_ref.at[i, j, place],
            semaphores.at[unit - FIRST],
        )

    def changed(unit, i, j, place):
        return pltpu.make_async_copy(
            patched.at[unit // PER], moved_ref.at[i, j, place], semaphores.at[unit - FIRST]
        )

    for unit in units:

        @pl.when(hit_unit != unit[0] % PER)
        def _():
            straight(*unit).start()

    fresh = [arrived_ref[0:1, 2048 + 128 * n : 2176 + 128 * n] for n in range(4)]
    start = pl.multiple_of(length // 16 * 16, 16)
    early = []
    for plane in range((FIRST + PER - 1) // PER):
        block = blocks_ref[plane].astype(jnp.float32)
        blocks[plane] = jnp.where(row_of(16) == length - start, fresh[plane], block).astype(
            jnp.bfloat16
        )
        write = pltpu.make_async_copy(
            blocks.at[plane], moved_ref.at[plane // 2, plane % 2, pl.ds(start, 16)],
            semaphores.at[SECOND + plane],
        )
        early.append((None if plane < FIRST // PER else plane * PER + hit_unit < FIRST, write))
    for inside, write in early:
        write.start() if inside is None else pl.when(inside)(write.start)
    for plane in range(FIRST // PER, 4):
        at = jnp.maximum(plane * PER + hit_unit - FIRST, 0) * UNIT
        whole = second_ref[pl.ds(pl.multiple_of(at, UNIT), UNIT), :].astype(jnp.float32)
        patched[plane] = jnp.where(
            row_of(UNIT) == length - hit_unit * UNIT, fresh[plane], whole
        ).astype(jnp.bfloat16)
    for unit in units:

        @pl.when(hit_unit == unit[0] % PER)
        def _():
            changed(*unit).start()

    rows[0:2, :] = stay_ref[...]
    rows[2:3, :] = arrived_ref[0:1, 0:2048]
    out = pltpu.make_async_copy(rows, out_ref, semaphores.at[SECOND + 4])
    out.start()
    for unit in units:
        straight(*unit).wait()
    for inside, write in early:
        write.wait() if inside is None else pl.when(inside)(write.wait)
    out.wait()


def fetch_kernel(layer, which, *refs):
    held, outputs, semaphores = refs[:5], refs[6 : 6 + len(which)], refs[-1]
    sources = parts_of(layer, *held)
    copies = [
        pltpu.make_async_copy(sources[i], output, semaphores.at[n])
        for n, (i, output) in enumerate(zip(which, outputs))
    ]
    for copy in copies:
        copy.start()
    for copy in copies:
        copy.wait()


def out_kernel(layer, state_ref, far_ref, side_ref, w_ref, after_ref, out_ref, w, semaphore):
    del after_ref
    copy = pltpu.make_async_copy(w_ref.at[layer], w, semaphore)
    copy.start()
    is_main = lax.rem(row_of(16), 8) < 3
    here, far = state_ref[...], far_ref[...]
    m_here, l_here, acc_here = here[:, 128:129], here[:, 192:193], here[:, :128]
    m_far, l_far, acc_far = far[:, 128:129], far[:, 192:193], far[:, :128]
    own, value = side_ref[:, 0:1], side_ref[:, 128:256]
    highest = jnp.maximum(jnp.maximum(m_here, m_far), own)
    f_here, f_far = jnp.exp(m_here - highest), jnp.exp(m_far - highest)
    own_weight = jnp.exp(own - highest)
    total = (l_here * f_here + l_far * f_far) + own_weight
    own_rounded = own_weight.astype(jnp.bfloat16).astype(jnp.float32)
    summed = (acc_here * f_here + acc_far * f_far) + own_rounded * value
    total = jnp.where(is_main, l_here, total)
    summed = jnp.where(is_main, acc_here, summed)
    attended = summed / total
    attended = jnp.concatenate([attended[:8], attended[8:]], axis=1).astype(jnp.bfloat16)
    copy.wait()
    out_ref[...] = jnp.dot(attended, w[...], preferred_element_type=jnp.float32)


def final_kernel(
    group_ref, before_ref, p_ref, r1_ref, r2_ref, r3_ref, fresh0_ref, fresh1_ref, after_ref,
    stay_ref, long_ref, leave_ref, scratch,
):
    del after_ref
    scratch[...] = before_ref[...] + total_of(p_ref, r1_ref, r2_ref, r3_ref)
    stay_ref[...] = scratch[0:2, :]
    odd = lax.rem(group_ref[0], 2) == 1
    long_ref[...] = jnp.where(odd, scratch[4:5, :], scratch[3:4, :])
    leave_ref[0:1, 0:2048] = scratch[2:3, :]
    for i, ref in enumerate((fresh0_ref, fresh1_ref)):
        for j in range(2):
            leave_ref[0:1, 2048 + 128 * (2 * i + j) : 2176 + 128 * (2 * i + j)] = ref[j : j + 1, :]


def local(
    tokens, long_tokens, cache, long_cache, lengths, long_lengths, norm_gain, q_gain, k_gain,
    w_query, key_weight, value_weight, w_out,
):
    groups = lax.axis_size("replica")
    group = lax.axis_index("replica")
    parity = group % 2
    group_1 = group[None]
    cache = cache.reshape(2, 2, 3, 2048, 128)
    long_cache = long_cache.reshape(2, 2, 1, 2, 2048, 128)

    params = pltpu.CompilerParams(vmem_limit_bytes=16 * 2**20)
    small = pltpu.CompilerParams(vmem_limit_bytes=2 * 2**20)
    held = in_hbm(cache)

    def leaving(begin, count, name):
        return pl.pallas_call(
            functools.partial(leaving_kernel, begin, begin + count),
            out_shape=(
                pltpu.VMEM((count * UNIT, 128), jnp.bfloat16),
                pltpu.VMEM((8, 128), jnp.float32),
            ),
            in_specs=[ANY],
            out_specs=(ANY, ANY),
            scratch_shapes=[pltpu.SemaphoreType.DMA((4,))],
            compiler_params=small,
            name=name,
        )(held)

    leaving_first, _ = leaving(0, FIRST, "leaving_first")
    leaving_second, _ = leaving(FIRST, SECOND, "leaving_second")
    first, second = (
        permute(piece, "replica", lambda i: (i + groups // 2) % groups)
        for piece in (leaving_first, leaving_second)
    )
    far_token = permute(long_tokens, "replica", lambda i: i ^ 1)

    places = jnp.concatenate(
        [
            lax.dynamic_slice_in_dim(lengths, group * 3, 3),
            lax.dynamic_slice_in_dim(long_lengths, group - parity, 2),
            jnp.zeros((3,), jnp.int32),
        ]
    ).astype(jnp.float32)
    inverse = np.float64(ROPE_BASE) ** (-2.0 * np.arange(64) / 128)
    inverse = jnp.asarray(np.concatenate([inverse, inverse]).astype(np.float32))
    sign = jnp.asarray(np.where(np.arange(128) < 64, -1.0, 1.0).astype(np.float32))
    angles = places[:, None] * inverse[None, :]
    cosine, sine = jnp.cos(angles), jnp.sin(angles) * sign

    out_shape = (
        jax.ShapeDtypeStruct((16, 256), jnp.float32),
        jax.ShapeDtypeStruct((16, 256), jnp.float32),
        jax.ShapeDtypeStruct((2, 128), jnp.float32),
        jax.ShapeDtypeStruct((ROWS, 2048), jnp.float32),
    )
    stored = (cache, long_cache, w_query, key_weight, value_weight)
    tables = (norm_gain, q_gain, k_gain, cosine, sine)

    def project_out(layer, state, side, after):
        far = permute(state, "replica", lambda i: i ^ 1)
        part = pl.pallas_call(
            functools.partial(out_kernel, layer),
            out_shape=jax.ShapeDtypeStruct((ROWS, 2048), jnp.float32),
            in_specs=[VM, VM, VM, ANY, ANY],
            out_specs=VM,
            scratch_shapes=[pltpu.VMEM((256, 2048), jnp.bfloat16), pltpu.SemaphoreType.DMA(())],
            compiler_params=params,
            name=f"out_projection_{layer}",
        )(state, far, side, w_out, after)
        part = (part + permute(part, "tensor", lambda i: i ^ 1)).astype(jnp.bfloat16)
        received = [permute(part, "tensor", lambda i, k=k: i ^ k) for k in (2, 4, 6)]
        return (part, *received)

    buffers = ((2048, 256), (2048, 128), (2048, 128)) + ((3, 2048, 128), (2, 2048, 128)) * 2

    def fetch(layer, which, after, name):
        return pl.pallas_call(
            functools.partial(fetch_kernel, layer, which),
            out_shape=tuple(pltpu.VMEM(buffers[i], jnp.bfloat16) for i in which),
            in_specs=[ANY] * 6,
            out_specs=(ANY,) * len(which),
            scratch_shapes=[pltpu.SemaphoreType.DMA((len(which),))],
            compiler_params=small,
            name=name,
        )(*map(in_hbm, stored), after)

    state, side, fresh_0, hidden = pl.pallas_call(
        first_kernel,
        out_shape=out_shape,
        in_specs=[SM] * 3 + [VM] * 13 + [ANY] * 2,
        out_specs=(VM,) * 4,
        scratch_shapes=[
            pltpu.VMEM((3, 2048, 128), jnp.bfloat16),
            pltpu.VMEM((2, 2048, 128), jnp.bfloat16),
            pltpu.SemaphoreType.DMA((2,)),
        ],
        compiler_params=params,
        name="attention_0",
    )(
        group_1, lengths, long_lengths, tokens, long_tokens, far_token, *tables,
        *fetch(0, (0, 1, 2, 3, 4), leaving_first, "fetch_0"), in_hbm(cache), in_hbm(long_cache),
    )
    resident = fetch(1, (0, 1, 2, 3, 4), state, "fetch_1_keys")
    terms = project_out(0, state, side, resident[1])
    resident = (*resident, *fetch(1, (5, 6), terms[0], "fetch_1_values"))
    state, side, fresh_1, hidden = pl.pallas_call(
        second_kernel,
        out_shape=out_shape,
        in_specs=[SM] * 3 + [VM] * 17,
        out_specs=(VM,) * 4,
        compiler_params=params,
        name="attention_1",
    )(group_1, lengths, long_lengths, hidden, *terms, *tables, *resident)
    terms = project_out(1, state, side, side)
    partner = (group + groups // 2) % groups
    arrived_len = lax.dynamic_slice_in_dim(lengths, partner * 3 + 2, 1)
    stored_first, blocks, place = pl.pallas_call(
        store_kernel,
        out_shape=(
            pltpu.HBM((2, 2, 2048, 128), jnp.bfloat16),
            pltpu.VMEM((4, 16, 128), jnp.bfloat16),
            pltpu.VMEM((8, 128), jnp.float32),
        ),
        in_specs=[SM, ANY, ANY],
        out_specs=(ANY, VM, VM),
        scratch_shapes=[
            pltpu.VMEM((FIRST * UNIT, 128), jnp.bfloat16),
            pltpu.SemaphoreType.DMA((2, FIRST)),
        ],
        compiler_params=pltpu.CompilerParams(vmem_limit_bytes=4 * 2**20),
        name="store_first",
    )(arrived_len, in_hbm(first), terms[0])
    stay, long_out, leave = pl.pallas_call(
        final_kernel,
        out_shape=(
            jax.ShapeDtypeStruct((2, 2048), jnp.float32),
            jax.ShapeDtypeStruct((1, 2048), jnp.float32),
            jax.ShapeDtypeStruct((1, 2560), jnp.float32),
        ),
        in_specs=[SM] + [VM] * 7 + [ANY],
        out_specs=(VM,) * 3,
        scratch_shapes=[pltpu.VMEM((ROWS, 2048), jnp.float32)],
        compiler_params=params,
        name="final_rows",
    )(group_1, hidden, *terms, fresh_0, fresh_1, blocks)
    arrived = permute(leave, "replica", lambda i: (i + groups // 2) % groups)
    out_hidden, moved = pl.pallas_call(
        arrival_kernel,
        out_shape=(
            pltpu.HBM((3, 2048), jnp.float32),
            pltpu.HBM((2, 2, 2048, 128), jnp.bfloat16),
        ),
        in_specs=[VM, VM, VM, VM, VM, ANY],
        out_specs=(ANY, ANY),
        input_output_aliases={5: 1},
        scratch_shapes=[
            pltpu.VMEM((3, 2048), jnp.float32),
            pltpu.VMEM((4, 16, 128), jnp.bfloat16),
            pltpu.VMEM((4, UNIT, 128), jnp.bfloat16),
            pltpu.SemaphoreType.DMA((SECOND + 5,)),
        ],
        compiler_params=small,
        name="arrival",
    )(place, stay, arrived, blocks, in_vmem(second), stored_first)
    return (out_hidden, long_out, moved[None, :, :, :, None, :])


def solution(mesh):
    return jax.shard_map(
        local,
        mesh=mesh,
        in_specs=(
            P("replica", None),
            P("replica", None),
            P(None, None, "replica", None, "tensor", None),
            P(None, None, "replica", None, None, "tensor", None),
            P(),
            P(),
            P(),
            P(),
            P(),
            P(None, None, "tensor"),
            P(None, None, "tensor"),
            P(None, None, "tensor"),
            P(None, "tensor", None),
        ),
        out_specs=(
            P("replica", None),
            P("replica", None),
            P("replica", None, None, None, "tensor", None),
        ),
        check_vma=False,
    )
```
